32 devices in a mesh: dp: 8 (over z, y), seq: 4 (over x, core).
Axes of the slice: x: 2, y: 2, z: 4, core: 2. Of those that a mesh axis runs over, the one named last changes fastest.
Arguments:
- tokens: bfloat16 [16, 512, 1024], P('dp', 'seq'), may hold values from -6 to 6
- cotangent: bfloat16 [16, 512, 1024], P('dp', 'seq'), may hold values from -6 to 6
- lengths: int32 [16], P('dp'), may hold values from 64 to 512, as said below
- project_weight: bfloat16 [1024, 3072], P(('dp', 'seq')), may hold values from -0.1875 to 0.1875
- project_bias: bfloat16 [2, 1024], P(None, ('dp', 'seq')), may hold values from -3 to 3
- mixing_weight: bfloat16 [1024, 1024], P(('dp', 'seq')), may hold values from -2 to 2
- mixing_bias: bfloat16 [1024], P(('dp', 'seq')), may hold values from -3 to 3
- first_gain: bfloat16 [1024], P(('dp', 'seq')), may hold values from 0.099609375 to 1.8984375
- first_shift: bfloat16 [1024], P(('dp', 'seq')), may hold values from -3 to 3
- up_weight: bfloat16 [1024, 4096], P(('dp', 'seq')), may hold values from -0.1875 to 0.1875
- up_bias: bfloat16 [4096], P(('dp', 'seq')), may hold values from -3 to 3
- down_weight: bfloat16 [4096, 1024], P(('dp', 'seq')), may hold values from -0.09375 to 0.09375
- down_bias: bfloat16 [1024], P(('dp', 'seq')), may hold values from -3 to 3
- last_gain: bfloat16 [1024], P(('dp', 'seq')), may hold values from 0.099609375 to 1.8984375
- last_shift: bfloat16 [1024], P(('dp', 'seq')), may hold values from -3 to 3
Outputs:
- layer_output: float32 [16, 512, 1024], P('dp', 'seq')
- tokens_gradient: float32 [16, 512, 1024], P('dp', 'seq')
- project_weight_gradient: float32 [1024, 3072], P(('dp', 'seq'))
- project_bias_gradient: float32 [2, 1024], P(None, ('dp', 'seq'))
- mixing_weight_gradient: float32 [1024, 1024], P(('dp', 'seq'))
- mixing_bias_gradient: float32 [1024], P(('dp', 'seq'))
- first_gain_gradient: float32 [1024], P(('dp', 'seq'))
- first_shift_gradient: float32 [1024], P(('dp', 'seq'))
- up_weight_gradient: float32 [1024, 4096], P(('dp', 'seq'))
- up_bias_gradient: float32 [4096], P(('dp', 'seq'))
- down_weight_gradient: float32 [4096, 1024], P(('dp', 'seq'))
- down_bias_gradient: float32 [1024], P(('dp', 'seq'))
- last_gain_gradient: float32 [1024], P(('dp', 'seq'))
- last_shift_gradient: float32 [1024], P(('dp', 'seq'))
The draws below stay inside these ranges and needn't reach their ends.
Inputs may be any that keep to these rules, and one draw needn't show every extreme that they name: `lengths`: entry p counts the leading tokens of page p that are not padding; keys at later positions are masked. Some page is full, with 512 tokens.
All inputs are finite; a program needn't handle non-finite values.
Results may differ from the reference program's by a relative error of at most 0.012.
Values may be sent and summed in bfloat16 or wider, within the bound.
A program may use at most 256 MiB of HBM per device.

```python
import jax
import jax.numpy as jnp
from jax import lax

D = 1024
HEADS = 16
HEAD_DIM = 64
FF = 4096
PAGE_LEN = 512
PAGES = 16


def draw_lengths(key, part):
    counts = jax.random.randint(jax.random.fold_in(key, 11), (PAGES,), PAGE_LEN // 8, PAGE_LEN + 1, dtype=jnp.int32)
    chosen = jax.random.randint(jax.random.fold_in(key, 12), (), 0, PAGES, dtype=jnp.int32)
    full = jnp.arange(PAGES, dtype=jnp.int32) == chosen
    return jnp.where(full, jnp.int32(PAGE_LEN), counts).astype(jnp.int32)


def spiked(values, own_key, source, target, parts, factor):
    owner, partner = [(jnp.arange(values.shape[dim]) // (values.shape[dim] // parts)).reshape([-1 if axis == dim else 1 for axis in range(values.ndim)]) for dim in (source, target)]
    chosen = jax.random.permutation(own_key, parts)[partner]
    strong = (owner == chosen) | (owner == (partner + parts // 2) % parts)
    return jnp.where(strong, factor * values, values)


def block_levels(stream_key, shape, shards, least, high):
    factor_of, own = 1.0, jax.random.fold_in(stream_key, 6)
    for position, blocks in shards:
        steps = jnp.exp(jax.random.uniform(jax.random.fold_in(own, position), (blocks,), jnp.float32, least / len(shards), high / len(shards)))
        factor_of = factor_of * jnp.repeat(steps, shape[position] // blocks).reshape([-1 if axis == position else 1 for axis in range(len(shape))])
    return factor_of


def centred(own_key, extent, deviation, limit, pieces=(), held_as=jnp.bfloat16):
    factor_of = block_levels(own_key, extent, pieces, -0.22, 0.18) if pieces else 1.0
    entries = jax.random.normal(own_key, extent, jnp.float32) * deviation * factor_of
    return jnp.minimum(jnp.maximum(entries, -limit), limit).astype(held_as)


def bell_draw_with(key, extent, deviation, limit, cuts, heavy, kind=jnp.bfloat16):
    array = deviation * jax.random.normal(key, extent, jnp.float32)
    if cuts:
        array = array * block_levels(key, extent, cuts, -0.22, 0.18)
    return jnp.clip(spiked(array, jax.random.fold_in(key, 3), *heavy), -limit, limit).astype(kind)


def setup_inputs(seed: int = 0) -> dict:
    key_list = jax.random.split(jax.random.key(seed), 16)
    tokens = centred(key_list[0], (PAGES, PAGE_LEN, D), 1.0, 6.0, ((0, 8), (1, 4)))
    cotangent = bell_draw_with(key_list[1], (PAGES, PAGE_LEN, D), 1.0, 6.0, ((0, 8), (1, 4)), (0, 2, 8, 2.0))
    lengths = draw_lengths(jax.random.fold_in(key_list[15], 71), 0)
    project_weight = centred(key_list[3], (D, 3 * D), D ** -0.5, 0.1875, ((0, 32),))
    project_bias = centred(key_list[4], (2, D), 0.5, 3.0, ((1, 32),))
    mixing_weight = centred(key_list[5], (D, D), (D // 128) ** -0.5, 2.0, ((0, 32),))
    mixing_bias = centred(key_list[6], (D,), 0.5, 3.0, ((0, 32),))
    first_gain = jnp.clip(1.0 + 0.18 * jax.random.normal(key_list[7], (D,), jnp.float32), 0.099609375, 1.8984375).astype(jnp.bfloat16)
    first_shift = centred(key_list[8], (D,), 0.5, 3.0, ((0, 32),))
    up_weight = centred(key_list[9], (D, FF), D ** -0.5, 0.1875, ((0, 32),))
    up_bias = centred(key_list[10], (FF,), 0.5, 3.0, ((0, 32),))
    down_weight = centred(key_list[11], (FF, D), FF ** -0.5, 0.09375, ((0, 32),))
    down_bias = centred(key_list[12], (D,), 0.5, 3.0, ((0, 32),))
    last_gain = jnp.clip(1.0 + 0.18 * jax.random.normal(key_list[13], (D,), jnp.float32), 0.099609375, 1.8984375).astype(jnp.bfloat16)
    last_shift = centred(key_list[14], (D,), 0.5, 3.0, ((0, 32),))
    return {"tokens": tokens, "cotangent": cotangent, "lengths": lengths, "project_weight": project_weight, "project_bias": project_bias, "mixing_weight": mixing_weight, "mixing_bias": mixing_bias, "first_gain": first_gain, "first_shift": first_shift, "up_weight": up_weight, "up_bias": up_bias, "down_weight": down_weight, "down_bias": down_bias, "last_gain": last_gain, "last_shift": last_shift}


@jax.custom_vjp
def low(v):
    return lax.optimization_barrier(v.astype(jnp.bfloat16)).astype(jnp.float32)

@jax.custom_vjp
def low_back(v):
    return v

def low_keep(v):
    return (low(v), None)

def low_pass(kept, grad):
    return (grad,)

def back_keep(v):
    return (v, None)

def back_low(kept, grad):
    return (low(grad),)
low.defvjp(low_keep, low_pass)
low_back.defvjp(back_keep, back_low)

def layer_norm(rows, gain, shift):
    center = rows - lax.optimization_barrier(jnp.mean(rows, axis=-1, keepdims=True))
    spread = lax.optimization_barrier(jnp.mean(center * center, axis=-1, keepdims=True))
    return center * lax.rsqrt(spread + 1e-05) * gain + shift

def gelu_exact(value):
    return 0.5 * value * (1.0 + lax.erf(value * 0.7071067811865476))

def one_page(rows, length, params):
    project_weight, project_bias, mixing_weight, mixing_bias, first_gain, first_shift, up_weight, up_bias, down_weight, down_bias, last_gain, last_shift = params
    highest = lax.Precision.HIGHEST
    width = rows.shape[0]
    bias = jnp.concatenate([project_bias[0], jnp.zeros_like(project_bias[0]), project_bias[1]])
    packed = low_back(low(jnp.dot(rows, project_weight, precision=highest) + bias))
    split = packed.reshape(width, 3, HEADS, HEAD_DIM)
    query = split[:, 0]
    keys = split[:, 1]
    values = split[:, 2]
    scores = low_back(jnp.einsum('qhd,khd->hqk', query, keys, precision=highest) * HEAD_DIM ** (-0.5))
    valid = jnp.arange(width) < length
    scores = jnp.where(valid[None, None, :], scores, -1e+30)
    top = lax.optimization_barrier(jnp.max(scores, axis=-1, keepdims=True))
    powers = jnp.exp(scores - top)
    probs = powers / lax.optimization_barrier(jnp.sum(powers, axis=-1, keepdims=True))
    context = jnp.einsum('hqk,khd->qhd', low(probs), values, precision=highest)
    context = low_back(low(context.reshape(width, HEADS * HEAD_DIM)))
    residual = rows + low_back(jnp.dot(context, mixing_weight, precision=highest)) + mixing_bias
    normed = layer_norm(residual, first_gain, first_shift)
    hidden_in = low_back(jnp.dot(low(normed), up_weight, precision=highest)) + up_bias
    activation = low(gelu_exact(hidden_in))
    residual = normed + low_back(jnp.dot(activation, down_weight, precision=highest)) + down_bias
    return layer_norm(residual, last_gain, last_shift)

def reference(tokens, cotangent, lengths, project_weight, project_bias, mixing_weight, mixing_bias, first_gain, first_shift, up_weight, up_bias, down_weight, down_bias, last_gain, last_shift):
    params = tuple((p.astype(jnp.float32) for p in (project_weight, project_bias, mixing_weight, mixing_bias, first_gain, first_shift, up_weight, up_bias, down_weight, down_bias, last_gain, last_shift)))

    def advance(totals, item):
        rows, grad_rows, length = item

        def forward(inputs, *weights):
            return one_page(inputs, length, weights)
        output, pull = jax.vjp(forward, rows.astype(jnp.float32), *params)
        grads = pull(grad_rows.astype(jnp.float32))
        return (tuple((t + g for t, g in zip(totals, grads[1:]))), (output, grads[0]))
    start = tuple((jnp.zeros(p.shape, p.dtype) for p in params))
    totals, (outputs, input_grads) = lax.scan(advance, start, (tokens, cotangent, lengths))
    return (outputs, input_grads, totals[0], totals[1], totals[2], totals[3], totals[4], totals[5], totals[6], totals[7], totals[8], totals[9], totals[10], totals[11])
```

```python
import functools
from types import SimpleNamespace

import jax
import jax.numpy as jnp
from jax import lax
from jax.experimental import pallas as pl
from jax.experimental.pallas import tpu as pltpu
from jax.sharding import PartitionSpec as P

HEADS = 16
HEAD_DIM = 64
F32 = jnp.float32
BF16 = jnp.bfloat16
MESH = pl.DeviceIdType.MESH
LANES = 128


def mm(left, right):
    return lax.dot_general(left, right, (((1,), (0,)), ((), ())), preferred_element_type=F32)


def mm_t(left, right):
    return lax.dot_general(left, right, (((1,), (1,)), ((), ())), preferred_element_type=F32)


def loop(count, body):
    def step(i, carry):
        body(i)
        return carry

    lax.fori_loop(0, count, step, 0)


def tile_of(columns):
    return 256 if columns % 256 == 0 else 128


def lanes(index, size):
    return pl.ds(pl.multiple_of(index * size, size), size)


QUERY_BIAS, VALUE_BIAS, MIX_BIAS, GAIN1, SHIFT1, DOWN_BIAS, GAIN2, SHIFT2, UP_BIAS = range(9)
TABLE = 16
PROJECT, MIXING, UP, DOWN, SMALL = range(5)


def layer_kernel(cfg, *refs):
    D, G, PG, L, C, F = cfg
    H = D // 2
    W = L * G
    HC = C // G
    FO = F // G
    CR = C // D
    SR = C // (D * G)
    FR = FO // D
    QC = 3 * HC
    heads = HEADS // G
    r = SimpleNamespace(**dict(zip(NAMES, refs)))

    dp = lax.axis_index("dp")
    s = lax.axis_index("seq")
    xx = lax.div(s, 2)
    cc = lax.rem(s, 2)
    side = lax.rem(dp, 2)
    pos = (1 - side) * lax.div(dp, 2) + side * (D - 1 - lax.div(dp, 2))

    def at_position(p):
        far = lax.div(p, H)
        return (1 - far) * 2 * p + far * (2 * (D - 1 - p) + 1)

    def shifted(k):
        return at_position(lax.rem(pos + (k + D) % D, D))

    right, left = (shifted(1), s), (shifted(-1), s)
    ways = (right, left)
    peer = {1: s + 1 - 2 * cc, 2: s + 2 - 4 * xx, 3: 3 - s}
    sibling, across = (dp, peer[1]), (dp, peer[2])

    def remote(src, dst, send, recv, device):
        return pltpu.make_async_remote_copy(
            src_ref=src, dst_ref=dst, send_sem=send, recv_sem=recv,
            device_id=device, device_id_type=MESH,
        )

    def block(index, size):
        return pl.ds(pl.multiple_of(index * size, size), size)

    local = []

    def load(src, dst):
        copy = pltpu.make_async_copy(src, dst, r.local_sem.at[len(local)])
        copy.start()
        local.append(copy)
        return copy

    load_mix = load(r.mw, r.wm.at[dp, s])
    load_tok = [load(r.tok.at[p], r.xg.at[p, block(s, L)]) for p in range(PG)]
    load_down = load(r.dw, r.wd.at[block(dp, FR)])

    barrier = pltpu.get_barrier_semaphore()
    partners = [right, left] + [(dp, peer[k]) for k in (1, 2, 3)]
    for device in partners:
        pl.semaphore_signal(barrier, inc=1, device_id=device, device_id_type=MESH)

    for q in range(G):
        for b in range(3):
            r.sp[q, :, b * HC:(b + 1) * HC] = r.pw[:, b * C + q * HC:b * C + (q + 1) * HC]
        for j in range(D):
            r.su[q, :, j * FR:(j + 1) * FR] = r.uw[:, (j * G + q) * FR:(j * G + q + 1) * FR]
    r.ss[...] = jnp.zeros_like(r.ss)
    r.ss[QUERY_BIAS:VALUE_BIAS + 1, 0:SR] = r.pb[...].astype(F32)
    for row, ref in ((MIX_BIAS, r.mb), (GAIN1, r.fg), (SHIFT1, r.fs), (DOWN_BIAS, r.db), (GAIN2, r.lg), (SHIFT2, r.ls)):
        r.ss[row:row + 1, 0:SR] = ref[...].astype(F32)
    r.ss[UP_BIAS:UP_BIAS + 1, 0:FR] = r.ub[...].astype(F32)

    pl.semaphore_wait(barrier, len(partners))

    exchanges = []

    def exchange(slot, source, target):
        def copy(k, which):
            return remote(source(peer[k]), target(which), r.xs.at[slot, k - 1], r.xr.at[slot, k - 1], (dp, peer[k]))

        def start():
            exchanges.append(lambda: [copy(k, s).wait_send() for k in (2, 3, 1)])
            for k in (2, 3, 1):
                copy(k, s).start()

        def finish():
            for k in (1, 2, 3):
                copy(k, peer[k]).wait_recv()

        return SimpleNamespace(start=start, finish=finish)

    def spread(slot, block):
        def copy(k):
            which = peer[2] if k == 2 else s
            device = across if k == 1 else sibling
            return remote(block(which), block(which), r.xs.at[slot, k], r.xr.at[slot, k], device)

        def arrived(k, which):
            return remote(block(which), block(which), r.xs.at[slot, k], r.xr.at[slot, k], sibling)

        def start():
            exchanges.append(lambda: [copy(k).wait_send() for k in range(3)])
            copy(1).start()
            copy(0).start()

        def forward():
            arrived(1, peer[2]).wait_recv()
            copy(2).start()

        def finish():
            arrived(0, peer[1]).wait_recv()
            arrived(2, peer[3]).wait_recv()

        return SimpleNamespace(start=start, forward=forward, finish=finish)

    def half_rows(count, half):
        return pl.ds(half * (count // 2), count // 2)

    def rows_of(ref, owner, count, half):
        if half is None:
            return ref.at[block(owner, count)]
        return ref.at[block(owner * 2 + half, count // 2)]

    def chunk_view(g, owner, half):
        if g == PROJECT:
            return rows_of(r.wq, owner, CR, half)
        if g == MIXING:
            return r.wm.at[owner, s] if half is None else r.wm.at[owner, s, half_rows(SR, half)]
        if g == UP:
            return rows_of(r.wu, owner, CR, half)
        if g == DOWN:
            return rows_of(r.wd, owner, FR, half)
        return r.sm.at[owner] if half is None else r.sm.at[owner, half_rows(G, half)]

    def gather_copy(g, d, t, owner):
        view = chunk_view(g, owner, d if t == H else None)
        return remote(view, view, r.gs.at[g, d, t - 1], r.gr.at[g, d, t - 1], ways[d])

    def sent(d, t):
        return shifted(-(t - 1) if d == 0 else t - 1)

    def gather_send(g, t):
        for d in range(2):
            gather_copy(g, d, t, sent(d, t)).start()

    def gather_step(g, t):
        for d in range(2):
            gather_copy(g, d, t, shifted(-t if d == 0 else t)).wait_recv()
            if t < H:
                gather_copy(g, d, t + 1, sent(d, t + 1)).start()

    fetched = dict.fromkeys(range(5), 0)

    def fetch(g, to=None):
        to = min(H, fetched[g] + 1 if to is None else to)
        while fetched[g] < to:
            fetched[g] += 1
            gather_step(g, fetched[g])

    def gather_drain(g):
        for t in range(1, H + 1):
            for d in range(2):
                gather_copy(g, d, t, sent(d, t)).wait_send()

    give_project = exchange(0, lambda q: r.sp.at[q], lambda q: r.wq.at[block(dp * G + q, SR)])
    give_small = exchange(1, lambda q: r.ss, lambda q: r.sm.at[dp, q])
    give_up = exchange(2, lambda q: r.su.at[q], lambda q: r.wu.at[block(dp * G + q, SR)])
    give_project.start()
    give_small.start()
    load_mix.wait()
    gather_send(MIXING, 1)
    tokens_in = [spread(3 + p, lambda q, p=p: r.xg.at[p, block(q, L)]) for p in range(PG)]
    for p in range(PG):
        load_tok[p].wait()
        tokens_in[p].start()
    give_up.start()
    r.wq[block(dp * G + s, SR), :] = r.sp[s]
    r.wu[block(dp * G + s, SR), :] = r.su[s]
    r.sm[dp, s] = r.ss[...]
    load_down.wait()
    give_project.finish()
    gather_send(PROJECT, 1)
    give_small.finish()
    gather_send(SMALL, 1)
    r.vs[...] = jnp.zeros_like(r.vs)
    give_up.finish()
    for t in range(1, H + 1):
        fetch(PROJECT)
        fetch(SMALL)
        fetch(MIXING)
        if t == 1:
            gather_send(UP, 1)
        if t == 2:
            gather_send(DOWN, 1)
        if t <= PG:
            tokens_in[t - 1].forward()
    mix_in = spread(3 + PG, lambda q: r.wm.at[:, q])
    mix_in.start()

    for row in range(UP_BIAS):
        piece = r.sm[:, 0, row, :]
        for q in range(1, G):
            piece = piece + pltpu.roll(r.sm[:, q, row, :], q * SR, 1)
        for j in range(D):
            r.pv[row:row + 1, j * CR:(j + 1) * CR] = piece[j:j + 1]
    for j in range(D):
        r.ubv[0:1, j * FR:(j + 1) * FR] = r.sm[j, s, UP_BIAS:UP_BIAS + 1, :]
    r.pbv[...] = jnp.zeros_like(r.pbv)
    own_heads = pl.ds(pl.multiple_of(s * HC, HC), HC)
    r.pbv[0:1, 0:HC] = r.pv[QUERY_BIAS:QUERY_BIAS + 1, own_heads]
    r.pbv[0:1, 2 * HC:3 * HC] = r.pv[VALUE_BIAS:VALUE_BIAS + 1, own_heads]

    def param(row):
        return r.pv[row:row + 1, :]

    tq = tile_of(QC)

    def project_page(p):
        def body(n):
            cols = lanes(n, tq)
            r.qkv[p, :, cols] = (mm(r.xg[p], r.wq[:, cols]) + r.pbv[0:1, cols]).astype(BF16)

        loop(QC // tq, body)

    for p in range(PG):
        tokens_in[p].finish()
        project_page(p)
    fetch(UP)

    pairs = heads // 2
    QB = 256 if W % 256 == 0 else W
    scale = HEAD_DIM ** -0.5

    def pair_of(p, hp):
        return [r.qkv[p, :, pl.ds(pl.multiple_of(b * HC + hp * LANES, LANES), LANES)] for b in range(3)]

    def only(half, rows):
        lane = lax.broadcasted_iota(jnp.int32, rows.shape, 1)
        mine = lane >= HEAD_DIM if half else lane < HEAD_DIM
        return jnp.where(mine, rows, jnp.zeros_like(rows))

    def attend_page(p):
        length = r.lens[p]

        def body(hp):
            query, keys, values = pair_of(p, hp)
            values_t = values.T
            halves = []
            for half in range(2):
                keys_h = only(half, keys)
                blocks = []
                for qb in range(W // QB):
                    scores = mm_t(keys_h, query[qb * QB:(qb + 1) * QB])
                    at_key = lax.broadcasted_iota(jnp.int32, scores.shape, 0)
                    scores = jnp.where(at_key < length, scores, -1e30)
                    top = jnp.max(scores, axis=0, keepdims=True)
                    powers = jnp.exp((scores - top) * scale)
                    probs = powers * (1.0 / jnp.sum(powers, axis=0, keepdims=True))
                    r.probs[(p * pairs + hp) * 2 + half, :, qb * QB:(qb + 1) * QB] = probs
                    blocks.append(mm(values_t[half * HEAD_DIM:(half + 1) * HEAD_DIM], probs.astype(BF16)))
                halves.append(jnp.concatenate(blocks, axis=1))
            both = jnp.concatenate(halves, axis=0).T
            r.ctx[p, :, lanes(hp, LANES)] = both.astype(BF16)

        loop(pairs, body)

    context_out = [
        exchange(4 + PG + p, lambda q, p=p: r.ctx.at[p, block(q, L)],
                 lambda q, p=p: r.cr.at[p, :, block(q, HC)])
        for p in range(PG)
    ]
    mix_in.forward()
    for p in range(PG):
        attend_page(p)
        context_out[p].start()
        r.cr[p, :, own_heads] = r.ctx[p, pl.ds(pl.multiple_of(s * L, L), L), :]
        fetch(DOWN if p else UP)
    mix_in.finish()
    fetch(UP)
    fetch(DOWN)

    own_rows = pl.ds(pl.multiple_of(s * L, L), L)
    tc = tile_of(C)
    for p in range(PG):
        context_out[p].finish()

    def mix_body(n):
        cols = lanes(n, tc)
        mixed = mm(r.cr[...].reshape(PG * L, C), r.wm[:, :, :, cols].reshape(C, tc))
        r.tg[:, :, cols] = mixed.reshape(PG, L, tc)

    loop(C // tc, mix_body)
    RB = 32

    def by_rows(p, body):
        def step(i):
            body(pl.ds(pl.multiple_of(i * RB, RB), RB), pl.ds(pl.multiple_of(s * L + i * RB, RB), RB))

        loop(L // RB, step)

    def standard(rows):
        center = rows - jnp.mean(rows, axis=-1, keepdims=True)
        inverse = lax.rsqrt(jnp.mean(center * center, axis=-1, keepdims=True) + 1e-05)
        return center * inverse, inverse

    def unstandard(grad, nhat, inverse):
        return inverse * (
            grad - jnp.mean(grad, axis=-1, keepdims=True) - nhat * jnp.mean(grad * nhat, axis=-1, keepdims=True)
        )

    def add_row(row, rows):
        r.vs[row:row + 1, :] += jnp.sum(rows, axis=0, keepdims=True)

    normed_in = [spread(4 + 2 * PG + p, lambda q, p=p: r.nlg.at[p, block(q, L)]) for p in range(PG)]

    def first_norm(p):
        def body(rows, group_rows):
            resid = r.xg[p, group_rows, :].astype(F32) + r.tg[p, rows, :] + param(MIX_BIAS)
            nhat, inverse = standard(resid)
            normed = nhat * param(GAIN1) + param(SHIFT1)
            r.nh1[p, rows, :] = nhat
            r.inv1[p, rows, :] = jnp.broadcast_to(inverse, (RB, LANES))
            r.tg[p, rows, :] = normed
            r.nlg[p, group_rows, :] = normed.astype(BF16)

        by_rows(p, body)

    for p in range(PG):
        first_norm(p)
        normed_in[p].start()
    fetch(UP, H)
    fetch(DOWN)
    for p in range(PG):
        normed_in[p].forward()

    tf = tile_of(FO)

    def up_page(p):
        def body(n):
            cols = lanes(n, tf)
            hidden = mm(r.nlg[p], r.wu[:, cols]) + r.ubv[0:1, cols]
            cdf = 0.5 * (1.0 + lax.erf(hidden * 0.7071067811865476))
            r.act[p, :, cols] = (hidden * cdf).astype(BF16)
            slope = cdf + hidden * (jnp.exp(hidden * hidden * -0.5) * 0.3989422804014327)
            r.gp[p, :, cols] = slope

        loop(FO // tf, body)

    for p in range(PG):
        normed_in[p].finish()
        up_page(p)
    fetch(DOWN, H)

    def fold(slot, part, r1, s2, r2):
        def near(k):
            return remote(part(2 * k + 1 - cc), r1.at[k], r.fs_.at[slot, k], r.fr_.at[slot, k], sibling)

        def far():
            return remote(s2, r2, r.fs_.at[slot, 2], r.fr_.at[slot, 2], across)

        def start():
            for k in range(2):
                near(k).start()

        def drain():
            for k in range(2):
                near(k).wait_send()
            far().wait_send()

        def middle():
            for k in range(2):
                near(k).wait_recv()
            count = s2.shape[0]

            def body(i):
                rows = pl.ds(pl.multiple_of(i * RB, RB), RB)
                s2[rows, :] = (part(peer[2])[rows, :] + r1[1 - xx, rows, :]).astype(BF16)

            loop(count // RB, body)
            far().start()

        def finish():
            far().wait_recv()

        def own(rows):
            return part(s)[rows, :] + r1[xx, rows, :] + r2[rows, :].astype(F32)

        return SimpleNamespace(start=start, middle=middle, finish=finish, own=own, drain=drain)

    def page_fold(slot, p):
        return fold(slot + p, lambda q: r.part.at[p * G + q], r.r1.at[p], r.s2.at[p], r.r2.at[p])

    def into_part(p, cols, value):
        r.part[p * G:(p + 1) * G, :, cols] = value.reshape(G, L, value.shape[-1])

    down_fold = [page_fold(0, p) for p in range(PG)]

    def down_page(p):
        def body(n):
            cols = lanes(n, tc)
            into_part(p, cols, mm(r.act[p], r.wd[:, cols]))

        loop(C // tc, body)

    for p in range(PG):
        down_page(p)
        down_fold[p].start()
        if p:
            down_fold[p - 1].middle()
    down_fold[PG - 1].middle()

    last_in = [spread(4 + 3 * PG + p, lambda q, p=p: r.lrg.at[p, block(q, L)]) for p in range(PG)]

    def last_norm(p):
        def body(rows, group_rows):
            resid = r.tg[p, rows, :] + down_fold[p].own(rows) + param(DOWN_BIAS)
            nhat, inverse = standard(resid)
            r.out[p, rows, :] = nhat * param(GAIN2) + param(SHIFT2)
            cot = r.cot[p, rows, :].astype(F32)
            add_row(GAIN2, cot * nhat)
            add_row(SHIFT2, cot)
            grad = unstandard(cot * param(GAIN2), nhat, inverse)
            add_row(DOWN_BIAS, grad)
            r.tg[p, rows, :] = grad
            r.lrg[p, group_rows, :] = grad.astype(BF16)

        by_rows(p, body)

    for p in range(PG):
        down_fold[p].finish()
        last_norm(p)
        last_in[p].start()
    for p in range(PG):
        last_in[p].forward()
    for p in range(PG):
        last_in[p].finish()

    def weight_chunks(lhs, rhs, owners, columns, width):
        count = len(owners)
        for i, j in enumerate(owners):
            for p in range(PG):
                r.tt[i * width:(i + 1) * width, p * W:(p + 1) * W] = lhs[p, :, block(j, width)].T
        tn = tile_of(columns)

        def value(n):
            block = rhs[:, :, lanes(n, tn)].reshape(PG * W, tn)
            full = mm(r.tt[0:count * width, :], block)
            return [full[i * width:(i + 1) * width] for i in range(count)]

        return value, columns // tn, tn

    def grad_chunks(g, owners):
        if g == PROJECT:
            return weight_chunks(r.xg, r.qkv, owners, QC, CR)
        if g == UP:
            return weight_chunks(r.nlg, r.hid, owners, FO, CR)
        if g == DOWN:
            return weight_chunks(r.act, r.lrg, owners, C, FR)
        if g == MIXING:
            return (lambda n: [mix_part(s)[block(j, SR), lanes(n, tc)] for j in owners]), C // tc, tc
        return (lambda n: [r.vc[j] for j in owners]), 1, CR

    bufs = {PROJECT: (r.bp, r.tp), MIXING: (r.bm, r.tm), UP: (r.bu, r.tu), DOWN: (r.bd, r.td), SMALL: (r.bs, r.ts)}

    def ring_copy(g, d, t):
        buf, first = bufs[g]
        count = first.shape[0]
        if t == 1:
            src, dst = first.at[half_rows(count, d)], buf.at[d, 0, half_rows(count, d)]
        else:
            src, dst = buf.at[d, t - 2], buf.at[d, t - 1]
        return remote(src, dst, r.rs.at[g, d, t - 1], r.rr.at[g, d, t - 1], ways[d])

    def ring_first(g):
        buf, first = bufs[g]
        value, count, tn = grad_chunks(g, [shifted(H)])

        def body(n):
            first[:, lanes(n, tn)] = value(n)[0].astype(first.dtype)

        loop(count, body)
        for d in range(2):
            ring_copy(g, d, 1).start()

    def ring_next(g, t):
        buf, first = bufs[g]
        size = first.shape[0]
        hop = H + 1 - t
        for d in range(2):
            ring_copy(g, d, t - 1).wait_recv()
        value, count, tn = grad_chunks(g, [shifted(hop), shifted(-hop)])

        def body(n):
            cols = lanes(n, tn)
            for d, val in enumerate(value(n)):
                if t == 2:
                    near, off = half_rows(size, d), half_rows(size, 1 - d)
                    lo, hi = d * (size // 2), (1 - d) * (size // 2)
                    buf[d, 0, near, cols] = (val[lo:lo + size // 2] + buf[d, 0, near, cols].astype(F32)).astype(buf.dtype)
                    buf[d, 0, off, cols] = val[hi:hi + size // 2].astype(buf.dtype)
                else:
                    buf[d, t - 2, :, cols] = (val + buf[d, t - 2, :, cols].astype(F32)).astype(buf.dtype)

        loop(count, body)
        for d in range(2):
            ring_copy(g, d, t).start()

    def ring_last(g, put):
        advance(g, H)
        buf, first = bufs[g]
        for d in range(2):
            ring_copy(g, d, H).wait_recv()
        value, count, tn = grad_chunks(g, [dp])

        def body(n):
            cols = lanes(n, tn)
            put(cols, value(n)[0] + buf[0, H - 1, :, cols].astype(F32) + buf[1, H - 1, :, cols].astype(F32))

        loop(count, body)
        for t in range(1, H + 1):
            for d in range(2):
                ring_copy(g, d, t).wait_send()

    reached = dict.fromkeys(range(5), 0)

    def advance(g, to=None):
        to = min(H, reached[g] + 1 if to is None else to)
        while reached[g] < to:
            reached[g] += 1
            ring_first(g) if reached[g] == 1 else ring_next(g, reached[g])

    advance(DOWN)

    def hidden_page(p):
        def body(n):
            cols = lanes(n, tf)
            grad = mm_t(r.lrg[p], r.wd[cols, :]) * r.gp[p, :, cols]
            r.vu[0:1, cols] += jnp.sum(grad, axis=0, keepdims=True)
            r.hid[p, :, cols] = grad.astype(BF16)

        loop(FO // tf, body)

    r.vu[...] = jnp.zeros_like(r.vu)
    normed_fold = [page_fold(PG, p) for p in range(PG)]

    def normed_page(p):
        def body(n):
            cols = lanes(n, tc)
            into_part(p, cols, mm_t(r.hid[p], r.wu[cols, :]))

        loop(C // tc, body)

    hidden_page(0)
    advance(DOWN)
    for p in range(PG):
        if p:
            hidden_page(p)
        down_fold[p].drain()
        normed_page(p)
        normed_fold[p].start()
        if p:
            normed_fold[p - 1].middle()
    normed_fold[PG - 1].middle()
    advance(DOWN)

    grads_out = [
        exchange(4 + 4 * PG + p, lambda q, p=p: r.cg.at[p, :, block(q, HC)],
                 lambda q, p=p: r.dc.at[p, block(q, L)])
        for p in range(PG)
    ]

    def first_back(p):
        def body(rows, group_rows):
            grad = r.tg[p, rows, :] + normed_fold[p].own(rows)
            nhat = r.nh1[p, rows, :]
            add_row(GAIN1, grad * nhat)
            add_row(SHIFT1, grad)
            grad = unstandard(grad * param(GAIN1), nhat, r.inv1[p, rows, 0:1])
            add_row(MIX_BIAS, grad)
            r.tg[p, rows, :] = grad
            r.frl[p, rows, :] = grad.astype(BF16)

        by_rows(p, body)

    def context_back(p):
        def body(n):
            cols = lanes(n, tc)
            r.cg[p, :, cols] = mm_t(r.frl[p], r.wm[block(n, tc // CR)].reshape(tc, C)).astype(BF16)

        loop(C // tc, body)

    for p in range(PG):
        normed_fold[p].finish()
        first_back(p)
        context_back(p)
        grads_out[p].start()
        r.dc[p, own_rows, :] = r.cg[p, :, own_heads]
    advance(DOWN)

    def mix_part(q):
        return r.gp.at[lax.div(q, W // HC), block(lax.rem(q, W // HC), HC)]

    for i in range(C // 256):
        for p in range(PG):
            r.tm_[:, p * L:(p + 1) * L] = r.cr[p, :, i * 256:(i + 1) * 256].T

        def body(n, i=i):
            cols = lanes(n, tc)
            full = mm(r.tm_[...], r.frl[:, :, cols].reshape(PG * L, tc))
            for k in range(256 // SR):
                j, q = divmod(i * (256 // SR) + k, G)
                r.gp[q * HC // W, q * HC % W + j * SR:q * HC % W + (j + 1) * SR, cols] = full[k * SR:(k + 1) * SR]

        loop(C // tc, body)
    mix_fold = fold(3 * PG, mix_part, r.m1, r.ms2, r.mr2)
    mix_fold.start()
    advance(UP)
    mix_fold.middle()
    ring_last(DOWN, lambda cols, val: r.gdw.__setitem__((slice(None), cols), val))

    def attend_back_page(p):
        def body(hp):
            query, keys, values = pair_of(p, hp)
            d_ctx = r.dc[p, :, lanes(hp, LANES)]
            keys_t = keys.T
            d_query, d_keys, d_values = [], None, None
            for half in range(2):
                values_h = only(half, values)
                row = []
                for qb in range(W // QB):
                    span = slice(qb * QB, (qb + 1) * QB)
                    d_probs = mm_t(values_h, d_ctx[span])
                    probs = r.probs[(p * pairs + hp) * 2 + half, :, span]
                    inner = jnp.sum(probs * d_probs, axis=0, keepdims=True)
                    d_scores = (probs * (d_probs - inner)).astype(BF16)
                    row.append(mm(keys_t[half * HEAD_DIM:(half + 1) * HEAD_DIM], d_scores))
                    dk = mm(d_scores, only(half, query[span]))
                    dv = mm(probs.astype(BF16), only(half, d_ctx[span]))
                    d_keys = dk if d_keys is None else d_keys + dk
                    d_values = dv if d_values is None else d_values + dv
                d_query.append(jnp.concatenate(row, axis=1))
            d_query = jnp.concatenate(d_query, axis=0).T * scale
            for b, val in enumerate((d_query, d_keys * scale, d_values)):
                cols = pl.ds(pl.multiple_of(b * HC + hp * LANES, LANES), LANES)
                low = val.astype(BF16)
                r.qkv[p, :, cols] = low
                r.vp[0:1, cols] += jnp.sum(low.astype(F32), axis=0, keepdims=True)

        loop(pairs, body)

    r.vp[...] = jnp.zeros_like(r.vp)
    tokens_fold = [page_fold(2 * PG, p) for p in range(PG)]

    def tokens_page(p):
        def body(n):
            cols = lanes(n, tc)
            into_part(p, cols, mm_t(r.qkv[p], r.wq[cols, :]))

        loop(C // tc, body)

    advance(UP)
    for p in range(PG):
        grads_out[p].finish()
        attend_back_page(p)
        advance(UP)
    mix_fold.finish()

    def own_mix(i):
        rows = pl.ds(pl.multiple_of(i * RB, RB), RB)
        mix_part(s)[rows, :] = mix_fold.own(rows)

    loop(HC // RB, own_mix)
    advance(PROJECT)
    advance(MIXING)
    for p in range(PG):
        normed_fold[p].drain()
        tokens_page(p)
        tokens_fold[p].start()

    r.vs[QUERY_BIAS:QUERY_BIAS + 1, own_heads] = r.vp[0:1, 0:HC]
    r.vs[VALUE_BIAS:VALUE_BIAS + 1, own_heads] = r.vp[0:1, 2 * HC:3 * HC]
    for j in range(D):
        r.vc[j] = r.vs[:, j * CR:(j + 1) * CR]
        r.vc[j, UP_BIAS:UP_BIAS + 1, :] = r.vu[0:1, j * FR:(j + 1) * FR]
    advance(SMALL)

    advance(PROJECT)
    advance(MIXING)
    advance(SMALL)
    for p in range(PG):
        tokens_fold[p].middle()

    up_out = exchange(4 + 5 * PG, lambda q: r.fu.at[block(q, SR)], lambda q: r.fur.at[q])

    ring_last(UP, lambda cols, val: r.fu.__setitem__((slice(None), cols), val))
    up_out.start()
    r.fur[s] = r.fu[block(s, SR), :]
    for t in range(3, H + 1):
        advance(PROJECT)
        advance(MIXING)
        advance(SMALL)

    for p in range(PG):
        tokens_fold[p].finish()

        def token_rows(rows, group_rows, p=p):
            r.tg[p, rows, :] = r.tg[p, rows, :] + tokens_fold[p].own(rows)

        by_rows(p, token_rows)
    up_out.finish()
    for q in range(G):
        for j in range(D):
            r.guw[:, (j * G + q) * FR:(j * G + q + 1) * FR] = r.fur[q, :, j * FR:(j + 1) * FR]

    project_out = exchange(5 + 5 * PG, lambda q: r.fp.at[block(q, SR)], lambda q: r.fpr.at[q])
    small_out = exchange(6 + 5 * PG, lambda q: r.fsm, lambda q: r.fsr.at[q])
    ring_last(PROJECT, lambda cols, val: r.fp.__setitem__((slice(None), cols), val))
    project_out.start()
    ring_last(SMALL, lambda cols, val: r.fsm.__setitem__((slice(None), cols), val))
    small_out.start()
    ring_last(MIXING, lambda cols, val: r.gmw.__setitem__((slice(None), cols), val))
    r.fpr[s] = r.fp[block(s, SR), :]
    r.fsr[s] = r.fsm[...]
    project_out.finish()
    for q in range(G):
        for b in range(3):
            r.gpw[:, b * C + q * HC:b * C + (q + 1) * HC] = r.fpr[q, :, b * HC:(b + 1) * HC]
    small_out.finish()
    total = r.fsr[0]
    for q in range(1, G):
        total = total + r.fsr[q]
    mine = jnp.zeros((TABLE, SR), F32)
    for q in range(G):
        mine = mine + jnp.where(s == q, 1.0, 0.0) * pltpu.roll(total, (CR - q * SR) % CR, 1)[:, 0:SR]
    r.gpb[...] = mine[QUERY_BIAS:VALUE_BIAS + 1]
    for row, ref in ((MIX_BIAS, r.gmb), (GAIN1, r.gfg), (SHIFT1, r.gfs), (DOWN_BIAS, r.gdb), (GAIN2, r.glg), (SHIFT2, r.gls)):
        ref[...] = mine[row:row + 1]
    r.gub[...] = r.fsm[UP_BIAS:UP_BIAS + 1, :]

    for g in range(5):
        gather_drain(g)
    for one in tokens_fold + [mix_fold]:
        one.drain()
    for done in exchanges:
        done()

INPUTS = ["tok", "cot", "lens", "pw", "pb", "mw", "mb", "fg", "fs", "uw", "ub", "dw", "db", "lg", "ls"]
OUTPUTS = ["out", "tg", "gpw", "gpb", "gmw", "gmb", "gfg", "gfs", "guw", "gub", "gdw", "gdb", "glg", "gls"]


def scratch_of(cfg):
    D, G, PG, L, C, F = cfg
    H = D // 2
    W, HC, FO, CR, SR = L * G, C // G, F // G, C // D, C // (D * G)
    FR, QC, heads = FO // D, 3 * HC, HEADS // G
    low = dict(
        wq=(C, QC), wm=(D, G, SR, C), wu=(C, FO), wd=(FO, C), sp=(G, SR, QC), su=(G, SR, FO), xg=(PG, W, C),
        qkv=(PG, W, QC), ctx=(PG, W, HC), cr=(PG, L, C), nlg=(PG, W, C), act=(PG, W, FO), hid=(PG, W, FO),
        s2=(PG, L, C), r2=(PG, L, C), lrg=(PG, W, C), frl=(PG, L, C), cg=(PG, L, C), dc=(PG, W, HC),
        ms2=(HC, C), mr2=(HC, C), tt=(2 * max(CR, FR), PG * W), tm_=(256, PG * L),
        bp=(2, H, CR, QC), tp=(CR, QC), bm=(2, H, SR, C), tm=(SR, C), bu=(2, H, CR, FO), tu=(CR, FO),
        bd=(2, H, FR, C), td=(FR, C),
    )
    wide = dict(
        ss=(TABLE, LANES), sm=(D, G, TABLE, LANES), probs=(PG * heads, W, W), nh1=(PG, L, C),
        inv1=(PG, L, LANES), gp=(PG, W, FO), part=(PG * G, L, C), r1=(PG, 2, L, C), m1=(2, HC, C),
        bs=(2, H, TABLE, CR), ts=(TABLE, CR), vs=(TABLE, C), vp=(8, QC), vu=(8, FO), vc=(D, TABLE, CR),
        pv=(TABLE, C), ubv=(8, FO), pbv=(8, QC), fu=(CR, FO), fur=(G, SR, FO), fp=(CR, QC), fpr=(G, SR, QC),
        fsm=(TABLE, CR), fsr=(G, TABLE, CR),
    )
    sems = dict(
        local_sem=(2 + PG,), gs=(5, 2, H), gr=(5, 2, H), rs=(5, 2, H), rr=(5, 2, H),
        xs=(7 + 5 * PG, 3), xr=(7 + 5 * PG, 3), fs_=(3 * PG + 1, 3), fr_=(3 * PG + 1, 3),
    )
    scratch = {k: pltpu.VMEM(v, BF16) for k, v in low.items()}
    scratch |= {k: pltpu.VMEM(v, F32) for k, v in wide.items()}
    scratch |= {k: pltpu.SemaphoreType.DMA(v) for k, v in sems.items()}
    return scratch


def fits(cfg):
    D, G, PG, L, C, F = cfg
    return (
        G == 4 and D % 2 == 0 and D >= 4 and L % 128 == 0 and (C // G) % 256 == 0 and C // D == 128 and F // (D * G) == 128
        and (HEADS // G) % 2 == 0 and PG * L * G == C and F // G == C and (L * G) % (C // G) == 0
    )


def fused(cfg, *args):
    D, G, PG, L, C, F = cfg
    SR = C // (D * G)
    scratch = scratch_of(cfg)
    global NAMES
    NAMES = INPUTS + OUTPUTS + list(scratch)
    vmem, anywhere = pl.BlockSpec(memory_space=pltpu.VMEM), pl.BlockSpec(memory_space=pl.ANY)
    where = {"tok": anywhere, "mw": anywhere, "dw": anywhere, "lens": pl.BlockSpec(memory_space=pltpu.SMEM)}
    flat = [a.reshape(1, -1) if name not in ("lens",) and a.ndim == 1 else a for name, a in zip(INPUTS, args)]
    shapes = dict(
        out=(PG, L, C), tg=(PG, L, C), gpw=(SR, 3 * C), gpb=(2, SR), gmw=(SR, C), gmb=(1, SR), gfg=(1, SR), gfs=(1, SR),
        guw=(SR, F), gub=(1, F // (D * G)), gdw=(F // (D * G), C), gdb=(1, SR), glg=(1, SR), gls=(1, SR),
    )
    results = pl.pallas_call(
        functools.partial(layer_kernel, cfg),
        out_shape=[jax.ShapeDtypeStruct(shapes[k], F32) for k in OUTPUTS],
        in_specs=[where.get(k, vmem) for k in INPUTS],
        out_specs=[vmem] * len(OUTPUTS),
        scratch_shapes=list(scratch.values()),
        compiler_params=pltpu.CompilerParams(collective_id=0, has_side_effects=True, vmem_limit_bytes=VMEM_LIMIT),
        name="encoder_layer",
    )(*flat)
    return tuple(v.reshape(-1) if v.shape[0] == 1 else v for v in results)


VMEM_LIMIT = 61 << 20


def per_device(*args):
    tokens, up_weight = args[0], args[9]
    D, G = lax.axis_size("dp"), lax.axis_size("seq")
    cfg = (D, G, tokens.shape[0], tokens.shape[1], tokens.shape[2], up_weight.shape[1])
    return fused(cfg, *args) if fits(cfg) else plain(*args)


MICRO = 2


def matmul(left, right):
    return jnp.dot(left, right, preferred_element_type=jnp.float32)


def against(left, right):
    return jnp.einsum("re,fe->rf", left, right, preferred_element_type=jnp.float32)


def contract_rows(left, right):
    return jnp.einsum("rd,re->de", left, right, preferred_element_type=jnp.float32)


def layer_norm(rows, gain, shift):
    center = rows - jnp.mean(rows, axis=-1, keepdims=True)
    spread = jnp.mean(center * center, axis=-1, keepdims=True)
    return center * lax.rsqrt(spread + 1e-05) * gain + shift


def gelu_exact(value):
    return 0.5 * value * (1.0 + lax.erf(value * 0.7071067811865476))


def masked_scores(query, keys, length):
    scores = jnp.einsum(
        "qhd,khd->hqk", query, keys, preferred_element_type=jnp.float32
    ) * query.shape[-1] ** (-0.5)
    valid = lax.iota(jnp.int32, keys.shape[0]) < length
    return jnp.where(valid[None, None, :], scores, -1e30)


def attend(packed, length):
    query, keys, values = (packed[:, 0], packed[:, 1], packed[:, 2])
    scores = masked_scores(query, keys, length)
    top = jnp.max(scores, axis=-1, keepdims=True)
    powers = jnp.exp(scores - top)
    total = jnp.sum(powers, axis=-1, keepdims=True)
    probs = (powers / total).astype(jnp.bfloat16)
    context = jnp.einsum("hqk,khd->qhd", probs, values, preferred_element_type=jnp.float32)
    return (
        context.astype(jnp.bfloat16).reshape(packed.shape[0], -1),
        (top + jnp.log(total))[..., 0],
    )


def attend_back(packed, context_grad, logsum, length):
    query, keys, values = (packed[:, 0], packed[:, 1], packed[:, 2])
    scale = query.shape[-1] ** (-0.5)
    scores = masked_scores(query, keys, length)
    probs = jnp.exp(scores - logsum[..., None])
    probs_grad = jnp.einsum(
        "qhd,khd->hqk", context_grad, values, preferred_element_type=jnp.float32
    )
    inner = jnp.sum(probs * probs_grad, axis=-1, keepdims=True)
    scores_grad = (probs * (probs_grad - inner)).astype(jnp.bfloat16)
    query_grad = (
        jnp.einsum("hqk,khd->qhd", scores_grad, keys, preferred_element_type=jnp.float32) * scale
    )
    keys_grad = (
        jnp.einsum("hqk,qhd->khd", scores_grad, query, preferred_element_type=jnp.float32) * scale
    )
    values_grad = jnp.einsum(
        "hqk,qhd->khd", probs.astype(jnp.bfloat16), context_grad, preferred_element_type=jnp.float32
    )
    return jnp.stack([query_grad, keys_grad, values_grad], axis=1).astype(jnp.bfloat16)


def plain(
    tokens,
    cotangent,
    lengths,
    project_weight,
    project_bias,
    mixing_weight,
    mixing_bias,
    first_gain,
    first_shift,
    up_weight,
    up_bias,
    down_weight,
    down_bias,
    last_gain,
    last_shift,
):
    groups = lax.axis_size("seq")
    (
        project_full,
        bias_pair,
        mixing_full,
        mixing_shift,
        first_scale,
        first_offset,
        up_full,
        up_shift,
        down_full,
        down_shift,
        last_scale,
        last_offset,
    ) = (
        lax.all_gather(project_weight, ("dp", "seq"), axis=0, tiled=True),
        lax.all_gather(project_bias, ("dp", "seq"), axis=1, tiled=True),
        lax.all_gather(mixing_weight, ("dp", "seq"), axis=0, tiled=True),
        lax.all_gather(mixing_bias, ("dp", "seq"), axis=0, tiled=True),
        lax.all_gather(first_gain, ("dp", "seq"), axis=0, tiled=True),
        lax.all_gather(first_shift, ("dp", "seq"), axis=0, tiled=True),
        lax.all_gather(up_weight, ("dp", "seq"), axis=0, tiled=True),
        lax.all_gather(up_bias, ("dp", "seq"), axis=0, tiled=True),
        lax.all_gather(down_weight, ("dp", "seq"), axis=0, tiled=True),
        lax.all_gather(down_bias, ("dp", "seq"), axis=0, tiled=True),
        lax.all_gather(last_gain, ("dp", "seq"), axis=0, tiled=True),
        lax.all_gather(last_shift, ("dp", "seq"), axis=0, tiled=True),
    )
    bias_pair = bias_pair.astype(jnp.float32)
    mixing_shift = mixing_shift.astype(jnp.float32)
    first_scale = first_scale.astype(jnp.float32)
    first_offset = first_offset.astype(jnp.float32)
    up_shift = up_shift.astype(jnp.float32)
    down_shift = down_shift.astype(jnp.float32)
    last_scale = last_scale.astype(jnp.float32)
    last_offset = last_offset.astype(jnp.float32)
    project_shift = jnp.concatenate([bias_pair[0], jnp.zeros_like(bias_pair[0]), bias_pair[1]])
    pages = tokens.shape[0] // MICRO
    local = tokens.shape[1]
    model = tokens.shape[2]
    width = local * groups
    slice_width = model // groups
    owned = HEADS // groups
    rows = pages * local
    outputs = []
    input_grads = []
    for micro in range(MICRO):
        begin = micro * pages
        flat = tokens[begin : begin + pages].reshape(rows, model)
        spans = lengths[begin : begin + pages]
        packed = (matmul(flat, project_full) + project_shift).astype(jnp.bfloat16)
        per_head = lax.all_to_all(
            packed.reshape(pages, local, 3, groups, slice_width),
            "seq",
            split_axis=3,
            concat_axis=1,
            tiled=True,
        )
        per_head = per_head.reshape(pages, width, 3, owned, HEAD_DIM)
        context, logsum = lax.map(lambda item: attend(item[0], item[1]), (per_head, spans))
        mixed = lax.all_to_all(context, "seq", split_axis=1, concat_axis=2, tiled=True).reshape(
            rows, model
        )
        residual = flat.astype(jnp.float32) + matmul(mixed, mixing_full) + mixing_shift
        normed, first_pull = jax.vjp(layer_norm, residual, first_scale, first_offset)
        normed_low = normed.astype(jnp.bfloat16)
        hidden_in = matmul(normed_low, up_full) + up_shift
        hidden_value, gelu_pull = jax.vjp(gelu_exact, hidden_in)
        activation = hidden_value.astype(jnp.bfloat16)
        last_resid = normed + matmul(activation, down_full) + down_shift
        output, last_pull = jax.vjp(layer_norm, last_resid, last_scale, last_offset)
        outputs.append(output.reshape(pages, local, model))
        seed_grad = cotangent[begin : begin + pages].reshape(rows, model).astype(jnp.float32)
        last_resid_grad, last_gain_grad, last_shift_grad = last_pull(seed_grad)
        down_bias_grad = jnp.sum(last_resid_grad, axis=0)
        last_resid_low = last_resid_grad.astype(jnp.bfloat16)
        down_weight_grad = contract_rows(activation, last_resid_low)
        (hidden_grad,) = gelu_pull(against(last_resid_low, down_full))
        up_bias_grad = jnp.sum(hidden_grad, axis=0)
        hidden_low = hidden_grad.astype(jnp.bfloat16)
        up_weight_grad = contract_rows(normed_low, hidden_low)
        feed_part = (
            up_weight_grad,
            up_bias_grad,
            down_weight_grad,
            down_bias_grad,
            last_gain_grad,
            last_shift_grad,
        )
        if micro == 0:
            feed_total = feed_part
        else:
            feed_total = tuple((a + b for a, b in zip(feed_total, feed_part)))
        normed_grad = last_resid_grad + against(hidden_low, up_full)
        first_resid_grad, first_gain_grad, first_shift_grad = first_pull(normed_grad)
        mixing_bias_grad = jnp.sum(first_resid_grad, axis=0)
        first_resid_low = first_resid_grad.astype(jnp.bfloat16)
        mixing_weight_grad = contract_rows(mixed, first_resid_low)
        context_grad = against(first_resid_low, mixing_full).astype(jnp.bfloat16)
        context_heads = lax.all_to_all(
            context_grad.reshape(pages, local, model),
            "seq",
            split_axis=2,
            concat_axis=1,
            tiled=True,
        )
        context_heads = context_heads.reshape(pages, width, owned, HEAD_DIM)
        packed_grad = lax.map(
            lambda item: attend_back(item[0], item[1], item[2], item[3]),
            (per_head, context_heads, logsum, spans),
        )
        packed_grad = lax.all_to_all(
            packed_grad.reshape(pages, width, 3, 1, slice_width),
            "seq",
            split_axis=1,
            concat_axis=3,
            tiled=True,
        )
        packed_grad = packed_grad.reshape(rows, 3 * model)
        bias_grad = jnp.stack(
            [
                jnp.sum(packed_grad[:, :model], axis=0, dtype=jnp.float32),
                jnp.sum(packed_grad[:, 2 * model :], axis=0, dtype=jnp.float32),
            ]
        )
        project_weight_grad = contract_rows(flat, packed_grad)
        input_grads.append(
            (first_resid_grad + against(packed_grad, project_full)).reshape(pages, local, model)
        )
        attend_part = (
            project_weight_grad,
            bias_grad,
            mixing_weight_grad,
            mixing_bias_grad,
            first_gain_grad,
            first_shift_grad,
        )
        if micro == 0:
            attend_total = attend_part
        else:
            attend_total = tuple((a + b for a, b in zip(attend_total, attend_part)))
    shards = (
        lax.psum_scatter(attend_total[0], ("dp", "seq"), scatter_dimension=0, tiled=True),
        lax.psum_scatter(attend_total[1], ("dp", "seq"), scatter_dimension=1, tiled=True),
        lax.psum_scatter(attend_total[2], ("dp", "seq"), scatter_dimension=0, tiled=True),
        lax.psum_scatter(attend_total[3], ("dp", "seq"), scatter_dimension=0, tiled=True),
        lax.psum_scatter(attend_total[4], ("dp", "seq"), scatter_dimension=0, tiled=True),
        lax.psum_scatter(attend_total[5], ("dp", "seq"), scatter_dimension=0, tiled=True),
        lax.psum_scatter(feed_total[0], ("dp", "seq"), scatter_dimension=0, tiled=True),
        lax.psum_scatter(feed_total[1], ("dp", "seq"), scatter_dimension=0, tiled=True),
        lax.psum_scatter(feed_total[2], ("dp", "seq"), scatter_dimension=0, tiled=True),
        lax.psum_scatter(feed_total[3], ("dp", "seq"), scatter_dimension=0, tiled=True),
        lax.psum_scatter(feed_total[4], ("dp", "seq"), scatter_dimension=0, tiled=True),
        lax.psum_scatter(feed_total[5], ("dp", "seq"), scatter_dimension=0, tiled=True),
    )
    layer_output = jnp.concatenate(outputs, axis=0)
    tokens_gradient = jnp.concatenate(input_grads, axis=0)
    return (
        layer_output,
        tokens_gradient,
        shards[0],
        shards[1],
        shards[2],
        shards[3],
        shards[4],
        shards[5],
        shards[6],
        shards[7],
        shards[8],
        shards[9],
        shards[10],
        shards[11],
    )


def solution(mesh):
    placed = (
        P("dp", "seq", None),
        P("dp", "seq", None),
        P("dp"),
        P(("dp", "seq"), None),
        P(None, ("dp", "seq")),
        P(("dp", "seq"), None),
        P(("dp", "seq")),
        P(("dp", "seq")),
        P(("dp", "seq")),
        P(("dp", "seq"), None),
        P(("dp", "seq")),
        P(("dp", "seq"), None),
        P(("dp", "seq")),
        P(("dp", "seq")),
        P(("dp", "seq")),
    )
    return jax.shard_map(
        per_device,
        mesh=mesh,
        in_specs=placed,
        out_specs=(
            P("dp", "seq", None),
            P("dp", "seq", None),
            P(("dp", "seq"), None),
            P(None, ("dp", "seq")),
            P(("dp", "seq"), None),
            P(("dp", "seq")),
            P(("dp", "seq")),
            P(("dp", "seq")),
            P(("dp", "seq"), None),
            P(("dp", "seq")),
            P(("dp", "seq"), None),
            P(("dp", "seq")),
            P(("dp", "seq")),
            P(("dp", "seq")),
        ),
        check_vma=False,
    )
```

```python
import functools
from types import SimpleNamespace

import jax
import jax.numpy as jnp
from jax import lax
from jax.experimental import pallas as pl
from jax.experimental.pallas import tpu as pltpu
from jax.sharding import PartitionSpec as P

HEADS = 16
HEAD_DIM = 64
F32 = jnp.float32
BF16 = jnp.bfloat16
MESH = pl.DeviceIdType.MESH
LANES = 128


def mm(left, right):
    return lax.dot_general(left, right, (((1,), (0,)), ((), ())), preferred_element_type=F32)


def mm_t(left, right):
    return lax.dot_general(left, right, (((1,), (1,)), ((), ())), preferred_element_type=F32)


def loop(count, body):
    def step(i, carry):
        body(i)
        return carry

    lax.fori_loop(0, count, step, 0)


def tile_of(columns):
    return 256 if columns % 256 == 0 else 128


def lanes(index, size):
    return pl.ds(pl.multiple_of(index * size, size), size)


QUERY_BIAS, VALUE_BIAS, MIX_BIAS, GAIN1, SHIFT1, DOWN_BIAS, GAIN2, SHIFT2, UP_BIAS = range(9)
TABLE = 16
PROJECT, MIXING, UP, DOWN_A, DOWN_B, SMALL = range(6)
DOWN = DOWN_A


def layer_kernel(cfg, *refs):
    D, G, PG, L, C, F = cfg
    H = D // 2
    W = L * G
    HC = C // G
    FO = F // G
    CR = C // D
    SR = C // (D * G)
    FR = FO // D
    QC = 3 * HC
    heads = HEADS // G
    r = SimpleNamespace(**dict(zip(NAMES, refs)))

    dp = lax.axis_index("dp")
    s = lax.axis_index("seq")
    xx = lax.div(s, 2)
    cc = lax.rem(s, 2)
    side = lax.rem(dp, 2)
    pos = (1 - side) * lax.div(dp, 2) + side * (D - 1 - lax.div(dp, 2))

    def at_position(p):
        far = lax.div(p, H)
        return (1 - far) * 2 * p + far * (2 * (D - 1 - p) + 1)

    def shifted(k):
        return at_position(lax.rem(pos + (k + D) % D, D))

    right, left = (shifted(1), s), (shifted(-1), s)
    ways = (right, left)
    peer = {1: s + 1 - 2 * cc, 2: s + 2 - 4 * xx, 3: 3 - s}
    sibling, across = (dp, peer[1]), (dp, peer[2])

    def remote(src, dst, send, recv, device):
        return pltpu.make_async_remote_copy(
            src_ref=src, dst_ref=dst, send_sem=send, recv_sem=recv,
            device_id=device, device_id_type=MESH,
        )

    def block(index, size):
        return pl.ds(pl.multiple_of(index * size, size), size)

    local = []

    def load(src, dst):
        copy = pltpu.make_async_copy(src, dst, r.local_sem.at[len(local)])
        copy.start()
        local.append(copy)
        return copy

    load_mix = load(r.mw, r.wm.at[dp, s])
    load_tok = [load(r.tok.at[p], r.xg.at[p, block(s, L)]) for p in range(PG)]
    load_down = load(r.dw, r.wd.at[block(dp, FR)])

    barrier = pltpu.get_barrier_semaphore()
    partners = [right, left] + [(dp, peer[k]) for k in (1, 2, 3)]
    for device in partners:
        pl.semaphore_signal(barrier, inc=1, device_id=device, device_id_type=MESH)

    for q in range(G):
        for b in range(3):
            r.sp[q, :, b * HC:(b + 1) * HC] = r.pw[:, b * C + q * HC:b * C + (q + 1) * HC]
        for j in range(D):
            r.su[q, :, j * FR:(j + 1) * FR] = r.uw[:, (j * G + q) * FR:(j * G + q + 1) * FR]
    r.ss[...] = jnp.zeros_like(r.ss)
    r.ss[QUERY_BIAS:VALUE_BIAS + 1, 0:SR] = r.pb[...].astype(F32)
    for row, ref in ((MIX_BIAS, r.mb), (GAIN1, r.fg), (SHIFT1, r.fs), (DOWN_BIAS, r.db), (GAIN2, r.lg), (SHIFT2, r.ls)):
        r.ss[row:row + 1, 0:SR] = ref[...].astype(F32)
    r.ss[UP_BIAS:UP_BIAS + 1, 0:FR] = r.ub[...].astype(F32)

    pl.semaphore_wait(barrier, len(partners))

    exchanges = []

    def exchange(slot, source, target):
        def copy(k, which):
            return remote(source(peer[k]), target(which), r.xs.at[slot, k - 1], r.xr.at[slot, k - 1], (dp, peer[k]))

        def start():
            exchanges.append(lambda: [copy(k, s).wait_send() for k in (2, 3, 1)])
            for k in (2, 3, 1):
                copy(k, s).start()

        def finish():
            for k in (1, 2, 3):
                copy(k, peer[k]).wait_recv()

        return SimpleNamespace(start=start, finish=finish)

    def spread(slot, block):
        def copy(k):
            which = peer[2] if k == 2 else s
            device = across if k == 1 else sibling
            return remote(block(which), block(which), r.xs.at[slot, k], r.xr.at[slot, k], device)

        def arrived(k, which):
            return remote(block(which), block(which), r.xs.at[slot, k], r.xr.at[slot, k], sibling)

        def start():
            exchanges.append(lambda: [copy(k).wait_send() for k in range(3)])
            copy(1).start()
            copy(0).start()

        def forward():
            arrived(1, peer[2]).wait_recv()
            copy(2).start()

        def finish():
            arrived(0, peer[1]).wait_recv()
            arrived(2, peer[3]).wait_recv()

        return SimpleNamespace(start=start, forward=forward, finish=finish)

    def half_rows(count, half):
        return pl.ds(half * (count // 2), count // 2)

    def rows_of(ref, owner, count, half):
        if half is None:
            return ref.at[block(owner, count)]
        return ref.at[block(owner * 2 + half, count // 2)]

    def side_columns(half):
        return pl.ds(half * (C // 2), C // 2)

    def chunk_view(g, owner, half):
        if g == PROJECT:
            return rows_of(r.wq, owner, CR, half)
        if g == MIXING:
            return r.wm.at[owner, s] if half is None else r.wm.at[owner, s, half_rows(SR, half)]
        if g == UP:
            return rows_of(r.wu, owner, CR, half)
        if g in (DOWN_A, DOWN_B):
            return rows_of(r.wd.at[:, side_columns(g - DOWN_A)], owner, FR, half)
        return r.sm.at[owner] if half is None else r.sm.at[owner, half_rows(G, half)]

    def gather_copy(g, d, t, owner):
        view = chunk_view(g, owner, d if t == H else None)
        return remote(view, view, r.gs.at[g, d, t - 1], r.gr.at[g, d, t - 1], ways[d])

    def sent(d, t):
        return shifted(-(t - 1) if d == 0 else t - 1)

    def gather_send(g, t):
        for d in range(2):
            gather_copy(g, d, t, sent(d, t)).start()

    def gather_step(g, t):
        for d in range(2):
            gather_copy(g, d, t, shifted(-t if d == 0 else t)).wait_recv()
            if t < H:
                gather_copy(g, d, t + 1, sent(d, t + 1)).start()

    fetched = dict.fromkeys(range(6), 0)

    def fetch(g, to=None):
        to = min(H, fetched[g] + 1 if to is None else to)
        while fetched[g] < to:
            fetched[g] += 1
            gather_step(g, fetched[g])

    def gather_drain(g):
        for t in range(1, H + 1):
            for d in range(2):
                gather_copy(g, d, t, sent(d, t)).wait_send()

    give_project = exchange(0, lambda q: r.sp.at[q], lambda q: r.wq.at[block(dp * G + q, SR)])
    give_small = exchange(1, lambda q: r.ss, lambda q: r.sm.at[dp, q])
    give_up = exchange(2, lambda q: r.su.at[q], lambda q: r.wu.at[block(dp * G + q, SR)])
    tokens_in = [spread(3 + p, lambda q, p=p: r.xg.at[p, block(q, L)]) for p in range(PG)]
    give_project.start()
    give_small.start()
    load_mix.wait()
    gather_send(MIXING, 1)
    for p in range(PG):
        load_tok[p].wait()
        tokens_in[p].start()
    give_up.start()
    load_down.wait()
    gather_send(DOWN_A, 1)
    r.wq[block(dp * G + s, SR), :] = r.sp[s]
    r.wu[block(dp * G + s, SR), :] = r.su[s]
    r.sm[dp, s] = r.ss[...]
    give_project.finish()
    gather_send(PROJECT, 1)
    give_small.finish()
    gather_send(SMALL, 1)
    r.vs[...] = jnp.zeros_like(r.vs)
    for t in range(1, H + 1):
        fetch(PROJECT)
        fetch(MIXING)
        fetch(SMALL)
        if t <= PG:
            tokens_in[t - 1].forward()
        if t == H - 1:
            give_up.finish()
            gather_send(UP, 1)
    fetch(DOWN_A)
    mix_in = spread(3 + PG, lambda q: r.wm.at[:, q])
    mix_in.start()

    for row in range(UP_BIAS):
        piece = r.sm[:, 0, row, :]
        for q in range(1, G):
            piece = piece + pltpu.roll(r.sm[:, q, row, :], q * SR, 1)
        for j in range(D):
            r.pv[row:row + 1, j * CR:(j + 1) * CR] = piece[j:j + 1]
    for j in range(D):
        r.ubv[0:1, j * FR:(j + 1) * FR] = r.sm[j, s, UP_BIAS:UP_BIAS + 1, :]
    r.pbv[...] = jnp.zeros_like(r.pbv)
    own_heads = pl.ds(pl.multiple_of(s * HC, HC), HC)
    r.pbv[0:1, 0:HC] = r.pv[QUERY_BIAS:QUERY_BIAS + 1, own_heads]
    r.pbv[0:1, 2 * HC:3 * HC] = r.pv[VALUE_BIAS:VALUE_BIAS + 1, own_heads]

    def param(row):
        return r.pv[row:row + 1, :]

    tq = tile_of(QC)

    def project_page(p):
        def body(n):
            cols = lanes(n, tq)
            r.qkv[p, :, cols] = (mm(r.xg[p], r.wq[:, cols]) + r.pbv[0:1, cols]).astype(BF16)

        loop(QC // tq, body)

    for p in range(PG):
        tokens_in[p].finish()
        project_page(p)
    gather_send(DOWN_B, 1)
    fetch(UP)

    pairs = heads // 2
    QB = 256 if W % 256 == 0 else W
    scale = HEAD_DIM ** -0.5

    def pair_of(p, hp):
        return [r.qkv[p, :, pl.ds(pl.multiple_of(b * HC + hp * LANES, LANES), LANES)] for b in range(3)]

    def only(half, rows):
        lane = lax.broadcasted_iota(jnp.int32, rows.shape, 1)
        mine = lane >= HEAD_DIM if half else lane < HEAD_DIM
        return jnp.where(mine, rows, jnp.zeros_like(rows))

    def attend_page(p):
        length = r.lens[p]

        def body(hp):
            query, keys, values = pair_of(p, hp)
            values_t = values.T
            halves = []
            for half in range(2):
                keys_h = only(half, keys)
                blocks = []
                for qb in range(W // QB):
                    scores = mm_t(keys_h, query[qb * QB:(qb + 1) * QB])
                    at_key = lax.broadcasted_iota(jnp.int32, scores.shape, 0)
                    scores = jnp.where(at_key < length, scores, -1e30)
                    top = jnp.max(scores, axis=0, keepdims=True)
                    powers = jnp.exp((scores - top) * scale)
                    probs = powers * (1.0 / jnp.sum(powers, axis=0, keepdims=True))
                    r.probs[(p * pairs + hp) * 2 + half, :, qb * QB:(qb + 1) * QB] = probs
                    blocks.append(mm(values_t[half * HEAD_DIM:(half + 1) * HEAD_DIM], probs.astype(BF16)))
                halves.append(jnp.concatenate(blocks, axis=1))
            both = jnp.concatenate(halves, axis=0).T
            r.ctx[p, :, lanes(hp, LANES)] = both.astype(BF16)

        loop(pairs, body)

    context_out = [
        exchange(4 + PG + p, lambda q, p=p: r.ctx.at[p, block(q, L)],
                 lambda q, p=p: r.cr.at[p, :, block(q, HC)])
        for p in range(PG)
    ]
    for p in range(PG):
        attend_page(p)
        context_out[p].start()
        r.cr[p, :, own_heads] = r.ctx[p, block(s, L), :]
        if p == 0:
            mix_in.forward()
        fetch(DOWN_A)
        fetch(UP)
    mix_in.finish()

    own_rows = pl.ds(pl.multiple_of(s * L, L), L)
    tc = tile_of(C)

    def mix_page(p):
        def body(n):
            cols = lanes(n, tc)
            r.tg[p, :, cols] = mm(r.cr[p], r.wm[:, :, :, cols].reshape(C, tc))

        loop(C // tc, body)

    RB = 32

    def by_rows(p, body):
        def step(i):
            body(pl.ds(pl.multiple_of(i * RB, RB), RB), pl.ds(pl.multiple_of(s * L + i * RB, RB), RB))

        loop(L // RB, step)

    def standard(rows):
        center = rows - jnp.mean(rows, axis=-1, keepdims=True)
        inverse = lax.rsqrt(jnp.mean(center * center, axis=-1, keepdims=True) + 1e-05)
        return center * inverse, inverse

    def unstandard(grad, nhat, inverse):
        return inverse * (
            grad - jnp.mean(grad, axis=-1, keepdims=True) - nhat * jnp.mean(grad * nhat, axis=-1, keepdims=True)
        )

    def add_row(row, rows):
        r.vs[row:row + 1, :] += jnp.sum(rows, axis=0, keepdims=True)

    normed_in = [spread(4 + 2 * PG + p, lambda q, p=p: r.nlg.at[p, block(q, L)]) for p in range(PG)]

    def first_norm(p):
        def body(rows, group_rows):
            resid = r.xg[p, group_rows, :].astype(F32) + r.tg[p, rows, :] + param(MIX_BIAS)
            nhat, inverse = standard(resid)
            normed = nhat * param(GAIN1) + param(SHIFT1)
            r.nh1[p, rows, :] = nhat
            r.inv1[p, rows, :] = jnp.broadcast_to(inverse, (RB, LANES))
            r.tg[p, rows, :] = normed
            r.nlg[p, group_rows, :] = normed.astype(BF16)

        by_rows(p, body)

    for p in range(PG):
        context_out[p].finish()
        mix_page(p)
        first_norm(p)
        normed_in[p].start()
    fetch(DOWN_B)
    fetch(UP, H)
    fetch(DOWN_A, H)

    tf = tile_of(FO)

    def up_page(p):
        def body(n):
            cols = lanes(n, tf)
            hidden = mm(r.nlg[p], r.wu[:, cols]) + r.ubv[0:1, cols]
            cdf = 0.5 * (1.0 + lax.erf(hidden * 0.7071067811865476))
            r.act[p, :, cols] = (hidden * cdf).astype(BF16)
            slope = cdf + hidden * (jnp.exp(hidden * hidden * -0.5) * 0.3989422804014327)
            r.gp[p, :, cols] = slope

        loop(FO // tf, body)

    normed_in[0].forward()
    for p in range(PG):
        normed_in[p].finish()
        up_page(p)
        if p + 1 < PG:
            normed_in[p + 1].forward()
        fetch(DOWN_B)

    def fold(slot, part, r1, s2, r2):
        def near(k):
            return remote(part(2 * k + 1 - cc), r1.at[k], r.fs_.at[slot, k], r.fr_.at[slot, k], sibling)

        def far():
            return remote(s2, r2, r.fs_.at[slot, 2], r.fr_.at[slot, 2], across)

        def start():
            for k in range(2):
                near(k).start()

        def drain():
            for k in range(2):
                near(k).wait_send()
            far().wait_send()

        def middle():
            for k in range(2):
                near(k).wait_recv()
            count = s2.shape[0]

            def body(i):
                rows = pl.ds(pl.multiple_of(i * RB, RB), RB)
                s2[rows, :] = (part(peer[2])[rows, :] + r1[1 - xx, rows, :]).astype(BF16)

            loop(count // RB, body)
            far().start()

        def finish():
            far().wait_recv()

        def own(rows):
            return part(s)[rows, :] + r1[xx, rows, :] + r2[rows, :].astype(F32)

        return SimpleNamespace(start=start, middle=middle, finish=finish, own=own, drain=drain)

    def page_fold(slot, p, cols=slice(None)):
        return fold(slot, lambda q: r.part.at[p * G + q, :, cols], r.r1.at[p, :, :, cols], r.s2.at[p, :, cols], r.r2.at[p, :, cols])

    def into_part(p, cols, value):
        r.part[p * G:(p + 1) * G, :, cols] = value.reshape(G, L, value.shape[-1])

    half_columns = C // 2
    down_fold = [[page_fold(2 * p + a, p, pl.ds(a * half_columns, half_columns)) for a in range(2)] for p in range(PG)]

    def down_page(p, a):
        def body(n):
            cols = pl.ds(pl.multiple_of(a * half_columns + n * tc, tc), tc)
            into_part(p, cols, mm(r.act[p], r.wd[:, cols]))

        loop(half_columns // tc, body)

    for a in range(2):
        fetch(DOWN_A + a, H)
        for p in range(PG):
            down_page(p, a)
            down_fold[p][a].start()
        for p in range(PG):
            down_fold[p][a].middle()

    def down_own(p, rows):
        return r.part[p * G + s, rows, :] + r.r1[p, xx, rows, :] + r.r2[p, rows, :].astype(F32)

    last_in = [spread(4 + 3 * PG + p, lambda q, p=p: r.lrg.at[p, block(q, L)]) for p in range(PG)]

    def last_norm(p):
        def body(rows, group_rows):
            resid = r.tg[p, rows, :] + down_own(p, rows) + param(DOWN_BIAS)
            nhat, inverse = standard(resid)
            r.out[p, rows, :] = nhat * param(GAIN2) + param(SHIFT2)
            cot = r.cot[p, rows, :].astype(F32)
            add_row(GAIN2, cot * nhat)
            add_row(SHIFT2, cot)
            grad = unstandard(cot * param(GAIN2), nhat, inverse)
            add_row(DOWN_BIAS, grad)
            r.tg[p, rows, :] = grad
            r.lrg[p, group_rows, :] = grad.astype(BF16)

        by_rows(p, body)

    for p in range(PG):
        for a in range(2):
            down_fold[p][a].finish()
        last_norm(p)
        last_in[p].start()

    def weight_chunks(lhs, rhs, owners, columns, width):
        count = len(owners)
        for i, j in enumerate(owners):
            for p in range(PG):
                r.tt[i * width:(i + 1) * width, p * W:(p + 1) * W] = lhs[p, :, block(j, width)].T
        tn = tile_of(columns)

        def value(n):
            block = rhs[:, :, lanes(n, tn)].reshape(PG * W, tn)
            full = mm(r.tt[0:count * width, :], block)
            return [full[i * width:(i + 1) * width] for i in range(count)]

        return value, columns // tn, tn

    def grad_chunks(g, owners):
        if g == PROJECT:
            return weight_chunks(r.xg, r.qkv, owners, QC, CR)
        if g == UP:
            return weight_chunks(r.nlg, r.hid, owners, FO, CR)
        if g == DOWN:
            return weight_chunks(r.act, r.lrg, owners, C, FR)
        if g == MIXING:
            return (lambda n: [mix_part(s)[block(j, SR), lanes(n, tc)] for j in owners]), C // tc, tc
        return (lambda n: [r.vc[j] for j in owners]), 1, CR

    bufs = {PROJECT: (r.bp, r.tp), MIXING: (r.bm, r.tm), UP: (r.bu, r.tu), DOWN: (r.bd, r.td), SMALL: (r.bs, r.ts)}

    def ring_copy(g, d, t):
        buf, first = bufs[g]
        count = first.shape[0]
        if t == 1:
            src, dst = first.at[half_rows(count, d)], buf.at[d, 0, half_rows(count, d)]
        else:
            src, dst = buf.at[d, t - 2], buf.at[d, t - 1]
        return remote(src, dst, r.rs.at[g, d, t - 1], r.rr.at[g, d, t - 1], ways[d])

    def ring_first(g):
        buf, first = bufs[g]
        value, count, tn = grad_chunks(g, [shifted(H)])

        def body(n):
            first[:, lanes(n, tn)] = value(n)[0].astype(first.dtype)

        loop(count, body)
        for d in range(2):
            ring_copy(g, d, 1).start()

    def ring_next(g, t):
        buf, first = bufs[g]
        size = first.shape[0]
        hop = H + 1 - t
        for d in range(2):
            ring_copy(g, d, t - 1).wait_recv()
        value, count, tn = grad_chunks(g, [shifted(hop), shifted(-hop)])

        def body(n):
            cols = lanes(n, tn)
            for d, val in enumerate(value(n)):
                if t == 2:
                    near, off = half_rows(size, d), half_rows(size, 1 - d)
                    lo, hi = d * (size // 2), (1 - d) * (size // 2)
                    buf[d, 0, near, cols] = (val[lo:lo + size // 2] + buf[d, 0, near, cols].astype(F32)).astype(buf.dtype)
                    buf[d, 0, off, cols] = val[hi:hi + size // 2].astype(buf.dtype)
                else:
                    buf[d, t - 2, :, cols] = (val + buf[d, t - 2, :, cols].astype(F32)).astype(buf.dtype)

        loop(count, body)
        for d in range(2):
            ring_copy(g, d, t).start()

    def ring_last(g, put):
        advance(g, H)
        buf, first = bufs[g]
        for d in range(2):
            ring_copy(g, d, H).wait_recv()
        value, count, tn = grad_chunks(g, [dp])

        def body(n):
            cols = lanes(n, tn)
            put(cols, value(n)[0] + buf[0, H - 1, :, cols].astype(F32) + buf[1, H - 1, :, cols].astype(F32))

        loop(count, body)
        for t in range(1, H + 1):
            for d in range(2):
                ring_copy(g, d, t).wait_send()

    reached = dict.fromkeys(range(6), 0)

    def advance(g, to=None):
        to = min(H, reached[g] + 1 if to is None else to)
        while reached[g] < to:
            reached[g] += 1
            ring_first(g) if reached[g] == 1 else ring_next(g, reached[g])

    def hidden_page(p):
        def body(n):
            cols = lanes(n, tf)
            grad = mm_t(r.lrg[p], r.wd[cols, :]) * r.gp[p, :, cols]
            r.vu[0:1, cols] += jnp.sum(grad, axis=0, keepdims=True)
            r.hid[p, :, cols] = grad.astype(BF16)

        loop(FO // tf, body)

    r.vu[...] = jnp.zeros_like(r.vu)
    normed_fold = [page_fold(2 * PG + p, p) for p in range(PG)]

    def normed_page(p):
        def body(n):
            cols = lanes(n, tc)
            into_part(p, cols, mm_t(r.hid[p], r.wu[cols, :]))

        loop(C // tc, body)

    for p in range(PG):
        last_in[p].forward()
        last_in[p].finish()
        if p == PG - 1:
            advance(DOWN)
        hidden_page(p)
        if p == PG - 1:
            advance(UP)
        for a in range(2):
            down_fold[p][a].drain()
        normed_page(p)
        normed_fold[p].start()
        normed_fold[p].middle()
    advance(DOWN)

    grads_out = [
        exchange(4 + 4 * PG + p, lambda q, p=p: r.cg.at[p, :, block(q, HC)],
                 lambda q, p=p: r.dc.at[p, block(q, L)])
        for p in range(PG)
    ]

    def first_back(p):
        def body(rows, group_rows):
            grad = r.tg[p, rows, :] + normed_fold[p].own(rows)
            nhat = r.nh1[p, rows, :]
            add_row(GAIN1, grad * nhat)
            add_row(SHIFT1, grad)
            grad = unstandard(grad * param(GAIN1), nhat, r.inv1[p, rows, 0:1])
            add_row(MIX_BIAS, grad)
            r.tg[p, rows, :] = grad
            r.frl[p, rows, :] = grad.astype(BF16)

        by_rows(p, body)

    def context_back(p):
        def body(n):
            cols = lanes(n, tc)
            r.cg[p, :, cols] = mm_t(r.frl[p], r.wm[block(n, tc // CR)].reshape(tc, C)).astype(BF16)

        loop(C // tc, body)

    for p in range(PG):
        normed_fold[p].finish()
        first_back(p)
        context_back(p)
        grads_out[p].start()
        r.dc[p, own_rows, :] = r.cg[p, :, own_heads]
        advance(UP)

    def mix_part(q):
        return r.gp.at[lax.div(q, W // HC), block(lax.rem(q, W // HC), HC)]

    for i in range(C // 256):
        for p in range(PG):
            r.tm_[:, p * L:(p + 1) * L] = r.cr[p, :, i * 256:(i + 1) * 256].T

        def body(n, i=i):
            cols = lanes(n, tc)
            full = mm(r.tm_[...], r.frl[:, :, cols].reshape(PG * L, tc))
            for k in range(256 // SR):
                j, q = divmod(i * (256 // SR) + k, G)
                r.gp[q * HC // W, q * HC % W + j * SR:q * HC % W + (j + 1) * SR, cols] = full[k * SR:(k + 1) * SR]

        loop(C // tc, body)
    mix_fold = fold(4 * PG, mix_part, r.m1, r.ms2, r.mr2)
    mix_fold.start()
    advance(DOWN)
    mix_fold.middle()

    def attend_back_page(p):
        def body(hp):
            query, keys, values = pair_of(p, hp)
            d_ctx = r.dc[p, :, lanes(hp, LANES)]
            keys_t = keys.T
            d_query, d_keys, d_values = [], None, None
            for half in range(2):
                values_h = only(half, values)
                row = []
                for qb in range(W // QB):
                    span = slice(qb * QB, (qb + 1) * QB)
                    d_probs = mm_t(values_h, d_ctx[span])
                    probs = r.probs[(p * pairs + hp) * 2 + half, :, span]
                    inner = jnp.sum(probs * d_probs, axis=0, keepdims=True)
                    d_scores = (probs * (d_probs - inner)).astype(BF16)
                    row.append(mm(keys_t[half * HEAD_DIM:(half + 1) * HEAD_DIM], d_scores))
                    dk = mm(d_scores, only(half, query[span]))
                    dv = mm(probs.astype(BF16), only(half, d_ctx[span]))
                    d_keys = dk if d_keys is None else d_keys + dk
                    d_values = dv if d_values is None else d_values + dv
                d_query.append(jnp.concatenate(row, axis=1))
            d_query = jnp.concatenate(d_query, axis=0).T * scale
            for b, val in enumerate((d_query, d_keys * scale, d_values)):
                cols = pl.ds(pl.multiple_of(b * HC + hp * LANES, LANES), LANES)
                low = val.astype(BF16)
                r.qkv[p, :, cols] = low
                r.vp[0:1, cols] += jnp.sum(low.astype(F32), axis=0, keepdims=True)

        for hp in range(pairs):
            body(hp)
            ring_between(p, hp)

    r.vp[...] = jnp.zeros_like(r.vp)
    tokens_fold = [page_fold(3 * PG + p, p) for p in range(PG)]

    def tokens_page(p):
        def body(n):
            cols = lanes(n, tc)
            into_part(p, cols, mm_t(r.qkv[p], r.wq[cols, :]))

        loop(C // tc, body)

    def own_mix(i):
        rows = pl.ds(pl.multiple_of(i * RB, RB), RB)
        mix_part(s)[rows, :] = mix_fold.own(rows)

    def ring_between(p, hp):
        step = p * pairs + hp
        if step % 2 == 0:
            advance(DOWN)
        else:
            advance(UP)
        if step == PG * pairs - 2:
            mix_fold.finish()
            loop(HC // RB, own_mix)
            advance(MIXING)

    for p in range(PG):
        grads_out[p].finish()
        attend_back_page(p)
    advance(PROJECT)
    advance(MIXING)

    r.vs[QUERY_BIAS:QUERY_BIAS + 1, own_heads] = r.vp[0:1, 0:HC]
    r.vs[VALUE_BIAS:VALUE_BIAS + 1, own_heads] = r.vp[0:1, 2 * HC:3 * HC]
    for j in range(D):
        r.vc[j] = r.vs[:, j * CR:(j + 1) * CR]
        r.vc[j, UP_BIAS:UP_BIAS + 1, :] = r.vu[0:1, j * FR:(j + 1) * FR]
    advance(SMALL)
    for p in range(PG):
        normed_fold[p].drain()
        tokens_page(p)
        tokens_fold[p].start()
        if p == 0:
            advance(PROJECT)
            advance(SMALL)
            advance(MIXING)
        tokens_fold[p].middle()

    up_out = exchange(4 + 5 * PG, lambda q: r.fu.at[block(q, SR)], lambda q: r.fur.at[q])

    advance(UP, H)
    advance(PROJECT)
    advance(SMALL)
    advance(MIXING)
    ring_last(UP, lambda cols, val: r.fu.__setitem__((slice(None), cols), val))
    up_out.start()
    r.fur[s] = r.fu[block(s, SR), :]
    advance(PROJECT)
    advance(SMALL)
    advance(MIXING)
    ring_last(DOWN, lambda cols, val: r.gdw.__setitem__((slice(None), cols), val))

    for p in range(PG):
        tokens_fold[p].finish()

        def token_rows(rows, group_rows, p=p):
            r.tg[p, rows, :] = r.tg[p, rows, :] + tokens_fold[p].own(rows)

        by_rows(p, token_rows)
    up_out.finish()
    for q in range(G):
        for j in range(D):
            r.guw[:, (j * G + q) * FR:(j * G + q + 1) * FR] = r.fur[q, :, j * FR:(j + 1) * FR]

    project_out = exchange(5 + 5 * PG, lambda q: r.fp.at[block(q, SR)], lambda q: r.fpr.at[q])
    small_out = exchange(6 + 5 * PG, lambda q: r.fsm, lambda q: r.fsr.at[q])
    ring_last(PROJECT, lambda cols, val: r.fp.__setitem__((slice(None), cols), val))
    project_out.start()
    ring_last(SMALL, lambda cols, val: r.fsm.__setitem__((slice(None), cols), val))
    small_out.start()
    ring_last(MIXING, lambda cols, val: r.gmw.__setitem__((slice(None), cols), val))
    r.fpr[s] = r.fp[block(s, SR), :]
    r.fsr[s] = r.fsm[...]
    project_out.finish()
    for q in range(G):
        for b in range(3):
            r.gpw[:, b * C + q * HC:b * C + (q + 1) * HC] = r.fpr[q, :, b * HC:(b + 1) * HC]
    small_out.finish()
    total = r.fsr[0]
    for q in range(1, G):
        total = total + r.fsr[q]
    mine = jnp.zeros((TABLE, SR), F32)
    for q in range(G):
        mine = mine + jnp.where(s == q, 1.0, 0.0) * pltpu.roll(total, (CR - q * SR) % CR, 1)[:, 0:SR]
    r.small[:, 0:SR] = mine
    r.small[UP_BIAS:UP_BIAS + 1, :] = r.fsm[UP_BIAS:UP_BIAS + 1, :]

    for g in range(6):
        gather_drain(g)
    for one in tokens_fold + [mix_fold]:
        one.drain()
    for done in exchanges:
        done()

INPUTS = ["tok", "cot", "lens", "pw", "pb", "mw", "mb", "fg", "fs", "uw", "ub", "dw", "db", "lg", "ls"]
BIG = ["out", "tg", "gpw", "gmw", "guw", "gdw"]
OUTPUTS = ["out", "tg", "gpw", "gpb", "gmw", "gmb", "gfg", "gfs", "guw", "gub", "gdw", "gdb", "glg", "gls"]
ROWS = dict(
    gpb=(QUERY_BIAS, 2), gmb=(MIX_BIAS, 1), gfg=(GAIN1, 1), gfs=(SHIFT1, 1), gub=(UP_BIAS, 1), gdb=(DOWN_BIAS, 1),
    glg=(GAIN2, 1), gls=(SHIFT2, 1),
)


def scratch_of(cfg):
    D, G, PG, L, C, F = cfg
    H = D // 2
    W, HC, FO, CR, SR = L * G, C // G, F // G, C // D, C // (D * G)
    FR, QC, heads = FO // D, 3 * HC, HEADS // G
    low = dict(
        wq=(C, QC), wm=(D, G, SR, C), wu=(C, FO), wd=(FO, C), sp=(G, SR, QC), su=(G, SR, FO), xg=(PG, W, C),
        qkv=(PG, W, QC), ctx=(PG, W, HC), cr=(PG, L, C), nlg=(PG, W, C), act=(PG, W, FO), hid=(PG, W, FO),
        s2=(PG, L, C), r2=(PG, L, C), lrg=(PG, W, C), frl=(PG, L, C), cg=(PG, L, C), dc=(PG, W, HC),
        ms2=(HC, C), mr2=(HC, C), tt=(2 * max(CR, FR), PG * W), tm_=(256, PG * L),
        bp=(2, H, CR, QC), tp=(CR, QC), bm=(2, H, SR, C), tm=(SR, C), bu=(2, H, CR, FO), tu=(CR, FO),
        bd=(2, H, FR, C), td=(FR, C),
    )
    wide = dict(
        ss=(TABLE, LANES), sm=(D, G, TABLE, LANES), probs=(PG * heads, W, W), nh1=(PG, L, C),
        inv1=(PG, L, LANES), gp=(PG, W, FO), part=(PG * G, L, C), r1=(PG, 2, L, C), m1=(2, HC, C),
        bs=(2, H, TABLE, CR), ts=(TABLE, CR), vs=(TABLE, C), vp=(8, QC), vu=(8, FO), vc=(D, TABLE, CR),
        pv=(TABLE, C), ubv=(8, FO), pbv=(8, QC), fu=(CR, FO), fur=(G, SR, FO), fp=(CR, QC), fpr=(G, SR, QC),
        fsm=(TABLE, CR), fsr=(G, TABLE, CR),
    )
    sems = dict(
        local_sem=(2 + PG,), gs=(6, 2, H), gr=(6, 2, H), rs=(6, 2, H), rr=(6, 2, H),
        xs=(7 + 5 * PG, 3), xr=(7 + 5 * PG, 3), fs_=(4 * PG + 1, 3), fr_=(4 * PG + 1, 3),
    )
    scratch = {k: pltpu.VMEM(v, BF16) for k, v in low.items()}
    scratch |= {k: pltpu.VMEM(v, F32) for k, v in wide.items()}
    scratch |= {k: pltpu.SemaphoreType.DMA(v) for k, v in sems.items()}
    return scratch


def fits(cfg):
    D, G, PG, L, C, F = cfg
    return (
        G == 4 and D % 2 == 0 and D >= 4 and L % 128 == 0 and (C // G) % 256 == 0 and C // D == 128 and F // (D * G) == 128
        and (HEADS // G) % 2 == 0 and PG * L * G == C and F // G == C and (L * G) % (C // G) == 0
    )


def fused(cfg, *args):
    D, G, PG, L, C, F = cfg
    SR = C // (D * G)
    scratch = scratch_of(cfg)
    global NAMES
    NAMES = INPUTS + BIG + ["small"] + list(scratch)
    vmem, anywhere = pl.BlockSpec(memory_space=pltpu.VMEM), pl.BlockSpec(memory_space=pl.ANY)
    where = {"tok": anywhere, "mw": anywhere, "dw": anywhere, "lens": pl.BlockSpec(memory_space=pltpu.SMEM)}
    flat = [a.reshape(1, -1) if name not in ("lens",) and a.ndim == 1 else a for name, a in zip(INPUTS, args)]
    shapes = dict(
        out=(PG, L, C), tg=(PG, L, C), gpw=(SR, 3 * C), gpb=(2, SR), gmw=(SR, C), gmb=(1, SR), gfg=(1, SR), gfs=(1, SR),
        guw=(SR, F), gub=(1, F // (D * G)), gdw=(F // (D * G), C), gdb=(1, SR), glg=(1, SR), gls=(1, SR),
    )
    given = pl.pallas_call(
        functools.partial(layer_kernel, cfg),
        out_shape=[jax.ShapeDtypeStruct(shapes[k], F32) for k in BIG] + [jax.ShapeDtypeStruct((TABLE, LANES), F32)],
        in_specs=[where.get(k, vmem) for k in INPUTS],
        out_specs=[vmem] * (len(BIG) + 1),
        scratch_shapes=list(scratch.values()),
        compiler_params=pltpu.CompilerParams(collective_id=0, has_side_effects=True, vmem_limit_bytes=VMEM_LIMIT),
        name="encoder_layer",
    )(*flat)
    count = len(BIG)
    results = pl.pallas_call(
        write_out,
        out_shape=[jax.ShapeDtypeStruct(shapes[k], F32) for k in OUTPUTS],
        in_specs=[anywhere] * count + [vmem],
        out_specs=[anywhere if k in BIG else vmem for k in OUTPUTS],
        scratch_shapes=[pltpu.VMEM(shapes[k], F32) for k in BIG] + [pltpu.SemaphoreType.DMA((2, count))],
        compiler_params=pltpu.CompilerParams(vmem_limit_bytes=VMEM_LIMIT),
        name="write_out",
    )(*given)
    return tuple(v.reshape(-1) if v.shape[0] == 1 else v for v in results)


def write_out(*refs):
    count = len(BIG)
    given, small = refs[:count], refs[count]
    result = dict(zip(OUTPUTS, refs[count + 1:]))
    held, sems = refs[count + 1 + len(OUTPUTS):-1], refs[-1]
    fetch = [pltpu.make_async_copy(given[i], held[i], sems.at[0, i]) for i in range(count)]
    store = [pltpu.make_async_copy(held[i], result[k], sems.at[1, i]) for i, k in enumerate(BIG)]
    for copy in fetch:
        copy.start()
    for k, (row, rows) in ROWS.items():
        result[k][...] = small[row:row + rows, 0:result[k].shape[1]]
    for i in range(count):
        fetch[i].wait()
        store[i].start()
    for copy in store:
        copy.wait()


VMEM_LIMIT = 63 << 20


def per_device(*args):
    tokens, up_weight = args[0], args[9]
    D, G = lax.axis_size("dp"), lax.axis_size("seq")
    cfg = (D, G, tokens.shape[0], tokens.shape[1], tokens.shape[2], up_weight.shape[1])
    return fused(cfg, *args) if fits(cfg) else plain(*args)


MICRO = 2


def matmul(left, right):
    return jnp.dot(left, right, preferred_element_type=jnp.float32)


def against(left, right):
    return jnp.einsum("re,fe->rf", left, right, preferred_element_type=jnp.float32)


def contract_rows(left, right):
    return jnp.einsum("rd,re->de", left, right, preferred_element_type=jnp.float32)


def layer_norm(rows, gain, shift):
    center = rows - jnp.mean(rows, axis=-1, keepdims=True)
    spread = jnp.mean(center * center, axis=-1, keepdims=True)
    return center * lax.rsqrt(spread + 1e-05) * gain + shift


def gelu_exact(value):
    return 0.5 * value * (1.0 + lax.erf(value * 0.7071067811865476))


def masked_scores(query, keys, length):
    scores = jnp.einsum(
        "qhd,khd->hqk", query, keys, preferred_element_type=jnp.float32
    ) * query.shape[-1] ** (-0.5)
    valid = lax.iota(jnp.int32, keys.shape[0]) < length
    return jnp.where(valid[None, None, :], scores, -1e30)


def attend(packed, length):
    query, keys, values = (packed[:, 0], packed[:, 1], packed[:, 2])
    scores = masked_scores(query, keys, length)
    top = jnp.max(scores, axis=-1, keepdims=True)
    powers = jnp.exp(scores - top)
    total = jnp.sum(powers, axis=-1, keepdims=True)
    probs = (powers / total).astype(jnp.bfloat16)
    context = jnp.einsum("hqk,khd->qhd", probs, values, preferred_element_type=jnp.float32)
    return (
        context.astype(jnp.bfloat16).reshape(packed.shape[0], -1),
        (top + jnp.log(total))[..., 0],
    )


def attend_back(packed, context_grad, logsum, length):
    query, keys, values = (packed[:, 0], packed[:, 1], packed[:, 2])
    scale = query.shape[-1] ** (-0.5)
    scores = masked_scores(query, keys, length)
    probs = jnp.exp(scores - logsum[..., None])
    probs_grad = jnp.einsum(
        "qhd,khd->hqk", context_grad, values, preferred_element_type=jnp.float32
    )
    inner = jnp.sum(probs * probs_grad, axis=-1, keepdims=True)
    scores_grad = (probs * (probs_grad - inner)).astype(jnp.bfloat16)
    query_grad = (
        jnp.einsum("hqk,khd->qhd", scores_grad, keys, preferred_element_type=jnp.float32) * scale
    )
    keys_grad = (
        jnp.einsum("hqk,qhd->khd", scores_grad, query, preferred_element_type=jnp.float32) * scale
    )
    values_grad = jnp.einsum(
        "hqk,qhd->khd", probs.astype(jnp.bfloat16), context_grad, preferred_element_type=jnp.float32
    )
    return jnp.stack([query_grad, keys_grad, values_grad], axis=1).astype(jnp.bfloat16)


def plain(
    tokens,
    cotangent,
    lengths,
    project_weight,
    project_bias,
    mixing_weight,
    mixing_bias,
    first_gain,
    first_shift,
    up_weight,
    up_bias,
    down_weight,
    down_bias,
    last_gain,
    last_shift,
):
    groups = lax.axis_size("seq")
    (
        project_full,
        bias_pair,
        mixing_full,
        mixing_shift,
        first_scale,
        first_offset,
        up_full,
        up_shift,
        down_full,
        down_shift,
        last_scale,
        last_offset,
    ) = (
        lax.all_gather(project_weight, ("dp", "seq"), axis=0, tiled=True),
        lax.all_gather(project_bias, ("dp", "seq"), axis=1, tiled=True),
        lax.all_gather(mixing_weight, ("dp", "seq"), axis=0, tiled=True),
        lax.all_gather(mixing_bias, ("dp", "seq"), axis=0, tiled=True),
        lax.all_gather(first_gain, ("dp", "seq"), axis=0, tiled=True),
        lax.all_gather(first_shift, ("dp", "seq"), axis=0, tiled=True),
        lax.all_gather(up_weight, ("dp", "seq"), axis=0, tiled=True),
        lax.all_gather(up_bias, ("dp", "seq"), axis=0, tiled=True),
        lax.all_gather(down_weight, ("dp", "seq"), axis=0, tiled=True),
        lax.all_gather(down_bias, ("dp", "seq"), axis=0, tiled=True),
        lax.all_gather(last_gain, ("dp", "seq"), axis=0, tiled=True),
        lax.all_gather(last_shift, ("dp", "seq"), axis=0, tiled=True),
    )
    bias_pair = bias_pair.astype(jnp.float32)
    mixing_shift = mixing_shift.astype(jnp.float32)
    first_scale = first_scale.astype(jnp.float32)
    first_offset = first_offset.astype(jnp.float32)
    up_shift = up_shift.astype(jnp.float32)
    down_shift = down_shift.astype(jnp.float32)
    last_scale = last_scale.astype(jnp.float32)
    last_offset = last_offset.astype(jnp.float32)
    project_shift = jnp.concatenate([bias_pair[0], jnp.zeros_like(bias_pair[0]), bias_pair[1]])
    pages = tokens.shape[0] // MICRO
    local = tokens.shape[1]
    model = tokens.shape[2]
    width = local * groups
    slice_width = model // groups
    owned = HEADS // groups
    rows = pages * local
    outputs = []
    input_grads = []
    for micro in range(MICRO):
        begin = micro * pages
        flat = tokens[begin : begin + pages].reshape(rows, model)
        spans = lengths[begin : begin + pages]
        packed = (matmul(flat, project_full) + project_shift).astype(jnp.bfloat16)
        per_head = lax.all_to_all(
            packed.reshape(pages, local, 3, groups, slice_width),
            "seq",
            split_axis=3,
            concat_axis=1,
            tiled=True,
        )
        per_head = per_head.reshape(pages, width, 3, owned, HEAD_DIM)
        context, logsum = lax.map(lambda item: attend(item[0], item[1]), (per_head, spans))
        mixed = lax.all_to_all(context, "seq", split_axis=1, concat_axis=2, tiled=True).reshape(
            rows, model
        )
        residual = flat.astype(jnp.float32) + matmul(mixed, mixing_full) + mixing_shift
        normed, first_pull = jax.vjp(layer_norm, residual, first_scale, first_offset)
        normed_low = normed.astype(jnp.bfloat16)
        hidden_in = matmul(normed_low, up_full) + up_shift
        hidden_value, gelu_pull = jax.vjp(gelu_exact, hidden_in)
        activation = hidden_value.astype(jnp.bfloat16)
        last_resid = normed + matmul(activation, down_full) + down_shift
        output, last_pull = jax.vjp(layer_norm, last_resid, last_scale, last_offset)
        outputs.append(output.reshape(pages, local, model))
        seed_grad = cotangent[begin : begin + pages].reshape(rows, model).astype(jnp.float32)
        last_resid_grad, last_gain_grad, last_shift_grad = last_pull(seed_grad)
        down_bias_grad = jnp.sum(last_resid_grad, axis=0)
        last_resid_low = last_resid_grad.astype(jnp.bfloat16)
        down_weight_grad = contract_rows(activation, last_resid_low)
        (hidden_grad,) = gelu_pull(against(last_resid_low, down_full))
        up_bias_grad = jnp.sum(hidden_grad, axis=0)
        hidden_low = hidden_grad.astype(jnp.bfloat16)
        up_weight_grad = contract_rows(normed_low, hidden_low)
        feed_part = (
            up_weight_grad,
            up_bias_grad,
            down_weight_grad,
            down_bias_grad,
            last_gain_grad,
            last_shift_grad,
        )
        if micro == 0:
            feed_total = feed_part
        else:
            feed_total = tuple((a + b for a, b in zip(feed_total, feed_part)))
        normed_grad = last_resid_grad + against(hidden_low, up_full)
        first_resid_grad, first_gain_grad, first_shift_grad = first_pull(normed_grad)
        mixing_bias_grad = jnp.sum(first_resid_grad, axis=0)
        first_resid_low = first_resid_grad.astype(jnp.bfloat16)
        mixing_weight_grad = contract_rows(mixed, first_resid_low)
        context_grad = against(first_resid_low, mixing_full).astype(jnp.bfloat16)
        context_heads = lax.all_to_all(
            context_grad.reshape(pages, local, model),
            "seq",
            split_axis=2,
            concat_axis=1,
            tiled=True,
        )
        context_heads = context_heads.reshape(pages, width, owned, HEAD_DIM)
        packed_grad = lax.map(
            lambda item: attend_back(item[0], item[1], item[2], item[3]),
            (per_head, context_heads, logsum, spans),
        )
        packed_grad = lax.all_to_all(
            packed_grad.reshape(pages, width, 3, 1, slice_width),
            "seq",
            split_axis=1,
            concat_axis=3,
            tiled=True,
        )
        packed_grad = packed_grad.reshape(rows, 3 * model)
        bias_grad = jnp.stack(
            [
                jnp.sum(packed_grad[:, :model], axis=0, dtype=jnp.float32),
                jnp.sum(packed_grad[:, 2 * model :], axis=0, dtype=jnp.float32),
            ]
        )
        project_weight_grad = contract_rows(flat, packed_grad)
        input_grads.append(
            (first_resid_grad + against(packed_grad, project_full)).reshape(pages, local, model)
        )
        attend_part = (
            project_weight_grad,
            bias_grad,
            mixing_weight_grad,
            mixing_bias_grad,
            first_gain_grad,
            first_shift_grad,
        )
        if micro == 0:
            attend_total = attend_part
        else:
            attend_total = tuple((a + b for a, b in zip(attend_total, attend_part)))
    shards = (
        lax.psum_scatter(attend_total[0], ("dp", "seq"), scatter_dimension=0, tiled=True),
        lax.psum_scatter(attend_total[1], ("dp", "seq"), scatter_dimension=1, tiled=True),
        lax.psum_scatter(attend_total[2], ("dp", "seq"), scatter_dimension=0, tiled=True),
        lax.psum_scatter(attend_total[3], ("dp", "seq"), scatter_dimension=0, tiled=True),
        lax.psum_scatter(attend_total[4], ("dp", "seq"), scatter_dimension=0, tiled=True),
        lax.psum_scatter(attend_total[5], ("dp", "seq"), scatter_dimension=0, tiled=True),
        lax.psum_scatter(feed_total[0], ("dp", "seq"), scatter_dimension=0, tiled=True),
        lax.psum_scatter(feed_total[1], ("dp", "seq"), scatter_dimension=0, tiled=True),
        lax.psum_scatter(feed_total[2], ("dp", "seq"), scatter_dimension=0, tiled=True),
        lax.psum_scatter(feed_total[3], ("dp", "seq"), scatter_dimension=0, tiled=True),
        lax.psum_scatter(feed_total[4], ("dp", "seq"), scatter_dimension=0, tiled=True),
        lax.psum_scatter(feed_total[5], ("dp", "seq"), scatter_dimension=0, tiled=True),
    )
    layer_output = jnp.concatenate(outputs, axis=0)
    tokens_gradient = jnp.concatenate(input_grads, axis=0)
    return (
        layer_output,
        tokens_gradient,
        shards[0],
        shards[1],
        shards[2],
        shards[3],
        shards[4],
        shards[5],
        shards[6],
        shards[7],
        shards[8],
        shards[9],
        shards[10],
        shards[11],
    )


def solution(mesh):
    placed = (
        P("dp", "seq", None),
        P("dp", "seq", None),
        P("dp"),
        P(("dp", "seq"), None),
        P(None, ("dp", "seq")),
        P(("dp", "seq"), None),
        P(("dp", "seq")),
        P(("dp", "seq")),
        P(("dp", "seq")),
        P(("dp", "seq"), None),
        P(("dp", "seq")),
        P(("dp", "seq"), None),
        P(("dp", "seq")),
        P(("dp", "seq")),
        P(("dp", "seq")),
    )
    return jax.shard_map(
        per_device,
        mesh=mesh,
        in_specs=placed,
        out_specs=(
            P("dp", "seq", None),
            P("dp", "seq", None),
            P(("dp", "seq"), None),
            P(None, ("dp", "seq")),
            P(("dp", "seq"), None),
            P(("dp", "seq")),
            P(("dp", "seq")),
            P(("dp", "seq")),
            P(("dp", "seq"), None),
            P(("dp", "seq")),
            P(("dp", "seq"), None),
            P(("dp", "seq")),
            P(("dp", "seq")),
            P(("dp", "seq")),
        ),
        check_vma=False,
    )
```

```python
import functools
from types import SimpleNamespace

import jax
import jax.numpy as jnp
from jax import lax
from jax.experimental import pallas as pl
from jax.experimental.pallas import tpu as pltpu
from jax.sharding import PartitionSpec as P

HEADS = 16
HEAD_DIM = 64
F32 = jnp.float32
BF16 = jnp.bfloat16
MESH = pl.DeviceIdType.MESH
LANES = 128


def mm(left, right):
    return lax.dot_general(left, right, (((1,), (0,)), ((), ())), preferred_element_type=F32)


def mm_t(left, right):
    return lax.dot_general(left, right, (((1,), (1,)), ((), ())), preferred_element_type=F32)


def loop(count, body):
    def step(i, carry):
        body(i)
        return carry

    lax.fori_loop(0, count, step, 0)


def tile_of(columns, most=512):
    return next(size for size in (512, 384, 256, 128) if size <= most and columns % size == 0)


def lanes(index, size):
    return pl.ds(pl.multiple_of(index * size, size), size)


QUERY_BIAS, VALUE_BIAS, MIX_BIAS, GAIN1, SHIFT1, DOWN_BIAS, GAIN2, SHIFT2, UP_BIAS = range(9)
TABLE = 16
PROJECT, MIXING, UP, DOWN_A, DOWN_B, SMALL = range(6)
DOWN = DOWN_A


def layer_kernel(cfg, *refs):
    D, G, PG, L, C, F = cfg
    H = D // 2
    W = L * G
    HC = C // G
    FO = F // G
    CR = C // D
    SR = C // (D * G)
    FR = FO // D
    QC = 3 * HC
    heads = HEADS // G
    r = SimpleNamespace(**dict(zip(NAMES, refs)))

    dp = lax.axis_index("dp")
    s = lax.axis_index("seq")
    xx = lax.div(s, 2)
    cc = lax.rem(s, 2)
    side = lax.rem(dp, 2)
    pos = (1 - side) * lax.div(dp, 2) + side * (D - 1 - lax.div(dp, 2))

    def at_position(p):
        far = lax.div(p, H)
        return (1 - far) * 2 * p + far * (2 * (D - 1 - p) + 1)

    def shifted(k):
        return at_position(lax.rem(pos + (k + D) % D, D))

    right, left = (shifted(1), s), (shifted(-1), s)
    ways = (right, left)
    peer = {1: s + 1 - 2 * cc, 2: s + 2 - 4 * xx, 3: 3 - s}
    sibling, across = (dp, peer[1]), (dp, peer[2])

    def remote(src, dst, send, recv, device):
        return pltpu.make_async_remote_copy(
            src_ref=src, dst_ref=dst, send_sem=send, recv_sem=recv,
            device_id=device, device_id_type=MESH,
        )

    def block(index, size):
        return pl.ds(pl.multiple_of(index * size, size), size)

    local = []

    def load(src, dst):
        copy = pltpu.make_async_copy(src, dst, r.local_sem.at[len(local)])
        copy.start()
        local.append(copy)
        return copy

    load_mix = load(r.mw, r.wm.at[dp, s])
    load_tok = [load(r.tok.at[p], r.xg.at[p, block(s, L)]) for p in range(PG)]
    load_down = load(r.dw, r.wd.at[block(dp, FR)])

    barrier = pltpu.get_barrier_semaphore()
    partners = [right, left] + [(dp, peer[k]) for k in (1, 2, 3)]
    for device in partners:
        pl.semaphore_signal(barrier, inc=1, device_id=device, device_id_type=MESH)

    for q in range(G):
        for b in range(3):
            r.sp[q, :, b * HC:(b + 1) * HC] = r.pw[:, b * C + q * HC:b * C + (q + 1) * HC]
        for j in range(D):
            r.su[q, :, j * FR:(j + 1) * FR] = r.uw[:, (j * G + q) * FR:(j * G + q + 1) * FR]
    r.ss[...] = jnp.zeros_like(r.ss)
    r.ss[QUERY_BIAS:VALUE_BIAS + 1, 0:SR] = r.pb[...].astype(F32)
    for row, ref in ((MIX_BIAS, r.mb), (GAIN1, r.fg), (SHIFT1, r.fs), (DOWN_BIAS, r.db), (GAIN2, r.lg), (SHIFT2, r.ls)):
        r.ss[row:row + 1, 0:SR] = ref[...].astype(F32)
    r.ss[UP_BIAS:UP_BIAS + 1, 0:FR] = r.ub[...].astype(F32)

    pl.semaphore_wait(barrier, len(partners))

    exchanges = []

    def exchange(slot, source, target):
        def copy(k, which):
            return remote(source(peer[k]), target(which), r.xs.at[slot, k - 1], r.xr.at[slot, k - 1], (dp, peer[k]))

        def start():
            exchanges.append(lambda: [copy(k, s).wait_send() for k in (2, 3, 1)])
            for k in (2, 3, 1):
                copy(k, s).start()

        def finish():
            for k in (1, 2, 3):
                copy(k, peer[k]).wait_recv()

        return SimpleNamespace(start=start, finish=finish)

    def spread(slot, block):
        def copy(k):
            which = peer[2] if k == 2 else s
            device = across if k == 1 else sibling
            return remote(block(which), block(which), r.xs.at[slot, k], r.xr.at[slot, k], device)

        def arrived(k, which):
            return remote(block(which), block(which), r.xs.at[slot, k], r.xr.at[slot, k], sibling)

        def start():
            exchanges.append(lambda: [copy(k).wait_send() for k in range(3)])
            copy(1).start()
            copy(0).start()

        def forward():
            arrived(1, peer[2]).wait_recv()
            copy(2).start()

        def finish():
            arrived(0, peer[1]).wait_recv()
            arrived(2, peer[3]).wait_recv()

        return SimpleNamespace(start=start, forward=forward, finish=finish)

    def half_rows(count, half):
        return pl.ds(half * (count // 2), count // 2)

    def rows_of(ref, owner, count, half):
        if half is None:
            return ref.at[block(owner, count)]
        return ref.at[block(owner * 2 + half, count // 2)]

    def side_columns(half):
        return pl.ds(half * (C // 2), C // 2)

    def chunk_view(g, owner, half):
        if g == PROJECT:
            return rows_of(r.wq, owner, CR, half)
        if g == MIXING:
            return r.wm.at[owner, s] if half is None else r.wm.at[owner, s, half_rows(SR, half)]
        if g == UP:
            return rows_of(r.wu, owner, CR, half)
        if g in (DOWN_A, DOWN_B):
            return rows_of(r.wd.at[:, side_columns(g - DOWN_A)], owner, FR, half)
        return r.sm.at[owner] if half is None else r.sm.at[owner, half_rows(G, half)]

    def gather_copy(g, d, t, owner):
        view = chunk_view(g, owner, d if t == H else None)
        return remote(view, view, r.gs.at[g, d, t - 1], r.gr.at[g, d, t - 1], ways[d])

    def sent(d, t):
        return shifted(-(t - 1) if d == 0 else t - 1)

    def gather_send(g, t):
        for d in range(2):
            gather_copy(g, d, t, sent(d, t)).start()

    def gather_step(g, t):
        for d in range(2):
            gather_copy(g, d, t, shifted(-t if d == 0 else t)).wait_recv()
            if t < H:
                gather_copy(g, d, t + 1, sent(d, t + 1)).start()

    fetched = dict.fromkeys(range(6), 0)

    def fetch(g, to=None):
        to = min(H, fetched[g] + 1 if to is None else to)
        while fetched[g] < to:
            fetched[g] += 1
            gather_step(g, fetched[g])

    def gather_drain(g):
        for t in range(1, H + 1):
            for d in range(2):
                gather_copy(g, d, t, sent(d, t)).wait_send()

    give_project = exchange(0, lambda q: r.sp.at[q], lambda q: r.wq.at[block(dp * G + q, SR)])
    give_small = exchange(1, lambda q: r.ss, lambda q: r.sm.at[dp, q])
    give_up = exchange(2, lambda q: r.su.at[q], lambda q: r.wu.at[block(dp * G + q, SR)])
    tokens_in = [spread(3 + p, lambda q, p=p: r.xg.at[p, block(q, L)]) for p in range(PG)]
    give_project.start()
    give_small.start()
    load_mix.wait()
    gather_send(MIXING, 1)
    for p in range(PG):
        load_tok[p].wait()
        tokens_in[p].start()
    give_up.start()
    load_down.wait()
    gather_send(DOWN_A, 1)
    r.wq[block(dp * G + s, SR), :] = r.sp[s]
    r.wu[block(dp * G + s, SR), :] = r.su[s]
    r.sm[dp, s] = r.ss[...]
    mix_in = spread(3 + PG, lambda q: r.wm.at[:, q])
    fetch(MIXING)
    give_project.finish()
    gather_send(PROJECT, 1)
    give_small.finish()
    gather_send(SMALL, 1)
    r.vs[...] = jnp.zeros_like(r.vs)
    for t in range(1, H):
        fetch(MIXING)
        fetch(PROJECT)
        fetch(SMALL)
        if t <= PG:
            tokens_in[t - 1].forward()
    mix_in.start()
    give_up.finish()
    gather_send(UP, 1)
    fetch(DOWN_A)
    fetch(PROJECT)
    fetch(SMALL)
    gather_send(DOWN_B, 1)

    for row in range(UP_BIAS):
        piece = r.sm[:, 0, row, :]
        for q in range(1, G):
            piece = piece + pltpu.roll(r.sm[:, q, row, :], q * SR, 1)
        for j in range(D):
            r.pv[row:row + 1, j * CR:(j + 1) * CR] = piece[j:j + 1]
    for j in range(D):
        r.ubv[0:1, j * FR:(j + 1) * FR] = r.sm[j, s, UP_BIAS:UP_BIAS + 1, :]
    r.pbv[...] = jnp.zeros_like(r.pbv)
    own_heads = pl.ds(pl.multiple_of(s * HC, HC), HC)
    r.pbv[0:1, 0:HC] = r.pv[QUERY_BIAS:QUERY_BIAS + 1, own_heads]
    r.pbv[0:1, 2 * HC:3 * HC] = r.pv[VALUE_BIAS:VALUE_BIAS + 1, own_heads]

    def param(row):
        return r.pv[row:row + 1, :]

    tq = tile_of(QC)

    def project_page(p):
        def body(n):
            cols = lanes(n, tq)
            r.qkv[p, :, cols] = (mm(r.xg[p], r.wq[:, cols]) + r.pbv[0:1, cols]).astype(BF16)

        loop(QC // tq, body)


    pairs = heads // 2
    QB = 256 if W % 256 == 0 else W
    QF = W
    scale = HEAD_DIM ** -0.5

    def pair_of(p, hp):
        return [r.qkv[p, :, pl.ds(pl.multiple_of(b * HC + hp * LANES, LANES), LANES)] for b in range(3)]

    def only(half, rows):
        lane = lax.broadcasted_iota(jnp.int32, rows.shape, 1)
        mine = lane >= HEAD_DIM if half else lane < HEAD_DIM
        return jnp.where(mine, rows, jnp.zeros_like(rows))

    def attend_page(p):
        length = r.lens[p]

        def body(hp):
            query, keys, values = pair_of(p, hp)
            values_t = values.T
            halves = []
            for half in range(2):
                keys_h = only(half, keys)
                blocks = []
                for qb in range(W // QF):
                    scores = mm_t(keys_h, query[qb * QF:(qb + 1) * QF])
                    at_key = lax.broadcasted_iota(jnp.int32, scores.shape, 0)
                    scores = jnp.where(at_key < length, scores, -1e30)
                    top = jnp.max(scores, axis=0, keepdims=True)
                    powers = jnp.exp((scores - top) * scale)
                    probs = powers * (1.0 / jnp.sum(powers, axis=0, keepdims=True))
                    r.probs[(p * pairs + hp) * 2 + half, :, qb * QF:(qb + 1) * QF] = probs
                    blocks.append(mm(values_t[half * HEAD_DIM:(half + 1) * HEAD_DIM], probs.astype(BF16)))
                halves.append(jnp.concatenate(blocks, axis=1))
            both = jnp.concatenate(halves, axis=0).T
            r.ctx[p, :, lanes(hp, LANES)] = both.astype(BF16)

        loop(pairs, body)

    context_out = [
        exchange(4 + PG + p, lambda q, p=p: r.ctx.at[p, block(q, L)],
                 lambda q, p=p: r.cr.at[p, :, block(q, HC)])
        for p in range(PG)
    ]
    for p in range(PG):
        tokens_in[p].finish()
        project_page(p)
        if p == 0:
            fetch(UP)
        attend_page(p)
        context_out[p].start()
        r.cr[p, :, own_heads] = r.ctx[p, block(s, L), :]
        if p == 0:
            mix_in.forward()
        fetch(DOWN_A)
    fetch(UP)
    fetch(DOWN_B)
    mix_in.finish()

    own_rows = pl.ds(pl.multiple_of(s * L, L), L)
    tc = tile_of(C)

    def mix_page(p):
        def body(n):
            cols = lanes(n, tc)
            r.tg[p, :, cols] = mm(r.cr[p], r.wm[:, :, :, cols].reshape(C, tc))

        loop(C // tc, body)

    RB = 32

    def by_rows(p, body):
        def step(i):
            body(pl.ds(pl.multiple_of(i * RB, RB), RB), pl.ds(pl.multiple_of(s * L + i * RB, RB), RB))

        loop(L // RB, step)

    def standard(rows):
        center = rows - jnp.mean(rows, axis=-1, keepdims=True)
        inverse = lax.rsqrt(jnp.mean(center * center, axis=-1, keepdims=True) + 1e-05)
        return center * inverse, inverse

    def unstandard(grad, nhat, inverse):
        return inverse * (
            grad - jnp.mean(grad, axis=-1, keepdims=True) - nhat * jnp.mean(grad * nhat, axis=-1, keepdims=True)
        )

    def add_row(row, rows):
        r.vs[row:row + 1, :] += jnp.sum(rows, axis=0, keepdims=True)

    normed_in = [spread(4 + 2 * PG + p, lambda q, p=p: r.nlg.at[p, block(q, L)]) for p in range(PG)]

    def first_norm(p):
        def body(rows, group_rows):
            resid = r.xg[p, group_rows, :].astype(F32) + r.tg[p, rows, :] + param(MIX_BIAS)
            nhat, inverse = standard(resid)
            normed = nhat * param(GAIN1) + param(SHIFT1)
            r.nh1[p, rows, :] = nhat
            r.inv1[p, rows, :] = jnp.broadcast_to(inverse, (RB, LANES))
            r.tg[p, rows, :] = normed
            r.nlg[p, group_rows, :] = normed.astype(BF16)

        by_rows(p, body)

    for p in range(PG):
        context_out[p].finish()
        mix_page(p)
        first_norm(p)
        normed_in[p].start()
        if p == 0:
            fetch(UP)
    fetch(DOWN_B)

    tf = tile_of(FO)
    tu = tile_of(FO, 256)

    def up_page(p):
        def body(n):
            cols = lanes(n, tu)
            hidden = mm(r.nlg[p], r.wu[:, cols]) + r.ubv[0:1, cols]
            cdf = 0.5 * (1.0 + lax.erf(hidden * 0.7071067811865476))
            r.act[p, :, cols] = (hidden * cdf).astype(BF16)
            slope = cdf + hidden * (jnp.exp(hidden * hidden * -0.5) * 0.3989422804014327)
            r.gp[p, :, cols] = slope

        loop(FO // tu, body)

    normed_in[0].forward()
    fetch(DOWN_A, H)
    fetch(UP, H)
    for p in range(PG):
        normed_in[p].finish()
        up_page(p)
        if p + 1 < PG:
            normed_in[p + 1].forward()
        fetch(DOWN_B)

    def fold(slot, part, r1, s2, r2):
        def near(k):
            return remote(part(2 * k + 1 - cc), r1.at[k], r.fs_.at[slot, k], r.fr_.at[slot, k], sibling)

        def far():
            return remote(s2, r2, r.fs_.at[slot, 2], r.fr_.at[slot, 2], across)

        def start():
            for k in range(2):
                near(k).start()

        def drain():
            for k in range(2):
                near(k).wait_send()
            far().wait_send()

        def middle():
            for k in range(2):
                near(k).wait_recv()
            count = s2.shape[0]

            def body(i):
                rows = pl.ds(pl.multiple_of(i * RB, RB), RB)
                s2[rows, :] = (part(peer[2])[rows, :] + r1[1 - xx, rows, :]).astype(BF16)

            loop(count // RB, body)
            far().start()

        def finish():
            far().wait_recv()

        def own(rows):
            return part(s)[rows, :] + r1[xx, rows, :] + r2[rows, :].astype(F32)

        return SimpleNamespace(start=start, middle=middle, finish=finish, own=own, drain=drain)

    def page_fold(slot, p, cols=slice(None)):
        return fold(slot, lambda q: r.part.at[p * G + q, :, cols], r.r1.at[p, :, :, cols], r.s2.at[p, :, cols], r.r2.at[p, :, cols])

    def into_part(p, cols, value):
        r.part[p * G:(p + 1) * G, :, cols] = value.reshape(G, L, value.shape[-1])

    half_columns = C // 2
    down_fold = [[page_fold(2 * p + a, p, pl.ds(a * half_columns, half_columns)) for a in range(2)] for p in range(PG)]

    def down_page(p, a):
        def body(n):
            cols = pl.ds(pl.multiple_of(a * half_columns + n * tc, tc), tc)
            into_part(p, cols, mm(r.act[p], r.wd[:, cols]))

        loop(half_columns // tc, body)

    for a in range(2):
        fetch(DOWN_A + a, H)
        for p in range(PG):
            down_page(p, a)
            down_fold[p][a].start()
        for p in range(PG):
            down_fold[p][a].middle()

    def down_own(p, rows):
        return r.part[p * G + s, rows, :] + r.r1[p, xx, rows, :] + r.r2[p, rows, :].astype(F32)

    last_in = [spread(4 + 3 * PG + p, lambda q, p=p: r.lrg.at[p, block(q, L)]) for p in range(PG)]

    def last_norm(p):
        def body(rows, group_rows):
            resid = r.tg[p, rows, :] + down_own(p, rows) + param(DOWN_BIAS)
            nhat, inverse = standard(resid)
            r.out[p, rows, :] = nhat * param(GAIN2) + param(SHIFT2)
            cot = r.cot[p, rows, :].astype(F32)
            add_row(GAIN2, cot * nhat)
            add_row(SHIFT2, cot)
            grad = unstandard(cot * param(GAIN2), nhat, inverse)
            add_row(DOWN_BIAS, grad)
            r.tg[p, rows, :] = grad
            r.lrg[p, group_rows, :] = grad.astype(BF16)

        by_rows(p, body)

    for p in range(PG):
        for a in range(2):
            down_fold[p][a].finish()
        last_norm(p)
        last_in[p].start()

    def weight_chunks(lhs, rhs, owners, columns, width):
        count = len(owners)
        for i, j in enumerate(owners):
            for p in range(PG):
                r.tt[i * width:(i + 1) * width, p * W:(p + 1) * W] = lhs[p, :, block(j, width)].T
        tn = tile_of(columns)

        def value(n):
            block = rhs[:, :, lanes(n, tn)].reshape(PG * W, tn)
            full = mm(r.tt[0:count * width, :], block)
            return [full[i * width:(i + 1) * width] for i in range(count)]

        return value, columns // tn, tn

    def grad_chunks(g, owners):
        if g == PROJECT:
            return weight_chunks(r.xg, r.qkv, owners, QC, CR)
        if g == UP:
            return weight_chunks(r.nlg, r.hid, owners, FO, CR)
        if g == DOWN:
            return weight_chunks(r.act, r.lrg, owners, C, FR)
        if g == MIXING:
            return (lambda n: [mix_part(s)[block(j, SR), lanes(n, tc)] for j in owners]), C // tc, tc
        return (lambda n: [r.vc[j] for j in owners]), 1, CR

    bufs = {PROJECT: (r.bp, r.tp), MIXING: (r.bm, r.tm), UP: (r.bu, r.tu), DOWN: (r.bd, r.td), SMALL: (r.bs, r.ts)}

    def ring_copy(g, d, t):
        buf, first = bufs[g]
        count = first.shape[0]
        if t == 1:
            src, dst = first.at[half_rows(count, d)], buf.at[d, 0, half_rows(count, d)]
        else:
            src, dst = buf.at[d, t - 2], buf.at[d, t - 1]
        return remote(src, dst, r.rs.at[g, d, t - 1], r.rr.at[g, d, t - 1], ways[d])

    def ring_first(g):
        buf, first = bufs[g]
        value, count, tn = grad_chunks(g, [shifted(H)])

        def body(n):
            first[:, lanes(n, tn)] = value(n)[0].astype(first.dtype)

        loop(count, body)
        for d in range(2):
            ring_copy(g, d, 1).start()

    def ring_next(g, t):
        buf, first = bufs[g]
        size = first.shape[0]
        hop = H + 1 - t
        for d in range(2):
            ring_copy(g, d, t - 1).wait_recv()
        value, count, tn = grad_chunks(g, [shifted(hop), shifted(-hop)])

        def body(n):
            cols = lanes(n, tn)
            for d, val in enumerate(value(n)):
                if t == 2:
                    near, off = half_rows(size, d), half_rows(size, 1 - d)
                    lo, hi = d * (size // 2), (1 - d) * (size // 2)
                    buf[d, 0, near, cols] = (val[lo:lo + size // 2] + buf[d, 0, near, cols].astype(F32)).astype(buf.dtype)
                    buf[d, 0, off, cols] = val[hi:hi + size // 2].astype(buf.dtype)
                else:
                    buf[d, t - 2, :, cols] = (val + buf[d, t - 2, :, cols].astype(F32)).astype(buf.dtype)

        loop(count, body)
        for d in range(2):
            ring_copy(g, d, t).start()

    def ring_last(g, put):
        advance(g, H)
        buf, first = bufs[g]
        for d in range(2):
            ring_copy(g, d, H).wait_recv()
        value, count, tn = grad_chunks(g, [dp])

        def body(n):
            cols = lanes(n, tn)
            put(cols, value(n)[0] + buf[0, H - 1, :, cols].astype(F32) + buf[1, H - 1, :, cols].astype(F32))

        loop(count, body)
        for t in range(1, H + 1):
            for d in range(2):
                ring_copy(g, d, t).wait_send()

    reached = dict.fromkeys(range(6), 0)

    def advance(g, to=None):
        to = min(H, reached[g] + 1 if to is None else to)
        while reached[g] < to:
            reached[g] += 1
            ring_first(g) if reached[g] == 1 else ring_next(g, reached[g])

    def hidden_page(p):
        def body(n):
            cols = lanes(n, tf)
            grad = mm_t(r.lrg[p], r.wd[cols, :]) * r.gp[p, :, cols]
            r.vu[0:1, cols] += jnp.sum(grad, axis=0, keepdims=True)
            r.hid[p, :, cols] = grad.astype(BF16)

        loop(FO // tf, body)

    r.vu[...] = jnp.zeros_like(r.vu)
    normed_fold = [page_fold(2 * PG + p, p) for p in range(PG)]

    def normed_page(p):
        def body(n):
            cols = lanes(n, tc)
            into_part(p, cols, mm_t(r.hid[p], r.wu[cols, :]))

        loop(C // tc, body)

    for p in range(PG):
        last_in[p].forward()
        last_in[p].finish()
        if p == PG - 1:
            advance(DOWN)
        hidden_page(p)
        for a in range(2):
            down_fold[p][a].drain()
        normed_page(p)
        normed_fold[p].start()
        if p == PG - 1:
            advance(UP)
        normed_fold[p].middle()
    advance(DOWN)

    grads_out = [
        exchange(4 + 4 * PG + p, lambda q, p=p: r.cg.at[p, :, block(q, HC)],
                 lambda q, p=p: r.dc.at[p, block(q, L)])
        for p in range(PG)
    ]

    def first_back(p):
        def body(rows, group_rows):
            grad = r.tg[p, rows, :] + normed_fold[p].own(rows)
            nhat = r.nh1[p, rows, :]
            add_row(GAIN1, grad * nhat)
            add_row(SHIFT1, grad)
            grad = unstandard(grad * param(GAIN1), nhat, r.inv1[p, rows, 0:1])
            add_row(MIX_BIAS, grad)
            r.tg[p, rows, :] = grad
            r.frl[p, rows, :] = grad.astype(BF16)

        by_rows(p, body)

    def context_back(p):
        def body(n):
            cols = lanes(n, tc)
            r.cg[p, :, cols] = mm_t(r.frl[p], r.wm[block(n, tc // CR)].reshape(tc, C)).astype(BF16)

        loop(C // tc, body)

    for p in range(PG):
        normed_fold[p].finish()
        first_back(p)
        context_back(p)
        grads_out[p].start()
        r.dc[p, own_rows, :] = r.cg[p, :, own_heads]
        advance(DOWN if p else UP)

    def mix_part(q):
        return r.gp.at[lax.div(q, W // HC), block(lax.rem(q, W // HC), HC)]

    def mix_grad():
        for i in range(C // 256):
            for p in range(PG):
                r.tm_[:, p * L:(p + 1) * L] = r.cr[p, :, i * 256:(i + 1) * 256].T

            def body(n, i=i):
                cols = lanes(n, tc)
                full = mm(r.tm_[...], r.frl[:, :, cols].reshape(PG * L, tc))
                for k in range(256 // SR):
                    j, q = divmod(i * (256 // SR) + k, G)
                    r.gp[q * HC // W, q * HC % W + j * SR:q * HC % W + (j + 1) * SR, cols] = full[k * SR:(k + 1) * SR]

            loop(C // tc, body)

    mix_fold = fold(4 * PG, mix_part, r.m1, r.ms2, r.mr2)

    def attend_back_page(p):
        def body(hp):
            query, keys, values = pair_of(p, hp)
            d_ctx = r.dc[p, :, lanes(hp, LANES)]
            keys_t = keys.T
            for half in range(2):
                values_h = only(half, values)
                for qb in range(W // QB):
                    span = slice(qb * QB, (qb + 1) * QB)
                    d_probs = mm_t(values_h, d_ctx[span])
                    probs = r.probs[(p * pairs + hp) * 2 + half, :, span]
                    inner = jnp.sum(probs * d_probs, axis=0, keepdims=True)
                    at = slice(half * W + qb * QB, half * W + (qb + 1) * QB)
                    r.wd[0:W, at] = (probs * (d_probs - inner)).astype(BF16)
                    r.wd[W:2 * W, at] = probs.astype(BF16)
            d_keys = mm(r.wd[0:W, :], jnp.concatenate([only(0, query), only(1, query)], axis=0))
            d_values = mm(r.wd[W:2 * W, :], jnp.concatenate([only(0, d_ctx), only(1, d_ctx)], axis=0))
            d_query = [
                mm(keys_t[half * HEAD_DIM:(half + 1) * HEAD_DIM], r.wd[0:W, half * W:(half + 1) * W]) for half in range(2)
            ]
            d_query = jnp.concatenate(d_query, axis=0).T * scale
            for b, val in enumerate((d_query, d_keys * scale, d_values)):
                cols = pl.ds(pl.multiple_of(b * HC + hp * LANES, LANES), LANES)
                low = val.astype(BF16)
                r.qkv[p, :, cols] = low
                r.vp[0:1, cols] += jnp.sum(low.astype(F32), axis=0, keepdims=True)

        for hp in range(pairs):
            body(hp)
            ring_between(p, hp)

    r.vp[...] = jnp.zeros_like(r.vp)
    tokens_fold = [page_fold(3 * PG + p, p) for p in range(PG)]

    def tokens_page(p):
        def body(n):
            cols = lanes(n, tc)
            into_part(p, cols, mm_t(r.qkv[p], r.wq[cols, :]))

        loop(C // tc, body)

    def own_mix(i):
        rows = pl.ds(pl.multiple_of(i * RB, RB), RB)
        mix_part(s)[rows, :] = mix_fold.own(rows)

    def ring_between(p, hp):
        step = p * pairs + hp
        if step == 1:
            mix_grad()
            mix_fold.start()
            advance(UP)
        if step == 2:
            mix_fold.middle()
            advance(DOWN)

    for g in (DOWN_A, DOWN_B):
        gather_drain(g)
    for p in range(PG):
        grads_out[p].finish()
        attend_back_page(p)
    advance(PROJECT)
    advance(UP)

    r.vs[QUERY_BIAS:QUERY_BIAS + 1, own_heads] = r.vp[0:1, 0:HC]
    r.vs[VALUE_BIAS:VALUE_BIAS + 1, own_heads] = r.vp[0:1, 2 * HC:3 * HC]
    for j in range(D):
        r.vc[j] = r.vs[:, j * CR:(j + 1) * CR]
        r.vc[j, UP_BIAS:UP_BIAS + 1, :] = r.vu[0:1, j * FR:(j + 1) * FR]
    advance(SMALL)
    for p in range(PG):
        normed_fold[p].drain()
        tokens_page(p)
        tokens_fold[p].start()
        if p == 0:
            mix_fold.finish()
            loop(HC // RB, own_mix)
            advance(MIXING)
            advance(PROJECT)
            advance(SMALL)
        tokens_fold[p].middle()

    up_out = exchange(4 + 5 * PG, lambda q: r.fu.at[block(q, SR)], lambda q: r.fur.at[q])

    advance(UP, H)
    advance(PROJECT)
    advance(SMALL)
    advance(MIXING)
    ring_last(UP, lambda cols, val: r.fu.__setitem__((slice(None), cols), val.astype(BF16)))
    up_out.start()
    r.fur[s] = r.fu[block(s, SR), :]
    advance(PROJECT)
    advance(SMALL)
    advance(MIXING)
    ring_last(DOWN, lambda cols, val: r.gdw.__setitem__((slice(None), cols), val))

    for p in range(PG):
        tokens_fold[p].finish()

        def token_rows(rows, group_rows, p=p):
            r.tg[p, rows, :] = r.tg[p, rows, :] + tokens_fold[p].own(rows)

        by_rows(p, token_rows)
    up_out.finish()
    for q in range(G):
        for j in range(D):
            r.guw[:, (j * G + q) * FR:(j * G + q + 1) * FR] = r.fur[q, :, j * FR:(j + 1) * FR].astype(F32)

    project_out = exchange(5 + 5 * PG, lambda q: r.fp.at[block(q, SR)], lambda q: r.fpr.at[q])
    small_out = exchange(6 + 5 * PG, lambda q: r.fsm, lambda q: r.fsr.at[q])
    ring_last(PROJECT, lambda cols, val: r.fp.__setitem__((slice(None), cols), val.astype(BF16)))
    project_out.start()
    ring_last(SMALL, lambda cols, val: r.fsm.__setitem__((slice(None), cols), val))
    small_out.start()
    ring_last(MIXING, lambda cols, val: r.gmw.__setitem__((slice(None), cols), val))
    r.fpr[s] = r.fp[block(s, SR), :]
    r.fsr[s] = r.fsm[...]
    project_out.finish()
    for q in range(G):
        for b in range(3):
            r.gpw[:, b * C + q * HC:b * C + (q + 1) * HC] = r.fpr[q, :, b * HC:(b + 1) * HC].astype(F32)
    small_out.finish()
    total = r.fsr[0]
    for q in range(1, G):
        total = total + r.fsr[q]
    mine = jnp.zeros((TABLE, SR), F32)
    for q in range(G):
        mine = mine + jnp.where(s == q, 1.0, 0.0) * pltpu.roll(total, (CR - q * SR) % CR, 1)[:, 0:SR]
    r.small[:, 0:SR] = mine
    r.small[UP_BIAS:UP_BIAS + 1, :] = r.fsm[UP_BIAS:UP_BIAS + 1, :]

    for g in (PROJECT, MIXING, UP, SMALL):
        gather_drain(g)
    for one in tokens_fold + [mix_fold]:
        one.drain()
    for done in exchanges:
        done()

INPUTS = ["tok", "cot", "lens", "pw", "pb", "mw", "mb", "fg", "fs", "uw", "ub", "dw", "db", "lg", "ls"]
BIG = ["out", "tg", "gpw", "gmw", "guw", "gdw"]
OUTPUTS = ["out", "tg", "gpw", "gpb", "gmw", "gmb", "gfg", "gfs", "guw", "gub", "gdw", "gdb", "glg", "gls"]
ROWS = dict(
    gpb=(QUERY_BIAS, 2), gmb=(MIX_BIAS, 1), gfg=(GAIN1, 1), gfs=(SHIFT1, 1), gub=(UP_BIAS, 1), gdb=(DOWN_BIAS, 1),
    glg=(GAIN2, 1), gls=(SHIFT2, 1),
)


def scratch_of(cfg):
    D, G, PG, L, C, F = cfg
    H = D // 2
    W, HC, FO, CR, SR = L * G, C // G, F // G, C // D, C // (D * G)
    FR, QC, heads = FO // D, 3 * HC, HEADS // G
    low = dict(
        wq=(C, QC), wm=(D, G, SR, C), wu=(C, FO), wd=(FO, C), sp=(G, SR, QC), su=(G, SR, FO), xg=(PG, W, C),
        qkv=(PG, W, QC), ctx=(PG, W, HC), cr=(PG, L, C), nlg=(PG, W, C), act=(PG, W, FO), hid=(PG, W, FO),
        s2=(PG, L, C), r2=(PG, L, C), lrg=(PG, W, C), frl=(PG, L, C), cg=(PG, L, C), dc=(PG, W, HC),
        ms2=(HC, C), mr2=(HC, C), tt=(2 * max(CR, FR), PG * W), tm_=(256, PG * L),
        bp=(2, H, CR, QC), tp=(CR, QC), bm=(2, H, SR, C), tm=(SR, C), bu=(2, H, CR, FO), tu=(CR, FO),
        bd=(2, H, FR, C), td=(FR, C),
        fu=(CR, FO), fur=(G, SR, FO), fp=(CR, QC), fpr=(G, SR, QC),
    )
    wide = dict(
        ss=(TABLE, LANES), sm=(D, G, TABLE, LANES), probs=(PG * heads, W, W), nh1=(PG, L, C),
        inv1=(PG, L, LANES), gp=(PG, W, FO), part=(PG * G, L, C), r1=(PG, 2, L, C), m1=(2, HC, C),
        bs=(2, H, TABLE, CR), ts=(TABLE, CR), vs=(TABLE, C), vp=(8, QC), vu=(8, FO), vc=(D, TABLE, CR),
        pv=(TABLE, C), ubv=(8, FO), pbv=(8, QC),
        fsm=(TABLE, CR), fsr=(G, TABLE, CR),
    )
    sems = dict(
        local_sem=(2 + PG,), gs=(6, 2, H), gr=(6, 2, H), rs=(6, 2, H), rr=(6, 2, H),
        xs=(7 + 5 * PG, 3), xr=(7 + 5 * PG, 3), fs_=(4 * PG + 1, 3), fr_=(4 * PG + 1, 3),
    )
    scratch = {k: pltpu.VMEM(v, BF16) for k, v in low.items()}
    scratch |= {k: pltpu.VMEM(v, F32) for k, v in wide.items()}
    scratch |= {k: pltpu.SemaphoreType.DMA(v) for k, v in sems.items()}
    return scratch


def fits(cfg):
    D, G, PG, L, C, F = cfg
    return (
        G == 4 and D % 2 == 0 and D >= 4 and L % 128 == 0 and (C // G) % 256 == 0 and C // D == 128 and F // (D * G) == 128
        and (HEADS // G) % 2 == 0 and PG == 2 and PG * L * G == C and F // G == C and (L * G) % (C // G) == 0
    )


def fused(cfg, *args):
    D, G, PG, L, C, F = cfg
    SR = C // (D * G)
    scratch = scratch_of(cfg)
    global NAMES
    NAMES = INPUTS + BIG + ["small"] + list(scratch)
    vmem, anywhere = pl.BlockSpec(memory_space=pltpu.VMEM), pl.BlockSpec(memory_space=pl.ANY)
    where = {"tok": anywhere, "mw": anywhere, "dw": anywhere, "lens": pl.BlockSpec(memory_space=pltpu.SMEM)}
    flat = [a.reshape(1, -1) if name not in ("lens",) and a.ndim == 1 else a for name, a in zip(INPUTS, args)]
    shapes = dict(
        out=(PG, L, C), tg=(PG, L, C), gpw=(SR, 3 * C), gpb=(2, SR), gmw=(SR, C), gmb=(1, SR), gfg=(1, SR), gfs=(1, SR),
        guw=(SR, F), gub=(1, F // (D * G)), gdw=(F // (D * G), C), gdb=(1, SR), glg=(1, SR), gls=(1, SR),
    )
    given = pl.pallas_call(
        functools.partial(layer_kernel, cfg),
        out_shape=[jax.ShapeDtypeStruct(shapes[k], F32) for k in BIG] + [jax.ShapeDtypeStruct((TABLE, LANES), F32)],
        in_specs=[where.get(k, vmem) for k in INPUTS],
        out_specs=[vmem] * (len(BIG) + 1),
        scratch_shapes=list(scratch.values()),
        compiler_params=pltpu.CompilerParams(collective_id=0, has_side_effects=True, vmem_limit_bytes=VMEM_LIMIT),
        name="encoder_layer",
    )(*flat)
    count = len(BIG)
    results = pl.pallas_call(
        write_out,
        out_shape=[jax.ShapeDtypeStruct(shapes[k], F32) for k in OUTPUTS],
        in_specs=[anywhere] * count + [vmem],
        out_specs=[anywhere if k in BIG else vmem for k in OUTPUTS],
        scratch_shapes=[pltpu.VMEM(shapes[k], F32) for k in BIG] + [pltpu.SemaphoreType.DMA((2, count))],
        compiler_params=pltpu.CompilerParams(vmem_limit_bytes=VMEM_LIMIT),
        name="write_out",
    )(*given)
    return tuple(v.reshape(-1) if v.shape[0] == 1 else v for v in results)


def write_out(*refs):
    count = len(BIG)
    given, small = refs[:count], refs[count]
    result = dict(zip(OUTPUTS, refs[count + 1:]))
    held, sems = refs[count + 1 + len(OUTPUTS):-1], refs[-1]
    fetch = [pltpu.make_async_copy(given[i], held[i], sems.at[0, i]) for i in range(count)]
    store = [pltpu.make_async_copy(held[i], result[k], sems.at[1, i]) for i, k in enumerate(BIG)]
    for copy in fetch:
        copy.start()
    for k, (row, rows) in ROWS.items():
        result[k][...] = small[row:row + rows, 0:result[k].shape[1]]
    for i in range(count):
        fetch[i].wait()
        store[i].start()
    for copy in store:
        copy.wait()


VMEM_LIMIT = 63 << 20


def per_device(*args):
    tokens, up_weight = args[0], args[9]
    D, G = lax.axis_size("dp"), lax.axis_size("seq")
    cfg = (D, G, tokens.shape[0], tokens.shape[1], tokens.shape[2], up_weight.shape[1])
    return fused(cfg, *args) if fits(cfg) else plain(*args)


MICRO = 2


def matmul(left, right):
    return jnp.dot(left, right, preferred_element_type=jnp.float32)


def against(left, right):
    return jnp.einsum("re,fe->rf", left, right, preferred_element_type=jnp.float32)


def contract_rows(left, right):
    return jnp.einsum("rd,re->de", left, right, preferred_element_type=jnp.float32)


def layer_norm(rows, gain, shift):
    center = rows - jnp.mean(rows, axis=-1, keepdims=True)
    spread = jnp.mean(center * center, axis=-1, keepdims=True)
    return center * lax.rsqrt(spread + 1e-05) * gain + shift


def gelu_exact(value):
    return 0.5 * value * (1.0 + lax.erf(value * 0.7071067811865476))


def masked_scores(query, keys, length):
    scores = jnp.einsum(
        "qhd,khd->hqk", query, keys, preferred_element_type=jnp.float32
    ) * query.shape[-1] ** (-0.5)
    valid = lax.iota(jnp.int32, keys.shape[0]) < length
    return jnp.where(valid[None, None, :], scores, -1e30)


def attend(packed, length):
    query, keys, values = (packed[:, 0], packed[:, 1], packed[:, 2])
    scores = masked_scores(query, keys, length)
    top = jnp.max(scores, axis=-1, keepdims=True)
    powers = jnp.exp(scores - top)
    total = jnp.sum(powers, axis=-1, keepdims=True)
    probs = (powers / total).astype(jnp.bfloat16)
    context = jnp.einsum("hqk,khd->qhd", probs, values, preferred_element_type=jnp.float32)
    return (
        context.astype(jnp.bfloat16).reshape(packed.shape[0], -1),
        (top + jnp.log(total))[..., 0],
    )


def attend_back(packed, context_grad, logsum, length):
    query, keys, values = (packed[:, 0], packed[:, 1], packed[:, 2])
    scale = query.shape[-1] ** (-0.5)
    scores = masked_scores(query, keys, length)
    probs = jnp.exp(scores - logsum[..., None])
    probs_grad = jnp.einsum(
        "qhd,khd->hqk", context_grad, values, preferred_element_type=jnp.float32
    )
    inner = jnp.sum(probs * probs_grad, axis=-1, keepdims=True)
    scores_grad = (probs * (probs_grad - inner)).astype(jnp.bfloat16)
    query_grad = (
        jnp.einsum("hqk,khd->qhd", scores_grad, keys, preferred_element_type=jnp.float32) * scale
    )
    keys_grad = (
        jnp.einsum("hqk,qhd->khd", scores_grad, query, preferred_element_type=jnp.float32) * scale
    )
    values_grad = jnp.einsum(
        "hqk,qhd->khd", probs.astype(jnp.bfloat16), context_grad, preferred_element_type=jnp.float32
    )
    return jnp.stack([query_grad, keys_grad, values_grad], axis=1).astype(jnp.bfloat16)


def plain(
    tokens,
    cotangent,
    lengths,
    project_weight,
    project_bias,
    mixing_weight,
    mixing_bias,
    first_gain,
    first_shift,
    up_weight,
    up_bias,
    down_weight,
    down_bias,
    last_gain,
    last_shift,
):
    groups = lax.axis_size("seq")
    (
        project_full,
        bias_pair,
        mixing_full,
        mixing_shift,
        first_scale,
        first_offset,
        up_full,
        up_shift,
        down_full,
        down_shift,
        last_scale,
        last_offset,
    ) = (
        lax.all_gather(project_weight, ("dp", "seq"), axis=0, tiled=True),
        lax.all_gather(project_bias, ("dp", "seq"), axis=1, tiled=True),
        lax.all_gather(mixing_weight, ("dp", "seq"), axis=0, tiled=True),
        lax.all_gather(mixing_bias, ("dp", "seq"), axis=0, tiled=True),
        lax.all_gather(first_gain, ("dp", "seq"), axis=0, tiled=True),
        lax.all_gather(first_shift, ("dp", "seq"), axis=0, tiled=True),
        lax.all_gather(up_weight, ("dp", "seq"), axis=0, tiled=True),
        lax.all_gather(up_bias, ("dp", "seq"), axis=0, tiled=True),
        lax.all_gather(down_weight, ("dp", "seq"), axis=0, tiled=True),
        lax.all_gather(down_bias, ("dp", "seq"), axis=0, tiled=True),
        lax.all_gather(last_gain, ("dp", "seq"), axis=0, tiled=True),
        lax.all_gather(last_shift, ("dp", "seq"), axis=0, tiled=True),
    )
    bias_pair = bias_pair.astype(jnp.float32)
    mixing_shift = mixing_shift.astype(jnp.float32)
    first_scale = first_scale.astype(jnp.float32)
    first_offset = first_offset.astype(jnp.float32)
    up_shift = up_shift.astype(jnp.float32)
    down_shift = down_shift.astype(jnp.float32)
    last_scale = last_scale.astype(jnp.float32)
    last_offset = last_offset.astype(jnp.float32)
    project_shift = jnp.concatenate([bias_pair[0], jnp.zeros_like(bias_pair[0]), bias_pair[1]])
    pages = tokens.shape[0] // MICRO
    local = tokens.shape[1]
    model = tokens.shape[2]
    width = local * groups
    slice_width = model // groups
    owned = HEADS // groups
    rows = pages * local
    outputs = []
    input_grads = []
    for micro in range(MICRO):
        begin = micro * pages
        flat = tokens[begin : begin + pages].reshape(rows, model)
        spans = lengths[begin : begin + pages]
        packed = (matmul(flat, project_full) + project_shift).astype(jnp.bfloat16)
        per_head = lax.all_to_all(
            packed.reshape(pages, local, 3, groups, slice_width),
            "seq",
            split_axis=3,
            concat_axis=1,
            tiled=True,
        )
        per_head = per_head.reshape(pages, width, 3, owned, HEAD_DIM)
        context, logsum = lax.map(lambda item: attend(item[0], item[1]), (per_head, spans))
        mixed = lax.all_to_all(context, "seq", split_axis=1, concat_axis=2, tiled=True).reshape(
            rows, model
        )
        residual = flat.astype(jnp.float32) + matmul(mixed, mixing_full) + mixing_shift
        normed, first_pull = jax.vjp(layer_norm, residual, first_scale, first_offset)
        normed_low = normed.astype(jnp.bfloat16)
        hidden_in = matmul(normed_low, up_full) + up_shift
        hidden_value, gelu_pull = jax.vjp(gelu_exact, hidden_in)
        activation = hidden_value.astype(jnp.bfloat16)
        last_resid = normed + matmul(activation, down_full) + down_shift
        output, last_pull = jax.vjp(layer_norm, last_resid, last_scale, last_offset)
        outputs.append(output.reshape(pages, local, model))
        seed_grad = cotangent[begin : begin + pages].reshape(rows, model).astype(jnp.float32)
        last_resid_grad, last_gain_grad, last_shift_grad = last_pull(seed_grad)
        down_bias_grad = jnp.sum(last_resid_grad, axis=0)
        last_resid_low = last_resid_grad.astype(jnp.bfloat16)
        down_weight_grad = contract_rows(activation, last_resid_low)
        (hidden_grad,) = gelu_pull(against(last_resid_low, down_full))
        up_bias_grad = jnp.sum(hidden_grad, axis=0)
        hidden_low = hidden_grad.astype(jnp.bfloat16)
        up_weight_grad = contract_rows(normed_low, hidden_low)
        feed_part = (
            up_weight_grad,
            up_bias_grad,
            down_weight_grad,
            down_bias_grad,
            last_gain_grad,
            last_shift_grad,
        )
        if micro == 0:
            feed_total = feed_part
        else:
            feed_total = tuple((a + b for a, b in zip(feed_total, feed_part)))
        normed_grad = last_resid_grad + against(hidden_low, up_full)
        first_resid_grad, first_gain_grad, first_shift_grad = first_pull(normed_grad)
        mixing_bias_grad = jnp.sum(first_resid_grad, axis=0)
        first_resid_low = first_resid_grad.astype(jnp.bfloat16)
        mixing_weight_grad = contract_rows(mixed, first_resid_low)
        context_grad = against(first_resid_low, mixing_full).astype(jnp.bfloat16)
        context_heads = lax.all_to_all(
            context_grad.reshape(pages, local, model),
            "seq",
            split_axis=2,
            concat_axis=1,
            tiled=True,
        )
        context_heads = context_heads.reshape(pages, width, owned, HEAD_DIM)
        packed_grad = lax.map(
            lambda item: attend_back(item[0], item[1], item[2], item[3]),
            (per_head, context_heads, logsum, spans),
        )
        packed_grad = lax.all_to_all(
            packed_grad.reshape(pages, width, 3, 1, slice_width),
            "seq",
            split_axis=1,
            concat_axis=3,
            tiled=True,
        )
        packed_grad = packed_grad.reshape(rows, 3 * model)
        bias_grad = jnp.stack(
            [
                jnp.sum(packed_grad[:, :model], axis=0, dtype=jnp.float32),
                jnp.sum(packed_grad[:, 2 * model :], axis=0, dtype=jnp.float32),
            ]
        )
        project_weight_grad = contract_rows(flat, packed_grad)
        input_grads.append(
            (first_resid_grad + against(packed_grad, project_full)).reshape(pages, local, model)
        )
        attend_part = (
            project_weight_grad,
            bias_grad,
            mixing_weight_grad,
            mixing_bias_grad,
            first_gain_grad,
            first_shift_grad,
        )
        if micro == 0:
            attend_total = attend_part
        else:
            attend_total = tuple((a + b for a, b in zip(attend_total, attend_part)))
    shards = (
        lax.psum_scatter(attend_total[0], ("dp", "seq"), scatter_dimension=0, tiled=True),
        lax.psum_scatter(attend_total[1], ("dp", "seq"), scatter_dimension=1, tiled=True),
        lax.psum_scatter(attend_total[2], ("dp", "seq"), scatter_dimension=0, tiled=True),
        lax.psum_scatter(attend_total[3], ("dp", "seq"), scatter_dimension=0, tiled=True),
        lax.psum_scatter(attend_total[4], ("dp", "seq"), scatter_dimension=0, tiled=True),
        lax.psum_scatter(attend_total[5], ("dp", "seq"), scatter_dimension=0, tiled=True),
        lax.psum_scatter(feed_total[0], ("dp", "seq"), scatter_dimension=0, tiled=True),
        lax.psum_scatter(feed_total[1], ("dp", "seq"), scatter_dimension=0, tiled=True),
        lax.psum_scatter(feed_total[2], ("dp", "seq"), scatter_dimension=0, tiled=True),
        lax.psum_scatter(feed_total[3], ("dp", "seq"), scatter_dimension=0, tiled=True),
        lax.psum_scatter(feed_total[4], ("dp", "seq"), scatter_dimension=0, tiled=True),
        lax.psum_scatter(feed_total[5], ("dp", "seq"), scatter_dimension=0, tiled=True),
    )
    layer_output = jnp.concatenate(outputs, axis=0)
    tokens_gradient = jnp.concatenate(input_grads, axis=0)
    return (
        layer_output,
        tokens_gradient,
        shards[0],
        shards[1],
        shards[2],
        shards[3],
        shards[4],
        shards[5],
        shards[6],
        shards[7],
        shards[8],
        shards[9],
        shards[10],
        shards[11],
    )


def solution(mesh):
    placed = (
        P("dp", "seq", None),
        P("dp", "seq", None),
        P("dp"),
        P(("dp", "seq"), None),
        P(None, ("dp", "seq")),
        P(("dp", "seq"), None),
        P(("dp", "seq")),
        P(("dp", "seq")),
        P(("dp", "seq")),
        P(("dp", "seq"), None),
        P(("dp", "seq")),
        P(("dp", "seq"), None),
        P(("dp", "seq")),
        P(("dp", "seq")),
        P(("dp", "seq")),
    )
    return jax.shard_map(
        per_device,
        mesh=mesh,
        in_specs=placed,
        out_specs=(
            P("dp", "seq", None),
            P("dp", "seq", None),
            P(("dp", "seq"), None),
            P(None, ("dp", "seq")),
            P(("dp", "seq"), None),
            P(("dp", "seq")),
            P(("dp", "seq")),
            P(("dp", "seq")),
            P(("dp", "seq"), None),
            P(("dp", "seq")),
            P(("dp", "seq"), None),
            P(("dp", "seq")),
            P(("dp", "seq")),
            P(("dp", "seq")),
        ),
        check_vma=False,
    )
```

```python
import functools
from types import SimpleNamespace

import jax
import jax.numpy as jnp
from jax import lax
from jax.experimental import pallas as pl
from jax.experimental.pallas import tpu as pltpu
from jax.sharding import PartitionSpec as P

HEADS = 16
HEAD_DIM = 64
F32 = jnp.float32
BF16 = jnp.bfloat16
MESH = pl.DeviceIdType.MESH
LANES = 128


def mm(left, right):
    return lax.dot_general(left, right, (((1,), (0,)), ((), ())), preferred_element_type=F32)


def mm_t(left, right):
    return lax.dot_general(left, right, (((1,), (1,)), ((), ())), preferred_element_type=F32)


def loop(count, body):
    def step(i, carry):
        body(i)
        return carry

    lax.fori_loop(0, count, step, 0)


def tile_of(columns, most=512):
    return next(size for size in (512, 384, 256, 128) if size <= most and columns % size == 0)


def lanes(index, size):
    return pl.ds(pl.multiple_of(index * size, size), size)


QUERY_BIAS, VALUE_BIAS, MIX_BIAS, GAIN1, SHIFT1, DOWN_BIAS, GAIN2, SHIFT2, UP_BIAS = range(9)
TABLE = 16
PROJECT, MIXING, UP, DOWN_A, DOWN_B, SMALL = range(6)
DOWN = DOWN_A


def layer_kernel(cfg, *refs):
    D, G, PG, L, C, F = cfg
    H = D // 2
    W = L * G
    HC = C // G
    FO = F // G
    CR = C // D
    SR = C // (D * G)
    FR = FO // D
    QC = 3 * HC
    heads = HEADS // G
    r = SimpleNamespace(**dict(zip(NAMES, refs)))

    dp = lax.axis_index("dp")
    s = lax.axis_index("seq")
    xx = lax.div(s, 2)
    cc = lax.rem(s, 2)
    side = lax.rem(dp, 2)
    pos = (1 - side) * lax.div(dp, 2) + side * (D - 1 - lax.div(dp, 2))

    def at_position(p):
        far = lax.div(p, H)
        return (1 - far) * 2 * p + far * (2 * (D - 1 - p) + 1)

    def shifted(k):
        return at_position(lax.rem(pos + (k + D) % D, D))

    right, left = (shifted(1), s), (shifted(-1), s)
    ways = (right, left)
    peer = {1: s + 1 - 2 * cc, 2: s + 2 - 4 * xx, 3: 3 - s}
    sibling, across = (dp, peer[1]), (dp, peer[2])

    def remote(src, dst, send, recv, device):
        return pltpu.make_async_remote_copy(
            src_ref=src, dst_ref=dst, send_sem=send, recv_sem=recv,
            device_id=device, device_id_type=MESH,
        )

    def block(index, size):
        return pl.ds(pl.multiple_of(index * size, size), size)

    local = []

    def load(src, dst):
        copy = pltpu.make_async_copy(src, dst, r.local_sem.at[len(local)])
        copy.start()
        local.append(copy)
        return copy

    load_mix = load(r.mw, r.wm.at[dp, s])
    load_tok = [load(r.tok.at[p], r.xg.at[p, block(s, L)]) for p in range(PG)]
    load_down = load(r.dw, r.wd.at[block(dp, FR)])

    barrier = pltpu.get_barrier_semaphore()
    partners = [right, left] + [(dp, peer[k]) for k in (1, 2, 3)]
    for device in partners:
        pl.semaphore_signal(barrier, inc=1, device_id=device, device_id_type=MESH)

    for q in range(G):
        for b in range(3):
            r.sp[q, :, b * HC:(b + 1) * HC] = r.pw[:, b * C + q * HC:b * C + (q + 1) * HC]
        for j in range(D):
            r.su[q, :, j * FR:(j + 1) * FR] = r.uw[:, (j * G + q) * FR:(j * G + q + 1) * FR]
    r.ss[...] = jnp.zeros_like(r.ss)
    per_row = LANES // SR
    smalls = {
        QUERY_BIAS: r.pb[0:1], VALUE_BIAS: r.pb[1:2], MIX_BIAS: r.mb[...], GAIN1: r.fg[...], SHIFT1: r.fs[...],
        DOWN_BIAS: r.db[...], GAIN2: r.lg[...], SHIFT2: r.ls[...],
    }
    for k, given in smalls.items():
        r.ss[k // per_row:k // per_row + 1, k % per_row * SR:(k % per_row + 1) * SR] = given.astype(F32)
    up_row = UP_BIAS // per_row
    r.ss[up_row:up_row + 1, :] = r.ub[...].astype(F32)

    pl.semaphore_wait(barrier, len(partners))

    exchanges = []

    def exchange(slot, source, target):
        def copy(k, which):
            return remote(source(peer[k]), target(which), r.xs.at[slot, k - 1], r.xr.at[slot, k - 1], (dp, peer[k]))

        def start():
            exchanges.append(lambda: [copy(k, s).wait_send() for k in (2, 3, 1)])
            for k in (2, 3, 1):
                copy(k, s).start()

        def finish():
            for k in (1, 2, 3):
                copy(k, peer[k]).wait_recv()

        return SimpleNamespace(start=start, finish=finish)

    def spread(slot, block):
        def copy(k):
            which = peer[2] if k == 2 else s
            device = across if k == 1 else sibling
            return remote(block(which), block(which), r.xs.at[slot, k], r.xr.at[slot, k], device)

        def arrived(k, which):
            return remote(block(which), block(which), r.xs.at[slot, k], r.xr.at[slot, k], sibling)

        def start():
            exchanges.append(lambda: [copy(k).wait_send() for k in range(3)])
            copy(1).start()
            copy(0).start()

        def forward():
            arrived(1, peer[2]).wait_recv()
            copy(2).start()

        def finish():
            arrived(0, peer[1]).wait_recv()
            arrived(2, peer[3]).wait_recv()

        return SimpleNamespace(start=start, forward=forward, finish=finish)

    def half_rows(count, half):
        return pl.ds(half * (count // 2), count // 2)

    def rows_of(ref, owner, count, half):
        if half is None:
            return ref.at[block(owner, count)]
        return ref.at[block(owner * 2 + half, count // 2)]

    def side_columns(half):
        return pl.ds(half * (C // 2), C // 2)

    def chunk_view(g, owner, half):
        if g == PROJECT:
            return rows_of(r.wq, owner, CR, half)
        if g == MIXING:
            return r.wm.at[owner, s] if half is None else r.wm.at[owner, s, half_rows(SR, half)]
        if g == UP:
            return rows_of(r.wu, owner, CR, half)
        if g in (DOWN_A, DOWN_B):
            return rows_of(r.wd.at[:, side_columns(g - DOWN_A)], owner, FR, half)
        return r.sm.at[owner] if half is None else r.sm.at[owner, half_rows(G, half)]

    def gather_copy(g, d, t, owner):
        view = chunk_view(g, owner, d if t == H else None)
        return remote(view, view, r.gs.at[g, d, t - 1], r.gr.at[g, d, t - 1], ways[d])

    def sent(d, t):
        return shifted(-(t - 1) if d == 0 else t - 1)

    def gather_send(g, t):
        for d in range(2):
            gather_copy(g, d, t, sent(d, t)).start()

    def gather_step(g, t):
        for d in range(2):
            gather_copy(g, d, t, shifted(-t if d == 0 else t)).wait_recv()
            if t < H:
                gather_copy(g, d, t + 1, sent(d, t + 1)).start()

    fetched = dict.fromkeys(range(6), 0)

    def fetch(g, to=None):
        to = min(H, fetched[g] + 1 if to is None else to)
        while fetched[g] < to:
            fetched[g] += 1
            gather_step(g, fetched[g])

    def gather_drain(g):
        for t in range(1, H + 1):
            for d in range(2):
                gather_copy(g, d, t, sent(d, t)).wait_send()

    give_project = exchange(0, lambda q: r.sp.at[q], lambda q: r.wq.at[block(dp * G + q, SR)])
    give_small = exchange(1, lambda q: r.ss, lambda q: r.sm.at[dp, q])
    give_up = exchange(2, lambda q: r.su.at[q], lambda q: r.wu.at[block(dp * G + q, SR)])
    tokens_in = [spread(3 + p, lambda q, p=p: r.xg.at[p, block(q, L)]) for p in range(PG)]
    give_project.start()
    give_small.start()
    load_mix.wait()
    gather_send(MIXING, 1)
    for p in range(PG):
        load_tok[p].wait()
        tokens_in[p].start()
    give_up.start()
    load_down.wait()
    gather_send(DOWN_A, 1)
    r.wq[block(dp * G + s, SR), :] = r.sp[s]
    r.wu[block(dp * G + s, SR), :] = r.su[s]
    r.sm[dp, s] = r.ss[...]
    mix_in = spread(3 + PG, lambda q: r.wm.at[:, q])
    fetch(MIXING)
    give_project.finish()
    gather_send(PROJECT, 1)
    give_small.finish()
    gather_send(SMALL, 1)
    r.vs[...] = jnp.zeros_like(r.vs)
    for t in range(1, H):
        if t == H - 1:
            give_up.finish()
            gather_send(UP, 1)
        fetch(MIXING)
        fetch(PROJECT)
        fetch(SMALL)
        if t <= PG:
            tokens_in[t - 1].forward()
    mix_in.start()
    fetch(DOWN_A)
    fetch(PROJECT)
    fetch(SMALL)
    gather_send(DOWN_B, 1)

    for row in range(UP_BIAS):
        piece = jnp.zeros((D, LANES), F32)
        lane = lax.broadcasted_iota(jnp.int32, piece.shape, 1)
        for q in range(G):
            turned = pltpu.roll(r.sm[:, q, row // per_row, :], (q - row % per_row) * SR % LANES, 1)
            piece = jnp.where((lane >= q * SR) & (lane < (q + 1) * SR), turned, piece)
        for j in range(D):
            r.pv[row:row + 1, j * CR:(j + 1) * CR] = piece[j:j + 1]
    for j in range(D):
        r.ubv[0:1, j * FR:(j + 1) * FR] = r.sm[j, s, up_row:up_row + 1, :]
    r.pbv[...] = jnp.zeros_like(r.pbv)
    own_heads = pl.ds(pl.multiple_of(s * HC, HC), HC)
    r.pbv[0:1, 0:HC] = r.pv[QUERY_BIAS:QUERY_BIAS + 1, own_heads]
    r.pbv[0:1, 2 * HC:3 * HC] = r.pv[VALUE_BIAS:VALUE_BIAS + 1, own_heads]

    def param(row):
        return r.pv[row:row + 1, :]

    tq = tile_of(QC)

    def project_page(p):
        def body(n):
            cols = lanes(n, tq)
            r.qkv[p, :, cols] = (mm(r.xg[p], r.wq[:, cols]) + r.pbv[0:1, cols]).astype(BF16)

        loop(QC // tq, body)


    pairs = heads // 2
    QB = 256 if W % 256 == 0 else W
    QF = W
    scale = HEAD_DIM ** -0.5

    def pair_of(p, hp):
        return [r.qkv[p, :, pl.ds(pl.multiple_of(b * HC + hp * LANES, LANES), LANES)] for b in range(3)]

    def only(half, rows):
        lane = lax.broadcasted_iota(jnp.int32, rows.shape, 1)
        mine = lane >= HEAD_DIM if half else lane < HEAD_DIM
        return jnp.where(mine, rows, jnp.zeros_like(rows))

    def attend_page(p):
        length = r.lens[p]

        def body(hp):
            query, keys, values = pair_of(p, hp)
            values_t = values.T
            halves = []
            for half in range(2):
                keys_h = only(half, keys)
                blocks = []
                for qb in range(W // QF):
                    scores = mm_t(keys_h, query[qb * QF:(qb + 1) * QF])
                    at_key = lax.broadcasted_iota(jnp.int32, scores.shape, 0)
                    scores = jnp.where(at_key < length, scores, -1e30)
                    top = jnp.max(scores, axis=0, keepdims=True)
                    powers = jnp.exp((scores - top) * scale)
                    probs = powers * (1.0 / jnp.sum(powers, axis=0, keepdims=True))
                    r.probs[(p * pairs + hp) * 2 + half, :, qb * QF:(qb + 1) * QF] = probs
                    blocks.append(mm(values_t[half * HEAD_DIM:(half + 1) * HEAD_DIM], probs.astype(BF16)))
                halves.append(jnp.concatenate(blocks, axis=1))
            both = jnp.concatenate(halves, axis=0).T
            r.ctx[p, :, lanes(hp, LANES)] = both.astype(BF16)

        loop(pairs, body)

    context_out = [
        exchange(4 + PG + p, lambda q, p=p: r.ctx.at[p, block(q, L)],
                 lambda q, p=p: r.cr.at[p, :, block(q, HC)])
        for p in range(PG)
    ]
    for p in range(PG):
        tokens_in[p].finish()
        project_page(p)
        if p == 0:
            fetch(UP)
        attend_page(p)
        context_out[p].start()
        r.cr[p, :, own_heads] = r.ctx[p, block(s, L), :]
        if p == 0:
            mix_in.forward()
        fetch(DOWN_A)
    fetch(UP)
    fetch(DOWN_B)
    mix_in.finish()

    own_rows = pl.ds(pl.multiple_of(s * L, L), L)
    tc = tile_of(C)

    def mix_page(p):
        def body(n):
            cols = lanes(n, tc)
            r.tg[p, :, cols] = mm(r.cr[p], r.wm[:, :, :, cols].reshape(C, tc))

        loop(C // tc, body)

    RB = 32

    def by_rows(p, body):
        def step(i):
            body(pl.ds(pl.multiple_of(i * RB, RB), RB), pl.ds(pl.multiple_of(s * L + i * RB, RB), RB))

        loop(L // RB, step)

    def standard(rows):
        center = rows - jnp.mean(rows, axis=-1, keepdims=True)
        inverse = lax.rsqrt(jnp.mean(center * center, axis=-1, keepdims=True) + 1e-05)
        return center * inverse, inverse

    def unstandard(grad, nhat, inverse):
        return inverse * (
            grad - jnp.mean(grad, axis=-1, keepdims=True) - nhat * jnp.mean(grad * nhat, axis=-1, keepdims=True)
        )

    def add_row(row, rows):
        r.vs[row:row + 1, :] += jnp.sum(rows, axis=0, keepdims=True)

    normed_in = [spread(4 + 2 * PG + p, lambda q, p=p: r.nlg.at[p, block(q, L)]) for p in range(PG)]

    def first_norm(p):
        def body(rows, group_rows):
            resid = r.xg[p, group_rows, :].astype(F32) + r.tg[p, rows, :] + param(MIX_BIAS)
            nhat, inverse = standard(resid)
            normed = nhat * param(GAIN1) + param(SHIFT1)
            r.nh1[p, rows, :] = nhat
            r.inv1[p, rows, :] = jnp.broadcast_to(inverse, (RB, LANES))
            r.tg[p, rows, :] = normed
            r.nlg[p, group_rows, :] = normed.astype(BF16)

        by_rows(p, body)

    for p in range(PG):
        context_out[p].finish()
        mix_page(p)
        first_norm(p)
        normed_in[p].start()
        if p == 0:
            fetch(UP)
    fetch(DOWN_B)

    tf = tile_of(FO)
    tu = tile_of(FO, 256)

    def up_page(p):
        def body(n):
            cols = lanes(n, tu)
            hidden = mm(r.nlg[p], r.wu[:, cols]) + r.ubv[0:1, cols]
            cdf = 0.5 * (1.0 + lax.erf(hidden * 0.7071067811865476))
            r.act[p, :, cols] = (hidden * cdf).astype(BF16)
            slope = cdf + hidden * (jnp.exp(hidden * hidden * -0.5) * 0.3989422804014327)
            r.gp[p, :, cols] = slope

        loop(FO // tu, body)

    normed_in[0].forward()
    fetch(DOWN_A, H)
    fetch(UP, H)
    for p in range(PG):
        normed_in[p].finish()
        up_page(p)
        if p + 1 < PG:
            normed_in[p + 1].forward()
        fetch(DOWN_B)

    def fold(slot, part, r1, s2, r2):
        def near(k):
            return remote(part(2 * k + 1 - cc), r1.at[k], r.fs_.at[slot, k], r.fr_.at[slot, k], sibling)

        def far():
            return remote(s2, r2, r.fs_.at[slot, 2], r.fr_.at[slot, 2], across)

        def start():
            for k in range(2):
                near(k).start()

        def drain():
            for k in range(2):
                near(k).wait_send()
            far().wait_send()

        def middle():
            for k in range(2):
                near(k).wait_recv()
            count = s2.shape[0]

            def body(i):
                rows = pl.ds(pl.multiple_of(i * RB, RB), RB)
                s2[rows, :] = (part(peer[2])[rows, :] + r1[1 - xx, rows, :]).astype(BF16)

            loop(count // RB, body)
            far().start()

        def finish():
            far().wait_recv()

        def own(rows):
            return part(s)[rows, :] + r1[xx, rows, :] + r2[rows, :].astype(F32)

        return SimpleNamespace(start=start, middle=middle, finish=finish, own=own, drain=drain)

    def page_fold(slot, p, cols=slice(None)):
        return fold(slot, lambda q: r.part.at[p * G + q, :, cols], r.r1.at[p, :, :, cols], r.s2.at[p, :, cols], r.r2.at[p, :, cols])

    def into_part(p, cols, value):
        r.part[p * G:(p + 1) * G, :, cols] = value.reshape(G, L, value.shape[-1])

    half_columns = C // 2
    down_fold = [[page_fold(2 * p + a, p, pl.ds(a * half_columns, half_columns)) for a in range(2)] for p in range(PG)]

    def down_page(p, a):
        def body(n):
            cols = pl.ds(pl.multiple_of(a * half_columns + n * tc, tc), tc)
            into_part(p, cols, mm(r.act[p], r.wd[:, cols]))

        loop(half_columns // tc, body)

    for a in range(2):
        fetch(DOWN_A + a, H)
        for p in range(PG):
            down_page(p, a)
            down_fold[p][a].start()
        for p in range(PG):
            down_fold[p][a].middle()

    def down_own(p, rows):
        return r.part[p * G + s, rows, :] + r.r1[p, xx, rows, :] + r.r2[p, rows, :].astype(F32)

    last_in = [spread(4 + 3 * PG + p, lambda q, p=p: r.lrg.at[p, block(q, L)]) for p in range(PG)]

    def last_norm(p):
        def body(rows, group_rows):
            resid = r.tg[p, rows, :] + down_own(p, rows) + param(DOWN_BIAS)
            nhat, inverse = standard(resid)
            r.out[p, rows, :] = nhat * param(GAIN2) + param(SHIFT2)
            cot = r.cot[p, rows, :].astype(F32)
            add_row(GAIN2, cot * nhat)
            add_row(SHIFT2, cot)
            grad = unstandard(cot * param(GAIN2), nhat, inverse)
            add_row(DOWN_BIAS, grad)
            r.tg[p, rows, :] = grad
            r.lrg[p, group_rows, :] = grad.astype(BF16)

        by_rows(p, body)

    for p in range(PG):
        for a in range(2):
            down_fold[p][a].finish()
        last_norm(p)
        last_in[p].start()

    def weight_chunks(lhs, rhs, owners, columns, width):
        count = len(owners)
        for i, j in enumerate(owners):
            for p in range(PG):
                r.tt[i * width:(i + 1) * width, p * W:(p + 1) * W] = lhs[p, :, block(j, width)].T
        tn = tile_of(columns)

        def value(n):
            block = rhs[:, :, lanes(n, tn)].reshape(PG * W, tn)
            full = mm(r.tt[0:count * width, :], block)
            return [full[i * width:(i + 1) * width] for i in range(count)]

        return value, columns // tn, tn

    def grad_chunks(g, owners):
        if g == PROJECT:
            return weight_chunks(r.xg, r.qkv, owners, QC, CR)
        if g == UP:
            return weight_chunks(r.nlg, r.hid, owners, FO, CR)
        if g == DOWN:
            return weight_chunks(r.act, r.lrg, owners, C, FR)
        if g == MIXING:
            return (lambda n: [mix_part(s)[block(j, SR), lanes(n, tc)] for j in owners]), C // tc, tc
        return (lambda n: [r.vc[j] for j in owners]), 1, CR

    bufs = {PROJECT: (r.bp, r.tp), MIXING: (r.bm, r.tm), UP: (r.bu, r.tu), DOWN: (r.bd, r.td), SMALL: (r.bs, r.ts)}

    def ring_copy(g, d, t):
        buf, first = bufs[g]
        count = first.shape[0]
        if t == 1:
            src, dst = first.at[half_rows(count, d)], buf.at[d, 0, half_rows(count, d)]
        else:
            src, dst = buf.at[d, t - 2], buf.at[d, t - 1]
        return remote(src, dst, r.rs.at[g, d, t - 1], r.rr.at[g, d, t - 1], ways[d])

    def ring_first(g):
        buf, first = bufs[g]
        value, count, tn = grad_chunks(g, [shifted(H)])

        def body(n):
            first[:, lanes(n, tn)] = value(n)[0].astype(first.dtype)

        loop(count, body)
        for d in range(2):
            ring_copy(g, d, 1).start()

    def ring_next(g, t):
        buf, first = bufs[g]
        size = first.shape[0]
        hop = H + 1 - t
        for d in range(2):
            ring_copy(g, d, t - 1).wait_recv()
        value, count, tn = grad_chunks(g, [shifted(hop), shifted(-hop)])

        def body(n):
            cols = lanes(n, tn)
            for d, val in enumerate(value(n)):
                if t == 2:
                    near, off = half_rows(size, d), half_rows(size, 1 - d)
                    lo, hi = d * (size // 2), (1 - d) * (size // 2)
                    buf[d, 0, near, cols] = (val[lo:lo + size // 2] + buf[d, 0, near, cols].astype(F32)).astype(buf.dtype)
                    buf[d, 0, off, cols] = val[hi:hi + size // 2].astype(buf.dtype)
                else:
                    buf[d, t - 2, :, cols] = (val + buf[d, t - 2, :, cols].astype(F32)).astype(buf.dtype)

        loop(count, body)
        for d in range(2):
            ring_copy(g, d, t).start()

    def ring_last(g, put):
        advance(g, H)
        buf, first = bufs[g]
        for d in range(2):
            ring_copy(g, d, H).wait_recv()
        value, count, tn = grad_chunks(g, [dp])

        def body(n):
            cols = lanes(n, tn)
            put(cols, value(n)[0] + buf[0, H - 1, :, cols].astype(F32) + buf[1, H - 1, :, cols].astype(F32))

        loop(count, body)
        for t in range(1, H + 1):
            for d in range(2):
                ring_copy(g, d, t).wait_send()

    reached = dict.fromkeys(range(6), 0)

    def advance(g, to=None):
        to = min(H, reached[g] + 1 if to is None else to)
        while reached[g] < to:
            reached[g] += 1
            ring_first(g) if reached[g] == 1 else ring_next(g, reached[g])

    def hidden_page(p):
        def body(n):
            cols = lanes(n, tf)
            grad = mm_t(r.lrg[p], r.wd[cols, :]) * r.gp[p, :, cols]
            r.vu[0:1, cols] += jnp.sum(grad, axis=0, keepdims=True)
            r.hid[p, :, cols] = grad.astype(BF16)

        loop(FO // tf, body)

    r.vu[...] = jnp.zeros_like(r.vu)
    normed_fold = [page_fold(2 * PG + p, p) for p in range(PG)]

    def normed_page(p):
        def body(n):
            cols = lanes(n, tc)
            into_part(p, cols, mm_t(r.hid[p], r.wu[cols, :]))

        loop(C // tc, body)

    for p in range(PG):
        last_in[p].forward()
        last_in[p].finish()
        if p == PG - 1:
            advance(DOWN)
        hidden_page(p)
        for a in range(2):
            down_fold[p][a].drain()
        normed_page(p)
        normed_fold[p].start()
        if p == PG - 1:
            advance(UP)
        normed_fold[p].middle()
    advance(DOWN)

    grads_out = [
        exchange(4 + 4 * PG + p, lambda q, p=p: r.cg.at[p, :, block(q, HC)],
                 lambda q, p=p: r.dc.at[p, block(q, L)])
        for p in range(PG)
    ]

    def first_back(p):
        def body(rows, group_rows):
            grad = r.tg[p, rows, :] + normed_fold[p].own(rows)
            nhat = r.nh1[p, rows, :]
            add_row(GAIN1, grad * nhat)
            add_row(SHIFT1, grad)
            grad = unstandard(grad * param(GAIN1), nhat, r.inv1[p, rows, 0:1])
            add_row(MIX_BIAS, grad)
            r.tg[p, rows, :] = grad
            r.frl[p, rows, :] = grad.astype(BF16)

        by_rows(p, body)

    def context_back(p):
        def body(n):
            cols = lanes(n, tc)
            r.cg[p, :, cols] = mm_t(r.frl[p], r.wm[block(n, tc // CR)].reshape(tc, C)).astype(BF16)

        loop(C // tc, body)

    for p in range(PG):
        normed_fold[p].finish()
        first_back(p)
        context_back(p)
        grads_out[p].start()
        r.dc[p, own_rows, :] = r.cg[p, :, own_heads]
        advance(DOWN if p else UP)

    def mix_part(q):
        return r.gp.at[lax.div(q, W // HC), block(lax.rem(q, W // HC), HC)]

    def mix_grad():
        for i in range(C // 256):
            for p in range(PG):
                r.tm_[:, p * L:(p + 1) * L] = r.cr[p, :, i * 256:(i + 1) * 256].T

            def body(n, i=i):
                cols = lanes(n, tc)
                full = mm(r.tm_[...], r.frl[:, :, cols].reshape(PG * L, tc))
                for k in range(256 // SR):
                    j, q = divmod(i * (256 // SR) + k, G)
                    r.gp[q * HC // W, q * HC % W + j * SR:q * HC % W + (j + 1) * SR, cols] = full[k * SR:(k + 1) * SR]

            loop(C // tc, body)

    mix_fold = fold(4 * PG, mix_part, r.m1, r.ms2, r.mr2)

    def attend_back_page(p):
        def body(hp):
            query, keys, values = pair_of(p, hp)
            d_ctx = r.dc[p, :, lanes(hp, LANES)]
            keys_t = keys.T
            for half in range(2):
                values_h = only(half, values)
                for qb in range(W // QB):
                    span = slice(qb * QB, (qb + 1) * QB)
                    d_probs = mm_t(values_h, d_ctx[span])
                    probs = r.probs[(p * pairs + hp) * 2 + half, :, span]
                    inner = jnp.sum(probs * d_probs, axis=0, keepdims=True)
                    at = slice(half * W + qb * QB, half * W + (qb + 1) * QB)
                    r.wd[0:W, at] = (probs * (d_probs - inner)).astype(BF16)
                    r.wd[W:2 * W, at] = probs.astype(BF16)
            d_keys = mm(r.wd[0:W, :], jnp.concatenate([only(0, query), only(1, query)], axis=0))
            d_values = mm(r.wd[W:2 * W, :], jnp.concatenate([only(0, d_ctx), only(1, d_ctx)], axis=0))
            d_query = [
                mm(keys_t[half * HEAD_DIM:(half + 1) * HEAD_DIM], r.wd[0:W, half * W:(half + 1) * W]) for half in range(2)
            ]
            d_query = jnp.concatenate(d_query, axis=0).T * scale
            for b, val in enumerate((d_query, d_keys * scale, d_values)):
                cols = pl.ds(pl.multiple_of(b * HC + hp * LANES, LANES), LANES)
                low = val.astype(BF16)
                r.qkv[p, :, cols] = low
                r.vp[0:1, cols] += jnp.sum(low.astype(F32), axis=0, keepdims=True)

        for hp in range(pairs):
            body(hp)
            ring_between(p, hp)

    r.vp[...] = jnp.zeros_like(r.vp)
    tokens_fold = [page_fold(3 * PG + p, p) for p in range(PG)]

    def tokens_page(p):
        def body(n):
            cols = lanes(n, tc)
            into_part(p, cols, mm_t(r.qkv[p], r.wq[cols, :]))

        loop(C // tc, body)

    def own_mix(i):
        rows = pl.ds(pl.multiple_of(i * RB, RB), RB)
        mix_part(s)[rows, :] = mix_fold.own(rows)

    def ring_between(p, hp):
        step = p * pairs + hp
        if step == 0:
            advance(UP)
        if step == 1:
            mix_grad()
            mix_fold.start()
        if step == 2:
            mix_fold.middle()
            advance(DOWN)

    for g in (DOWN_A, DOWN_B):
        gather_drain(g)
    for p in range(PG):
        grads_out[p].finish()
        attend_back_page(p)
    advance(PROJECT)
    advance(UP)

    r.vs[QUERY_BIAS:QUERY_BIAS + 1, own_heads] = r.vp[0:1, 0:HC]
    r.vs[VALUE_BIAS:VALUE_BIAS + 1, own_heads] = r.vp[0:1, 2 * HC:3 * HC]
    for j in range(D):
        r.vc[j] = r.vs[:, j * CR:(j + 1) * CR]
        r.vc[j, UP_BIAS:UP_BIAS + 1, :] = r.vu[0:1, j * FR:(j + 1) * FR]
    advance(SMALL)
    up_out = exchange(4 + 5 * PG, lambda q: r.fu.at[block(q, SR)], lambda q: r.fur.at[q])
    for p in range(PG):
        normed_fold[p].drain()
        tokens_page(p)
        tokens_fold[p].start()
        if p:
            tokens_fold[p - 1].middle()
    ring_last(DOWN, lambda cols, val: r.gdw.__setitem__((slice(None), cols), val))
    tokens_fold[PG - 1].middle()
    mix_fold.finish()
    loop(HC // RB, own_mix)
    advance(MIXING)
    advance(PROJECT)
    advance(SMALL)
    ring_last(UP, lambda cols, val: r.fu.__setitem__((slice(None), cols), val.astype(BF16)))
    up_out.start()
    r.fur[s] = r.fu[block(s, SR), :]
    for t in range(3, H + 1):
        advance(MIXING)
        advance(PROJECT)
        advance(SMALL)
    advance(MIXING, H)

    for p in range(PG):
        tokens_fold[p].finish()

        def token_rows(rows, group_rows, p=p):
            r.tg[p, rows, :] = r.tg[p, rows, :] + tokens_fold[p].own(rows)

        by_rows(p, token_rows)
    up_out.finish()
    for q in range(G):
        for j in range(D):
            r.guw[:, (j * G + q) * FR:(j * G + q + 1) * FR] = r.fur[q, :, j * FR:(j + 1) * FR].astype(F32)

    project_out = exchange(5 + 5 * PG, lambda q: r.fp.at[block(q, SR)], lambda q: r.fpr.at[q])
    small_out = exchange(6 + 5 * PG, lambda q: r.fsm, lambda q: r.fsr.at[q])
    ring_last(PROJECT, lambda cols, val: r.fp.__setitem__((slice(None), cols), val.astype(BF16)))
    project_out.start()
    ring_last(SMALL, lambda cols, val: r.fsm.__setitem__((slice(None), cols), val))
    small_out.start()
    ring_last(MIXING, lambda cols, val: r.gmw.__setitem__((slice(None), cols), val))
    r.fpr[s] = r.fp[block(s, SR), :]
    r.fsr[s] = r.fsm[...]
    project_out.finish()
    for q in range(G):
        for b in range(3):
            r.gpw[:, b * C + q * HC:b * C + (q + 1) * HC] = r.fpr[q, :, b * HC:(b + 1) * HC].astype(F32)
    small_out.finish()
    total = r.fsr[0]
    for q in range(1, G):
        total = total + r.fsr[q]
    mine = jnp.zeros((TABLE, SR), F32)
    for q in range(G):
        mine = mine + jnp.where(s == q, 1.0, 0.0) * pltpu.roll(total, (CR - q * SR) % CR, 1)[:, 0:SR]
    r.small[:, 0:SR] = mine
    r.small[UP_BIAS:UP_BIAS + 1, :] = r.fsm[UP_BIAS:UP_BIAS + 1, :]

    for g in (PROJECT, MIXING, UP, SMALL):
        gather_drain(g)
    for one in tokens_fold + [mix_fold]:
        one.drain()
    for done in exchanges:
        done()

INPUTS = ["tok", "cot", "lens", "pw", "pb", "mw", "mb", "fg", "fs", "uw", "ub", "dw", "db", "lg", "ls"]
BIG = ["out", "tg", "gpw", "gmw", "guw", "gdw"]
OUTPUTS = ["out", "tg", "gpw", "gpb", "gmw", "gmb", "gfg", "gfs", "guw", "gub", "gdw", "gdb", "glg", "gls"]
ROWS = dict(
    gpb=(QUERY_BIAS, 2), gmb=(MIX_BIAS, 1), gfg=(GAIN1, 1), gfs=(SHIFT1, 1), gub=(UP_BIAS, 1), gdb=(DOWN_BIAS, 1),
    glg=(GAIN2, 1), gls=(SHIFT2, 1),
)


def scratch_of(cfg):
    D, G, PG, L, C, F = cfg
    H = D // 2
    W, HC, FO, CR, SR = L * G, C // G, F // G, C // D, C // (D * G)
    FR, QC, heads = FO // D, 3 * HC, HEADS // G
    low = dict(
        wq=(C, QC), wm=(D, G, SR, C), wu=(C, FO), wd=(FO, C), sp=(G, SR, QC), su=(G, SR, FO), xg=(PG, W, C),
        qkv=(PG, W, QC), ctx=(PG, W, HC), cr=(PG, L, C), nlg=(PG, W, C), act=(PG, W, FO), hid=(PG, W, FO),
        s2=(PG, L, C), r2=(PG, L, C), lrg=(PG, W, C), frl=(PG, L, C), cg=(PG, L, C), dc=(PG, W, HC),
        ms2=(HC, C), mr2=(HC, C), tt=(2 * max(CR, FR), PG * W), tm_=(256, PG * L),
        bp=(2, H, CR, QC), tp=(CR, QC), bm=(2, H, SR, C), tm=(SR, C), bu=(2, H, CR, FO), tu=(CR, FO),
        bd=(2, H, FR, C), td=(FR, C),
        fu=(CR, FO), fur=(G, SR, FO), fp=(CR, QC), fpr=(G, SR, QC),
    )
    wide = dict(
        ss=(8, LANES), sm=(D, G, 8, LANES), probs=(PG * heads, W, W), nh1=(PG, L, C),
        inv1=(PG, L, LANES), gp=(PG, W, FO), part=(PG * G, L, C), r1=(PG, 2, L, C), m1=(2, HC, C),
        bs=(2, H, TABLE, CR), ts=(TABLE, CR), vs=(TABLE, C), vp=(8, QC), vu=(8, FO), vc=(D, TABLE, CR),
        pv=(TABLE, C), ubv=(8, FO), pbv=(8, QC),
        fsm=(TABLE, CR), fsr=(G, TABLE, CR),
    )
    sems = dict(
        local_sem=(2 + PG,), gs=(6, 2, H), gr=(6, 2, H), rs=(6, 2, H), rr=(6, 2, H),
        xs=(7 + 5 * PG, 3), xr=(7 + 5 * PG, 3), fs_=(4 * PG + 1, 3), fr_=(4 * PG + 1, 3),
    )
    scratch = {k: pltpu.VMEM(v, BF16) for k, v in low.items()}
    scratch |= {k: pltpu.VMEM(v, F32) for k, v in wide.items()}
    scratch |= {k: pltpu.SemaphoreType.DMA(v) for k, v in sems.items()}
    return scratch


def fits(cfg):
    D, G, PG, L, C, F = cfg
    return (
        G == 4 and D % 2 == 0 and D >= 4 and L % 128 == 0 and (C // G) % 256 == 0 and C // D == 128 and F // (D * G) == 128
        and (HEADS // G) % 2 == 0 and PG == 2 and PG * L * G == C and F // G == C and (L * G) % (C // G) == 0
    )


def fused(cfg, *args):
    D, G, PG, L, C, F = cfg
    SR = C // (D * G)
    scratch = scratch_of(cfg)
    global NAMES
    NAMES = INPUTS + BIG + ["small"] + list(scratch)
    vmem, anywhere = pl.BlockSpec(memory_space=pltpu.VMEM), pl.BlockSpec(memory_space=pl.ANY)
    where = {"tok": anywhere, "mw": anywhere, "dw": anywhere, "lens": pl.BlockSpec(memory_space=pltpu.SMEM)}
    flat = [a.reshape(1, -1) if name not in ("lens",) and a.ndim == 1 else a for name, a in zip(INPUTS, args)]
    shapes = dict(
        out=(PG, L, C), tg=(PG, L, C), gpw=(SR, 3 * C), gpb=(2, SR), gmw=(SR, C), gmb=(1, SR), gfg=(1, SR), gfs=(1, SR),
        guw=(SR, F), gub=(1, F // (D * G)), gdw=(F // (D * G), C), gdb=(1, SR), glg=(1, SR), gls=(1, SR),
    )
    given = pl.pallas_call(
        functools.partial(layer_kernel, cfg),
        out_shape=[pltpu.VMEM(shapes[k], F32) for k in BIG] + [jax.ShapeDtypeStruct((TABLE, LANES), F32)],
        in_specs=[where.get(k, vmem) for k in INPUTS],
        out_specs=[vmem] * (len(BIG) + 1),
        scratch_shapes=list(scratch.values()),
        compiler_params=pltpu.CompilerParams(collective_id=0, has_side_effects=True, vmem_limit_bytes=VMEM_LIMIT),
        name="encoder_layer",
    )(*flat)
    count = len(BIG)
    results = pl.pallas_call(
        write_out,
        out_shape=[jax.ShapeDtypeStruct(shapes[k], F32) for k in OUTPUTS],
        in_specs=[vmem] * (count + 1),
        out_specs=[anywhere if k in BIG else vmem for k in OUTPUTS],
        scratch_shapes=[pltpu.SemaphoreType.DMA((count,))],
        compiler_params=pltpu.CompilerParams(vmem_limit_bytes=VMEM_LIMIT),
        name="write_out",
    )(*[pltpu.with_memory_space_constraint(v, pltpu.VMEM) for v in given[:-1]], given[-1])
    return tuple(v.reshape(-1) if v.shape[0] == 1 else v for v in results)


def write_out(*refs):
    count = len(BIG)
    given, small = refs[:count], refs[count]
    result = dict(zip(OUTPUTS, refs[count + 1:]))
    sems = refs[-1]
    store = [pltpu.make_async_copy(given[i], result[k], sems.at[i]) for i, k in enumerate(BIG)]
    for copy in store:
        copy.start()
    for k, (row, rows) in ROWS.items():
        result[k][...] = small[row:row + rows, 0:result[k].shape[1]]
    for copy in store:
        copy.wait()


VMEM_LIMIT = 58 << 20


def per_device(*args):
    tokens, up_weight = args[0], args[9]
    D, G = lax.axis_size("dp"), lax.axis_size("seq")
    cfg = (D, G, tokens.shape[0], tokens.shape[1], tokens.shape[2], up_weight.shape[1])
    return fused(cfg, *args) if fits(cfg) else plain(*args)


MICRO = 2


def matmul(left, right):
    return jnp.dot(left, right, preferred_element_type=jnp.float32)


def against(left, right):
    return jnp.einsum("re,fe->rf", left, right, preferred_element_type=jnp.float32)


def contract_rows(left, right):
    return jnp.einsum("rd,re->de", left, right, preferred_element_type=jnp.float32)


def layer_norm(rows, gain, shift):
    center = rows - jnp.mean(rows, axis=-1, keepdims=True)
    spread = jnp.mean(center * center, axis=-1, keepdims=True)
    return center * lax.rsqrt(spread + 1e-05) * gain + shift


def gelu_exact(value):
    return 0.5 * value * (1.0 + lax.erf(value * 0.7071067811865476))


def masked_scores(query, keys, length):
    scores = jnp.einsum(
        "qhd,khd->hqk", query, keys, preferred_element_type=jnp.float32
    ) * query.shape[-1] ** (-0.5)
    valid = lax.iota(jnp.int32, keys.shape[0]) < length
    return jnp.where(valid[None, None, :], scores, -1e30)


def attend(packed, length):
    query, keys, values = (packed[:, 0], packed[:, 1], packed[:, 2])
    scores = masked_scores(query, keys, length)
    top = jnp.max(scores, axis=-1, keepdims=True)
    powers = jnp.exp(scores - top)
    total = jnp.sum(powers, axis=-1, keepdims=True)
    probs = (powers / total).astype(jnp.bfloat16)
    context = jnp.einsum("hqk,khd->qhd", probs, values, preferred_element_type=jnp.float32)
    return (
        context.astype(jnp.bfloat16).reshape(packed.shape[0], -1),
        (top + jnp.log(total))[..., 0],
    )


def attend_back(packed, context_grad, logsum, length):
    query, keys, values = (packed[:, 0], packed[:, 1], packed[:, 2])
    scale = query.shape[-1] ** (-0.5)
    scores = masked_scores(query, keys, length)
    probs = jnp.exp(scores - logsum[..., None])
    probs_grad = jnp.einsum(
        "qhd,khd->hqk", context_grad, values, preferred_element_type=jnp.float32
    )
    inner = jnp.sum(probs * probs_grad, axis=-1, keepdims=True)
    scores_grad = (probs * (probs_grad - inner)).astype(jnp.bfloat16)
    query_grad = (
        jnp.einsum("hqk,khd->qhd", scores_grad, keys, preferred_element_type=jnp.float32) * scale
    )
    keys_grad = (
        jnp.einsum("hqk,qhd->khd", scores_grad, query, preferred_element_type=jnp.float32) * scale
    )
    values_grad = jnp.einsum(
        "hqk,qhd->khd", probs.astype(jnp.bfloat16), context_grad, preferred_element_type=jnp.float32
    )
    return jnp.stack([query_grad, keys_grad, values_grad], axis=1).astype(jnp.bfloat16)


def plain(
    tokens,
    cotangent,
    lengths,
    project_weight,
    project_bias,
    mixing_weight,
    mixing_bias,
    first_gain,
    first_shift,
    up_weight,
    up_bias,
    down_weight,
    down_bias,
    last_gain,
    last_shift,
):
    groups = lax.axis_size("seq")
    (
        project_full,
        bias_pair,
        mixing_full,
        mixing_shift,
        first_scale,
        first_offset,
        up_full,
        up_shift,
        down_full,
        down_shift,
        last_scale,
        last_offset,
    ) = (
        lax.all_gather(project_weight, ("dp", "seq"), axis=0, tiled=True),
        lax.all_gather(project_bias, ("dp", "seq"), axis=1, tiled=True),
        lax.all_gather(mixing_weight, ("dp", "seq"), axis=0, tiled=True),
        lax.all_gather(mixing_bias, ("dp", "seq"), axis=0, tiled=True),
        lax.all_gather(first_gain, ("dp", "seq"), axis=0, tiled=True),
        lax.all_gather(first_shift, ("dp", "seq"), axis=0, tiled=True),
        lax.all_gather(up_weight, ("dp", "seq"), axis=0, tiled=True),
        lax.all_gather(up_bias, ("dp", "seq"), axis=0, tiled=True),
        lax.all_gather(down_weight, ("dp", "seq"), axis=0, tiled=True),
        lax.all_gather(down_bias, ("dp", "seq"), axis=0, tiled=True),
        lax.all_gather(last_gain, ("dp", "seq"), axis=0, tiled=True),
        lax.all_gather(last_shift, ("dp", "seq"), axis=0, tiled=True),
    )
    bias_pair = bias_pair.astype(jnp.float32)
    mixing_shift = mixing_shift.astype(jnp.float32)
    first_scale = first_scale.astype(jnp.float32)
    first_offset = first_offset.astype(jnp.float32)
    up_shift = up_shift.astype(jnp.float32)
    down_shift = down_shift.astype(jnp.float32)
    last_scale = last_scale.astype(jnp.float32)
    last_offset = last_offset.astype(jnp.float32)
    project_shift = jnp.concatenate([bias_pair[0], jnp.zeros_like(bias_pair[0]), bias_pair[1]])
    pages = tokens.shape[0] // MICRO
    local = tokens.shape[1]
    model = tokens.shape[2]
    width = local * groups
    slice_width = model // groups
    owned = HEADS // groups
    rows = pages * local
    outputs = []
    input_grads = []
    for micro in range(MICRO):
        begin = micro * pages
        flat = tokens[begin : begin + pages].reshape(rows, model)
        spans = lengths[begin : begin + pages]
        packed = (matmul(flat, project_full) + project_shift).astype(jnp.bfloat16)
        per_head = lax.all_to_all(
            packed.reshape(pages, local, 3, groups, slice_width),
            "seq",
            split_axis=3,
            concat_axis=1,
            tiled=True,
        )
        per_head = per_head.reshape(pages, width, 3, owned, HEAD_DIM)
        context, logsum = lax.map(lambda item: attend(item[0], item[1]), (per_head, spans))
        mixed = lax.all_to_all(context, "seq", split_axis=1, concat_axis=2, tiled=True).reshape(
            rows, model
        )
        residual = flat.astype(jnp.float32) + matmul(mixed, mixing_full) + mixing_shift
        normed, first_pull = jax.vjp(layer_norm, residual, first_scale, first_offset)
        normed_low = normed.astype(jnp.bfloat16)
        hidden_in = matmul(normed_low, up_full) + up_shift
        hidden_value, gelu_pull = jax.vjp(gelu_exact, hidden_in)
        activation = hidden_value.astype(jnp.bfloat16)
        last_resid = normed + matmul(activation, down_full) + down_shift
        output, last_pull = jax.vjp(layer_norm, last_resid, last_scale, last_offset)
        outputs.append(output.reshape(pages, local, model))
        seed_grad = cotangent[begin : begin + pages].reshape(rows, model).astype(jnp.float32)
        last_resid_grad, last_gain_grad, last_shift_grad = last_pull(seed_grad)
        down_bias_grad = jnp.sum(last_resid_grad, axis=0)
        last_resid_low = last_resid_grad.astype(jnp.bfloat16)
        down_weight_grad = contract_rows(activation, last_resid_low)
        (hidden_grad,) = gelu_pull(against(last_resid_low, down_full))
        up_bias_grad = jnp.sum(hidden_grad, axis=0)
        hidden_low = hidden_grad.astype(jnp.bfloat16)
        up_weight_grad = contract_rows(normed_low, hidden_low)
        feed_part = (
            up_weight_grad,
            up_bias_grad,
            down_weight_grad,
            down_bias_grad,
            last_gain_grad,
            last_shift_grad,
        )
        if micro == 0:
            feed_total = feed_part
        else:
            feed_total = tuple((a + b for a, b in zip(feed_total, feed_part)))
        normed_grad = last_resid_grad + against(hidden_low, up_full)
        first_resid_grad, first_gain_grad, first_shift_grad = first_pull(normed_grad)
        mixing_bias_grad = jnp.sum(first_resid_grad, axis=0)
        first_resid_low = first_resid_grad.astype(jnp.bfloat16)
        mixing_weight_grad = contract_rows(mixed, first_resid_low)
        context_grad = against(first_resid_low, mixing_full).astype(jnp.bfloat16)
        context_heads = lax.all_to_all(
            context_grad.reshape(pages, local, model),
            "seq",
            split_axis=2,
            concat_axis=1,
            tiled=True,
        )
        context_heads = context_heads.reshape(pages, width, owned, HEAD_DIM)
        packed_grad = lax.map(
            lambda item: attend_back(item[0], item[1], item[2], item[3]),
            (per_head, context_heads, logsum, spans),
        )
        packed_grad = lax.all_to_all(
            packed_grad.reshape(pages, width, 3, 1, slice_width),
            "seq",
            split_axis=1,
            concat_axis=3,
            tiled=True,
        )
        packed_grad = packed_grad.reshape(rows, 3 * model)
        bias_grad = jnp.stack(
            [
                jnp.sum(packed_grad[:, :model], axis=0, dtype=jnp.float32),
                jnp.sum(packed_grad[:, 2 * model :], axis=0, dtype=jnp.float32),
            ]
        )
        project_weight_grad = contract_rows(flat, packed_grad)
        input_grads.append(
            (first_resid_grad + against(packed_grad, project_full)).reshape(pages, local, model)
        )
        attend_part = (
            project_weight_grad,
            bias_grad,
            mixing_weight_grad,
            mixing_bias_grad,
            first_gain_grad,
            first_shift_grad,
        )
        if micro == 0:
            attend_total = attend_part
        else:
            attend_total = tuple((a + b for a, b in zip(attend_total, attend_part)))
    shards = (
        lax.psum_scatter(attend_total[0], ("dp", "seq"), scatter_dimension=0, tiled=True),
        lax.psum_scatter(attend_total[1], ("dp", "seq"), scatter_dimension=1, tiled=True),
        lax.psum_scatter(attend_total[2], ("dp", "seq"), scatter_dimension=0, tiled=True),
        lax.psum_scatter(attend_total[3], ("dp", "seq"), scatter_dimension=0, tiled=True),
        lax.psum_scatter(attend_total[4], ("dp", "seq"), scatter_dimension=0, tiled=True),
        lax.psum_scatter(attend_total[5], ("dp", "seq"), scatter_dimension=0, tiled=True),
        lax.psum_scatter(feed_total[0], ("dp", "seq"), scatter_dimension=0, tiled=True),
        lax.psum_scatter(feed_total[1], ("dp", "seq"), scatter_dimension=0, tiled=True),
        lax.psum_scatter(feed_total[2], ("dp", "seq"), scatter_dimension=0, tiled=True),
        lax.psum_scatter(feed_total[3], ("dp", "seq"), scatter_dimension=0, tiled=True),
        lax.psum_scatter(feed_total[4], ("dp", "seq"), scatter_dimension=0, tiled=True),
        lax.psum_scatter(feed_total[5], ("dp", "seq"), scatter_dimension=0, tiled=True),
    )
    layer_output = jnp.concatenate(outputs, axis=0)
    tokens_gradient = jnp.concatenate(input_grads, axis=0)
    return (
        layer_output,
        tokens_gradient,
        shards[0],
        shards[1],
        shards[2],
        shards[3],
        shards[4],
        shards[5],
        shards[6],
        shards[7],
        shards[8],
        shards[9],
        shards[10],
        shards[11],
    )


def solution(mesh):
    placed = (
        P("dp", "seq", None),
        P("dp", "seq", None),
        P("dp"),
        P(("dp", "seq"), None),
        P(None, ("dp", "seq")),
        P(("dp", "seq"), None),
        P(("dp", "seq")),
        P(("dp", "seq")),
        P(("dp", "seq")),
        P(("dp", "seq"), None),
        P(("dp", "seq")),
        P(("dp", "seq"), None),
        P(("dp", "seq")),
        P(("dp", "seq")),
        P(("dp", "seq")),
    )
    return jax.shard_map(
        per_device,
        mesh=mesh,
        in_specs=placed,
        out_specs=(
            P("dp", "seq", None),
            P("dp", "seq", None),
            P(("dp", "seq"), None),
            P(None, ("dp", "seq")),
            P(("dp", "seq"), None),
            P(("dp", "seq")),
            P(("dp", "seq")),
            P(("dp", "seq")),
            P(("dp", "seq"), None),
            P(("dp", "seq")),
            P(("dp", "seq"), None),
            P(("dp", "seq")),
            P(("dp", "seq")),
            P(("dp", "seq")),
        ),
        check_vma=False,
    )
```

```python
import functools
from types import SimpleNamespace

import jax
import jax.numpy as jnp
from jax import lax
from jax.experimental import pallas as pl
from jax.experimental.pallas import tpu as pltpu
from jax.sharding import PartitionSpec as P

HEADS = 16
HEAD_DIM = 64
F32 = jnp.float32
BF16 = jnp.bfloat16
MESH = pl.DeviceIdType.MESH
LANES = 128


def mm(left, right):
    return lax.dot_general(left, right, (((1,), (0,)), ((), ())), preferred_element_type=F32)


def mm_t(left, right):
    return lax.dot_general(left, right, (((1,), (1,)), ((), ())), preferred_element_type=F32)


def loop(count, body):
    def step(i, carry):
        body(i)
        return carry

    lax.fori_loop(0, count, step, 0)


def tile_of(columns, most=512):
    return next(size for size in (512, 384, 256, 128) if size <= most and columns % size == 0)


def lanes(index, size):
    return pl.ds(pl.multiple_of(index * size, size), size)


QUERY_BIAS, VALUE_BIAS, MIX_BIAS, GAIN1, SHIFT1, DOWN_BIAS, GAIN2, SHIFT2, UP_BIAS = range(9)
TABLE = 16
PROJECT, MIXING, UP, DOWN_A, DOWN_B, SMALL = range(6)
DOWN = DOWN_A


def layer_kernel(cfg, *refs):
    D, G, PG, L, C, F = cfg
    H = D // 2
    W = L * G
    HC = C // G
    FO = F // G
    CR = C // D
    SR = C // (D * G)
    FR = FO // D
    QC = 3 * HC
    heads = HEADS // G
    r = SimpleNamespace(**dict(zip(NAMES, refs)))

    dp = lax.axis_index("dp")
    s = lax.axis_index("seq")
    xx = lax.div(s, 2)
    cc = lax.rem(s, 2)
    side = lax.rem(dp, 2)
    pos = (1 - side) * lax.div(dp, 2) + side * (D - 1 - lax.div(dp, 2))

    def at_position(p):
        far = lax.div(p, H)
        return (1 - far) * 2 * p + far * (2 * (D - 1 - p) + 1)

    def shifted(k):
        return at_position(lax.rem(pos + (k + D) % D, D))

    right, left = (shifted(1), s), (shifted(-1), s)
    ways = (right, left)
    peer = {1: s + 1 - 2 * cc, 2: s + 2 - 4 * xx, 3: 3 - s}
    sibling, across = (dp, peer[1]), (dp, peer[2])

    def remote(src, dst, send, recv, device):
        return pltpu.make_async_remote_copy(
            src_ref=src, dst_ref=dst, send_sem=send, recv_sem=recv,
            device_id=device, device_id_type=MESH,
        )

    def block(index, size):
        return pl.ds(pl.multiple_of(index * size, size), size)

    local = []

    def load(src, dst):
        copy = pltpu.make_async_copy(src, dst, r.local_sem.at[len(local)])
        copy.start()
        local.append(copy)
        return copy

    load_mix = load(r.mw, r.wm.at[dp, s])
    load_tok = [load(r.tok.at[p], r.xg.at[p, block(s, L)]) for p in range(PG)]
    load_down = load(r.dw, r.wd.at[block(dp, FR)])

    barrier = pltpu.get_barrier_semaphore()
    partners = [right, left] + [(dp, peer[k]) for k in (1, 2, 3)]
    for device in partners:
        pl.semaphore_signal(barrier, inc=1, device_id=device, device_id_type=MESH)

    for q in range(G):
        for b in range(3):
            r.sp[q, :, b * HC:(b + 1) * HC] = r.pw[:, b * C + q * HC:b * C + (q + 1) * HC]
        for j in range(D):
            r.su[q, :, j * FR:(j + 1) * FR] = r.uw[:, (j * G + q) * FR:(j * G + q + 1) * FR]
    r.ss[...] = jnp.zeros_like(r.ss)
    per_row = LANES // SR
    smalls = {
        QUERY_BIAS: r.pb[0:1], VALUE_BIAS: r.pb[1:2], MIX_BIAS: r.mb[...], GAIN1: r.fg[...], SHIFT1: r.fs[...],
        DOWN_BIAS: r.db[...], GAIN2: r.lg[...], SHIFT2: r.ls[...],
    }
    for k, given in smalls.items():
        r.ss[k // per_row:k // per_row + 1, k % per_row * SR:(k % per_row + 1) * SR] = given.astype(F32)
    up_row = UP_BIAS // per_row
    r.ss[up_row:up_row + 1, :] = r.ub[...].astype(F32)

    pl.semaphore_wait(barrier, len(partners))

    exchanges = []

    def exchange(slot, source, target):
        def copy(k, which):
            return remote(source(peer[k]), target(which), r.xs.at[slot, k - 1], r.xr.at[slot, k - 1], (dp, peer[k]))

        def start():
            exchanges.append(lambda: [copy(k, s).wait_send() for k in (2, 3, 1)])
            for k in (2, 3, 1):
                copy(k, s).start()

        def finish():
            for k in (1, 2, 3):
                copy(k, peer[k]).wait_recv()

        return SimpleNamespace(start=start, finish=finish)

    def spread(slot, block):
        def copy(k):
            which = peer[2] if k == 2 else s
            device = across if k == 1 else sibling
            return remote(block(which), block(which), r.xs.at[slot, k], r.xr.at[slot, k], device)

        def arrived(k, which):
            return remote(block(which), block(which), r.xs.at[slot, k], r.xr.at[slot, k], sibling)

        def start():
            exchanges.append(lambda: [copy(k).wait_send() for k in range(3)])
            copy(1).start()
            copy(0).start()

        def forward():
            arrived(1, peer[2]).wait_recv()
            copy(2).start()

        def finish():
            arrived(0, peer[1]).wait_recv()
            arrived(2, peer[3]).wait_recv()

        return SimpleNamespace(start=start, forward=forward, finish=finish)

    def half_rows(count, half):
        return pl.ds(half * (count // 2), count // 2)

    def rows_of(ref, owner, count, half):
        if half is None:
            return ref.at[block(owner, count)]
        return ref.at[block(owner * 2 + half, count // 2)]

    def side_columns(half):
        return pl.ds(half * (C // 2), C // 2)

    def chunk_view(g, owner, half):
        if g == PROJECT:
            return rows_of(r.wq, owner, CR, half)
        if g == MIXING:
            return r.wm.at[owner, s] if half is None else r.wm.at[owner, s, half_rows(SR, half)]
        if g == UP:
            return rows_of(r.wu, owner, CR, half)
        if g in (DOWN_A, DOWN_B):
            return rows_of(r.wd.at[:, side_columns(g - DOWN_A)], owner, FR, half)
        return r.sm.at[owner] if half is None else r.sm.at[owner, half_rows(G, half)]

    def gather_copy(g, d, t, owner):
        view = chunk_view(g, owner, d if t == H else None)
        return remote(view, view, r.gs.at[g, d, t - 1], r.gr.at[g, d, t - 1], ways[d])

    def sent(d, t):
        return shifted(-(t - 1) if d == 0 else t - 1)

    def gather_send(g, t):
        for d in range(2):
            gather_copy(g, d, t, sent(d, t)).start()

    def gather_step(g, t):
        for d in range(2):
            gather_copy(g, d, t, shifted(-t if d == 0 else t)).wait_recv()
            if t < H:
                gather_copy(g, d, t + 1, sent(d, t + 1)).start()

    fetched = dict.fromkeys(range(6), 0)

    def fetch(g, to=None):
        to = min(H, fetched[g] + 1 if to is None else to)
        while fetched[g] < to:
            fetched[g] += 1
            gather_step(g, fetched[g])

    def gather_drain(g):
        for t in range(1, H + 1):
            for d in range(2):
                gather_copy(g, d, t, sent(d, t)).wait_send()

    give_project = exchange(0, lambda q: r.sp.at[q], lambda q: r.wq.at[block(dp * G + q, SR)])
    give_small = exchange(1, lambda q: r.ss, lambda q: r.sm.at[dp, q])
    give_up = exchange(2, lambda q: r.su.at[q], lambda q: r.wu.at[block(dp * G + q, SR)])
    tokens_in = [spread(3 + p, lambda q, p=p: r.xg.at[p, block(q, L)]) for p in range(PG)]
    give_project.start()
    give_small.start()
    load_mix.wait()
    gather_send(MIXING, 1)
    for p in range(PG):
        load_tok[p].wait()
        tokens_in[p].start()
    give_up.start()
    load_down.wait()
    gather_send(DOWN_A, 1)
    r.wq[block(dp * G + s, SR), :] = r.sp[s]
    r.wu[block(dp * G + s, SR), :] = r.su[s]
    r.sm[dp, s] = r.ss[...]
    mix_in = spread(3 + PG, lambda q: r.wm.at[:, q])
    fetch(MIXING)
    give_project.finish()
    gather_send(PROJECT, 1)
    give_small.finish()
    gather_send(SMALL, 1)
    r.vs[...] = jnp.zeros_like(r.vs)
    for t in range(1, H):
        if t == H - 1:
            give_up.finish()
            gather_send(UP, 1)
        fetch(MIXING)
        fetch(PROJECT)
        fetch(SMALL)
        if t <= PG:
            tokens_in[t - 1].forward()
    mix_in.start()
    fetch(DOWN_A)
    fetch(PROJECT)
    fetch(SMALL)
    fetch(UP)

    for row in range(UP_BIAS):
        piece = jnp.zeros((D, LANES), F32)
        lane = lax.broadcasted_iota(jnp.int32, piece.shape, 1)
        for q in range(G):
            turned = pltpu.roll(r.sm[:, q, row // per_row, :], (q - row % per_row) * SR % LANES, 1)
            piece = jnp.where((lane >= q * SR) & (lane < (q + 1) * SR), turned, piece)
        for j in range(D):
            r.pv[row:row + 1, j * CR:(j + 1) * CR] = piece[j:j + 1]
    for j in range(D):
        r.ubv[0:1, j * FR:(j + 1) * FR] = r.sm[j, s, up_row:up_row + 1, :]
    r.pbv[...] = jnp.zeros_like(r.pbv)
    own_heads = pl.ds(pl.multiple_of(s * HC, HC), HC)
    r.pbv[0:1, 0:HC] = r.pv[QUERY_BIAS:QUERY_BIAS + 1, own_heads]
    r.pbv[0:1, 2 * HC:3 * HC] = r.pv[VALUE_BIAS:VALUE_BIAS + 1, own_heads]

    def param(row):
        return r.pv[row:row + 1, :]

    tq = tile_of(QC)

    def project_page(p):
        def body(n):
            cols = lanes(n, tq)
            r.qkv[p, :, cols] = (mm(r.xg[p], r.wq[:, cols]) + r.pbv[0:1, cols]).astype(BF16)

        loop(QC // tq, body)


    pairs = heads // 2
    QB = 256 if W % 256 == 0 else W
    QF = W
    scale = HEAD_DIM ** -0.5

    def pair_of(p, hp):
        return [r.qkv[p, :, pl.ds(pl.multiple_of(b * HC + hp * LANES, LANES), LANES)] for b in range(3)]

    def only(half, rows):
        lane = lax.broadcasted_iota(jnp.int32, rows.shape, 1)
        mine = lane >= HEAD_DIM if half else lane < HEAD_DIM
        return jnp.where(mine, rows, jnp.zeros_like(rows))

    def attend_page(p):
        length = r.lens[p]

        def body(hp):
            query, keys, values = pair_of(p, hp)
            values_t = values.T
            halves = []
            for half in range(2):
                keys_h = only(half, keys)
                blocks = []
                for qb in range(W // QF):
                    scores = mm_t(keys_h, query[qb * QF:(qb + 1) * QF])
                    at_key = lax.broadcasted_iota(jnp.int32, scores.shape, 0)
                    scores = jnp.where(at_key < length, scores, -1e30)
                    top = jnp.max(scores, axis=0, keepdims=True)
                    powers = jnp.exp((scores - top) * scale)
                    probs = powers * (1.0 / jnp.sum(powers, axis=0, keepdims=True))
                    r.probs[(p * pairs + hp) * 2 + half, :, qb * QF:(qb + 1) * QF] = probs
                    blocks.append(mm(values_t[half * HEAD_DIM:(half + 1) * HEAD_DIM], probs.astype(BF16)))
                halves.append(jnp.concatenate(blocks, axis=1))
            both = jnp.concatenate(halves, axis=0).T
            r.ctx[p, :, lanes(hp, LANES)] = both.astype(BF16)

        loop(pairs, body)

    context_out = [
        exchange(4 + PG + p, lambda q, p=p: r.ctx.at[p, block(q, L)],
                 lambda q, p=p: r.cr.at[p, :, block(q, HC)])
        for p in range(PG)
    ]
    for p in range(PG):
        tokens_in[p].finish()
        project_page(p)
        if p:
            fetch(UP)
        attend_page(p)
        context_out[p].start()
        r.cr[p, :, own_heads] = r.ctx[p, block(s, L), :]
        fetch(DOWN_A)
        if p == 0:
            mix_in.forward()
            gather_send(DOWN_B, 1)
    fetch(DOWN_B)
    mix_in.finish()

    own_rows = pl.ds(pl.multiple_of(s * L, L), L)
    tc = tile_of(C)

    def mix_page(p):
        def body(n):
            cols = lanes(n, tc)
            r.tg[p, :, cols] = mm(r.cr[p], r.wm[:, :, :, cols].reshape(C, tc))

        loop(C // tc, body)

    RB = 32

    def by_rows(p, body):
        def step(i):
            body(pl.ds(pl.multiple_of(i * RB, RB), RB), pl.ds(pl.multiple_of(s * L + i * RB, RB), RB))

        loop(L // RB, step)

    def standard(rows):
        center = rows - jnp.mean(rows, axis=-1, keepdims=True)
        inverse = lax.rsqrt(jnp.mean(center * center, axis=-1, keepdims=True) + 1e-05)
        return center * inverse, inverse

    def unstandard(grad, nhat, inverse):
        return inverse * (
            grad - jnp.mean(grad, axis=-1, keepdims=True) - nhat * jnp.mean(grad * nhat, axis=-1, keepdims=True)
        )

    def add_row(row, rows):
        r.vs[row:row + 1, :] += jnp.sum(rows, axis=0, keepdims=True)

    normed_in = [spread(4 + 2 * PG + p, lambda q, p=p: r.nlg.at[p, block(q, L)]) for p in range(PG)]

    def first_norm(p):
        def body(rows, group_rows):
            resid = r.xg[p, group_rows, :].astype(F32) + r.tg[p, rows, :] + param(MIX_BIAS)
            nhat, inverse = standard(resid)
            normed = nhat * param(GAIN1) + param(SHIFT1)
            r.nh1[p, rows, :] = nhat
            r.inv1[p, rows, :] = jnp.broadcast_to(inverse, (RB, LANES))
            r.tg[p, rows, :] = normed
            r.nlg[p, group_rows, :] = normed.astype(BF16)

        by_rows(p, body)

    for p in range(PG):
        context_out[p].finish()
        mix_page(p)
        first_norm(p)
        normed_in[p].start()
    fetch(UP)

    tf = tile_of(FO)
    tu = tile_of(FO, 256)

    def up_page(p):
        def body(n):
            cols = lanes(n, tu)
            hidden = mm(r.nlg[p], r.wu[:, cols]) + r.ubv[0:1, cols]
            cdf = 0.5 * (1.0 + lax.erf(hidden * 0.7071067811865476))
            r.act[p, :, cols] = (hidden * cdf).astype(BF16)
            slope = cdf + hidden * (jnp.exp(hidden * hidden * -0.5) * 0.3989422804014327)
            r.gp[p, :, cols] = slope

        loop(FO // tu, body)

    normed_in[0].forward()
    fetch(DOWN_B)
    fetch(DOWN_A, H)
    fetch(UP, H)

    def fold(slot, part, r1, s2, r2):
        def near(k):
            return remote(part(2 * k + 1 - cc), r1.at[k], r.fs_.at[slot, k], r.fr_.at[slot, k], sibling)

        def far():
            return remote(s2, r2, r.fs_.at[slot, 2], r.fr_.at[slot, 2], across)

        def start():
            for k in range(2):
                near(k).start()

        def drain():
            for k in range(2):
                near(k).wait_send()
            far().wait_send()

        def middle():
            for k in range(2):
                near(k).wait_recv()
            count = s2.shape[0]

            def body(i):
                rows = pl.ds(pl.multiple_of(i * RB, RB), RB)
                s2[rows, :] = (part(peer[2])[rows, :] + r1[1 - xx, rows, :]).astype(BF16)

            loop(count // RB, body)
            far().start()

        def finish():
            far().wait_recv()

        def own(rows):
            return part(s)[rows, :] + r1[xx, rows, :] + r2[rows, :].astype(F32)

        return SimpleNamespace(start=start, middle=middle, finish=finish, own=own, drain=drain)

    def page_fold(slot, p, cols=slice(None)):
        return fold(slot, lambda q: r.part.at[p * G + q, :, cols], r.r1.at[p, :, :, cols], r.s2.at[p, :, cols], r.r2.at[p, :, cols])

    def into_part(p, cols, value):
        r.part[p * G:(p + 1) * G, :, cols] = value.reshape(G, L, value.shape[-1])

    half_columns = C // 2
    down_fold = [[page_fold(2 * p + a, p, pl.ds(a * half_columns, half_columns)) for a in range(2)] for p in range(PG)]

    def down_page(p, a):
        def body(n):
            cols = pl.ds(pl.multiple_of(a * half_columns + n * tc, tc), tc)
            into_part(p, cols, mm(r.act[p], r.wd[:, cols]))

        loop(half_columns // tc, body)

    for p in range(PG):
        normed_in[p].finish()
        up_page(p)
        if p:
            down_fold[p - 1][0].middle()
        if p + 1 < PG:
            normed_in[p + 1].forward()
        down_page(p, 0)
        down_fold[p][0].start()
        if p + 1 < PG:
            fetch(DOWN_B)
    down_fold[PG - 1][0].middle()
    fetch(DOWN_B, H)
    for p in range(PG):
        down_page(p, 1)
        down_fold[p][1].start()
        if p:
            down_fold[p - 1][1].middle()
    down_fold[PG - 1][1].middle()

    def down_own(p, rows):
        return r.part[p * G + s, rows, :] + r.r1[p, xx, rows, :] + r.r2[p, rows, :].astype(F32)

    last_in = [spread(4 + 3 * PG + p, lambda q, p=p: r.lrg.at[p, block(q, L)]) for p in range(PG)]

    def last_norm(p):
        def body(rows, group_rows):
            resid = r.tg[p, rows, :] + down_own(p, rows) + param(DOWN_BIAS)
            nhat, inverse = standard(resid)
            r.out[p, rows, :] = nhat * param(GAIN2) + param(SHIFT2)
            cot = r.cot[p, rows, :].astype(F32)
            add_row(GAIN2, cot * nhat)
            add_row(SHIFT2, cot)
            grad = unstandard(cot * param(GAIN2), nhat, inverse)
            add_row(DOWN_BIAS, grad)
            r.tg[p, rows, :] = grad
            r.lrg[p, group_rows, :] = grad.astype(BF16)

        by_rows(p, body)

    for p in range(PG):
        for a in range(2):
            down_fold[p][a].finish()
        last_norm(p)
        last_in[p].start()

    def weight_chunks(lhs, rhs, owners, columns, width):
        count = len(owners)
        for i, j in enumerate(owners):
            for p in range(PG):
                r.tt[i * width:(i + 1) * width, p * W:(p + 1) * W] = lhs[p, :, block(j, width)].T
        tn = tile_of(columns)

        def value(n):
            block = rhs[:, :, lanes(n, tn)].reshape(PG * W, tn)
            full = mm(r.tt[0:count * width, :], block)
            return [full[i * width:(i + 1) * width] for i in range(count)]

        return value, columns // tn, tn

    def grad_chunks(g, owners):
        if g == PROJECT:
            return weight_chunks(r.xg, r.qkv, owners, QC, CR)
        if g == UP:
            return weight_chunks(r.nlg, r.hid, owners, FO, CR)
        if g == DOWN:
            return weight_chunks(r.act, r.lrg, owners, C, FR)
        if g == MIXING:
            return (lambda n: [mix_part(s)[block(j, SR), lanes(n, tc)] for j in owners]), C // tc, tc
        return (lambda n: [r.vc[j] for j in owners]), 1, CR

    bufs = {PROJECT: (r.bp, r.tp), MIXING: (r.bm, r.tm), UP: (r.bu, r.tu), DOWN: (r.bd, r.td), SMALL: (r.bs, r.ts)}

    def ring_copy(g, d, t):
        buf, first = bufs[g]
        count = first.shape[0]
        if t == 1:
            src, dst = first.at[half_rows(count, d)], buf.at[d, 0, half_rows(count, d)]
        else:
            src, dst = buf.at[d, t - 2], buf.at[d, t - 1]
        return remote(src, dst, r.rs.at[g, d, t - 1], r.rr.at[g, d, t - 1], ways[d])

    def ring_first(g):
        buf, first = bufs[g]
        value, count, tn = grad_chunks(g, [shifted(H)])

        def body(n):
            first[:, lanes(n, tn)] = value(n)[0].astype(first.dtype)

        loop(count, body)
        for d in range(2):
            ring_copy(g, d, 1).start()

    def ring_next(g, t):
        buf, first = bufs[g]
        size = first.shape[0]
        hop = H + 1 - t
        for d in range(2):
            ring_copy(g, d, t - 1).wait_recv()
        value, count, tn = grad_chunks(g, [shifted(hop), shifted(-hop)])

        def body(n):
            cols = lanes(n, tn)
            for d, val in enumerate(value(n)):
                if t == 2:
                    near, off = half_rows(size, d), half_rows(size, 1 - d)
                    lo, hi = d * (size // 2), (1 - d) * (size // 2)
                    buf[d, 0, near, cols] = (val[lo:lo + size // 2] + buf[d, 0, near, cols].astype(F32)).astype(buf.dtype)
                    buf[d, 0, off, cols] = val[hi:hi + size // 2].astype(buf.dtype)
                else:
                    buf[d, t - 2, :, cols] = (val + buf[d, t - 2, :, cols].astype(F32)).astype(buf.dtype)

        loop(count, body)
        for d in range(2):
            ring_copy(g, d, t).start()

    def ring_last(g, put):
        advance(g, H)
        buf, first = bufs[g]
        for d in range(2):
            ring_copy(g, d, H).wait_recv()
        value, count, tn = grad_chunks(g, [dp])

        def body(n):
            cols = lanes(n, tn)
            put(cols, value(n)[0] + buf[0, H - 1, :, cols].astype(F32) + buf[1, H - 1, :, cols].astype(F32))

        loop(count, body)
        for t in range(1, H + 1):
            for d in range(2):
                ring_copy(g, d, t).wait_send()

    reached = dict.fromkeys(range(6), 0)

    def advance(g, to=None):
        to = min(H, reached[g] + 1 if to is None else to)
        while reached[g] < to:
            reached[g] += 1
            ring_first(g) if reached[g] == 1 else ring_next(g, reached[g])

    def hidden_page(p):
        def body(n):
            cols = lanes(n, tf)
            grad = mm_t(r.lrg[p], r.wd[cols, :]) * r.gp[p, :, cols]
            r.vu[0:1, cols] += jnp.sum(grad, axis=0, keepdims=True)
            r.hid[p, :, cols] = grad.astype(BF16)

        loop(FO // tf, body)

    r.vu[...] = jnp.zeros_like(r.vu)
    normed_fold = [page_fold(2 * PG + p, p) for p in range(PG)]

    def normed_page(p):
        def body(n):
            cols = lanes(n, tc)
            into_part(p, cols, mm_t(r.hid[p], r.wu[cols, :]))

        loop(C // tc, body)

    for p in range(PG):
        last_in[p].forward()
        last_in[p].finish()
        if p:
            normed_fold[p - 1].middle()
        if p == PG - 1:
            advance(DOWN)
        hidden_page(p)
        for a in range(2):
            down_fold[p][a].drain()
        normed_page(p)
        normed_fold[p].start()
    advance(UP)
    normed_fold[PG - 1].middle()
    advance(DOWN)

    grads_out = [
        exchange(4 + 4 * PG + p, lambda q, p=p: r.cg.at[p, :, block(q, HC)],
                 lambda q, p=p: r.dc.at[p, block(q, L)])
        for p in range(PG)
    ]

    def first_back(p):
        def body(rows, group_rows):
            grad = r.tg[p, rows, :] + normed_fold[p].own(rows)
            nhat = r.nh1[p, rows, :]
            add_row(GAIN1, grad * nhat)
            add_row(SHIFT1, grad)
            grad = unstandard(grad * param(GAIN1), nhat, r.inv1[p, rows, 0:1])
            add_row(MIX_BIAS, grad)
            r.tg[p, rows, :] = grad
            r.frl[p, rows, :] = grad.astype(BF16)

        by_rows(p, body)

    def context_back(p):
        def body(n):
            cols = lanes(n, tc)
            r.cg[p, :, cols] = mm_t(r.frl[p], r.wm[block(n, tc // CR)].reshape(tc, C)).astype(BF16)

        loop(C // tc, body)

    for p in range(PG):
        normed_fold[p].finish()
        first_back(p)
        context_back(p)
        grads_out[p].start()
        r.dc[p, own_rows, :] = r.cg[p, :, own_heads]
        advance(DOWN if p else UP)

    def mix_part(q):
        return r.gp.at[lax.div(q, W // HC), block(lax.rem(q, W // HC), HC)]

    def mix_grad():
        for i in range(C // 256):
            for p in range(PG):
                r.tm_[:, p * L:(p + 1) * L] = r.cr[p, :, i * 256:(i + 1) * 256].T

            def body(n, i=i):
                cols = lanes(n, tc)
                full = mm(r.tm_[...], r.frl[:, :, cols].reshape(PG * L, tc))
                for k in range(256 // SR):
                    j, q = divmod(i * (256 // SR) + k, G)
                    r.gp[q * HC // W, q * HC % W + j * SR:q * HC % W + (j + 1) * SR, cols] = full[k * SR:(k + 1) * SR]

            loop(C // tc, body)

    mix_fold = fold(4 * PG, mix_part, r.m1, r.ms2, r.mr2)

    def attend_back_page(p):
        def body(hp):
            query, keys, values = pair_of(p, hp)
            d_ctx = r.dc[p, :, lanes(hp, LANES)]
            keys_t = keys.T
            for half in range(2):
                values_h = only(half, values)
                for qb in range(W // QB):
                    span = slice(qb * QB, (qb + 1) * QB)
                    d_probs = mm_t(values_h, d_ctx[span])
                    probs = r.probs[(p * pairs + hp) * 2 + half, :, span]
                    inner = jnp.sum(probs * d_probs, axis=0, keepdims=True)
                    at = slice(half * W + qb * QB, half * W + (qb + 1) * QB)
                    r.wd[0:W, at] = (probs * (d_probs - inner)).astype(BF16)
                    r.wd[W:2 * W, at] = probs.astype(BF16)
            d_keys = mm(r.wd[0:W, :], jnp.concatenate([only(0, query), only(1, query)], axis=0))
            d_values = mm(r.wd[W:2 * W, :], jnp.concatenate([only(0, d_ctx), only(1, d_ctx)], axis=0))
            d_query = [
                mm(keys_t[half * HEAD_DIM:(half + 1) * HEAD_DIM], r.wd[0:W, half * W:(half + 1) * W]) for half in range(2)
            ]
            d_query = jnp.concatenate(d_query, axis=0).T * scale
            for b, val in enumerate((d_query, d_keys * scale, d_values)):
                cols = pl.ds(pl.multiple_of(b * HC + hp * LANES, LANES), LANES)
                low = val.astype(BF16)
                r.qkv[p, :, cols] = low
                r.vp[0:1, cols] += jnp.sum(low.astype(F32), axis=0, keepdims=True)

        for hp in range(pairs):
            body(hp)
            ring_between(p, hp)

    r.vp[...] = jnp.zeros_like(r.vp)
    tokens_fold = [page_fold(3 * PG + p, p) for p in range(PG)]

    def tokens_page(p):
        def body(n):
            cols = lanes(n, tc)
            into_part(p, cols, mm_t(r.qkv[p], r.wq[cols, :]))

        loop(C // tc, body)

    def own_mix(i):
        rows = pl.ds(pl.multiple_of(i * RB, RB), RB)
        mix_part(s)[rows, :] = mix_fold.own(rows)

    def ring_between(p, hp):
        step = p * pairs + hp
        if step == 0:
            advance(UP)
        if step == 1:
            mix_grad()
            mix_fold.start()
        if step == 2:
            mix_fold.middle()
            advance(DOWN)

    for g in (DOWN_A, DOWN_B):
        gather_drain(g)
    for p in range(PG):
        grads_out[p].finish()
        attend_back_page(p)
    advance(PROJECT)
    advance(UP)

    r.vs[QUERY_BIAS:QUERY_BIAS + 1, own_heads] = r.vp[0:1, 0:HC]
    r.vs[VALUE_BIAS:VALUE_BIAS + 1, own_heads] = r.vp[0:1, 2 * HC:3 * HC]
    for j in range(D):
        r.vc[j] = r.vs[:, j * CR:(j + 1) * CR]
        r.vc[j, UP_BIAS:UP_BIAS + 1, :] = r.vu[0:1, j * FR:(j + 1) * FR]
    advance(SMALL)
    up_out = exchange(4 + 5 * PG, lambda q: r.fu.at[block(q, SR)], lambda q: r.fur.at[q])
    for p in range(PG):
        normed_fold[p].drain()
        tokens_page(p)
        tokens_fold[p].start()
        if p:
            tokens_fold[p - 1].middle()
    ring_last(DOWN, lambda cols, val: r.gdw.__setitem__((slice(None), cols), val))
    tokens_fold[PG - 1].middle()
    mix_fold.finish()
    loop(HC // RB, own_mix)
    advance(MIXING)
    advance(PROJECT)
    advance(SMALL)
    ring_last(UP, lambda cols, val: r.fu.__setitem__((slice(None), cols), val.astype(BF16)))
    up_out.start()
    r.fur[s] = r.fu[block(s, SR), :]
    for t in range(3, H + 1):
        advance(MIXING)
        advance(PROJECT)
        advance(SMALL)
    advance(MIXING, H)

    for p in range(PG):
        tokens_fold[p].finish()

        def token_rows(rows, group_rows, p=p):
            r.tg[p, rows, :] = r.tg[p, rows, :] + tokens_fold[p].own(rows)

        by_rows(p, token_rows)
    up_out.finish()
    for q in range(G):
        for j in range(D):
            r.guw[:, (j * G + q) * FR:(j * G + q + 1) * FR] = r.fur[q, :, j * FR:(j + 1) * FR].astype(F32)

    project_out = exchange(5 + 5 * PG, lambda q: r.fp.at[block(q, SR)], lambda q: r.fpr.at[q])
    small_out = exchange(6 + 5 * PG, lambda q: r.fsm, lambda q: r.fsr.at[q])
    ring_last(PROJECT, lambda cols, val: r.fp.__setitem__((slice(None), cols), val.astype(BF16)))
    project_out.start()
    ring_last(SMALL, lambda cols, val: r.fsm.__setitem__((slice(None), cols), val))
    small_out.start()
    ring_last(MIXING, lambda cols, val: r.gmw.__setitem__((slice(None), cols), val))
    r.fpr[s] = r.fp[block(s, SR), :]
    r.fsr[s] = r.fsm[...]
    project_out.finish()
    for q in range(G):
        for b in range(3):
            r.gpw[:, b * C + q * HC:b * C + (q + 1) * HC] = r.fpr[q, :, b * HC:(b + 1) * HC].astype(F32)
    small_out.finish()
    total = r.fsr[0]
    for q in range(1, G):
        total = total + r.fsr[q]
    mine = jnp.zeros((TABLE, SR), F32)
    for q in range(G):
        mine = mine + jnp.where(s == q, 1.0, 0.0) * pltpu.roll(total, (CR - q * SR) % CR, 1)[:, 0:SR]
    r.small[:, 0:SR] = mine
    r.small[UP_BIAS:UP_BIAS + 1, :] = r.fsm[UP_BIAS:UP_BIAS + 1, :]

    for g in (PROJECT, MIXING, UP, SMALL):
        gather_drain(g)
    for one in tokens_fold + [mix_fold]:
        one.drain()
    for done in exchanges:
        done()

INPUTS = ["tok", "cot", "lens", "pw", "pb", "mw", "mb", "fg", "fs", "uw", "ub", "dw", "db", "lg", "ls"]
BIG = ["out", "tg", "gpw", "gmw", "guw", "gdw"]
OUTPUTS = ["out", "tg", "gpw", "gpb", "gmw", "gmb", "gfg", "gfs", "guw", "gub", "gdw", "gdb", "glg", "gls"]
ROWS = dict(
    gpb=(QUERY_BIAS, 2), gmb=(MIX_BIAS, 1), gfg=(GAIN1, 1), gfs=(SHIFT1, 1), gub=(UP_BIAS, 1), gdb=(DOWN_BIAS, 1),
    glg=(GAIN2, 1), gls=(SHIFT2, 1),
)


def scratch_of(cfg):
    D, G, PG, L, C, F = cfg
    H = D // 2
    W, HC, FO, CR, SR = L * G, C // G, F // G, C // D, C // (D * G)
    FR, QC, heads = FO // D, 3 * HC, HEADS // G
    low = dict(
        wq=(C, QC), wm=(D, G, SR, C), wu=(C, FO), wd=(FO, C), sp=(G, SR, QC), su=(G, SR, FO), xg=(PG, W, C),
        qkv=(PG, W, QC), ctx=(PG, W, HC), cr=(PG, L, C), nlg=(PG, W, C), act=(PG, W, FO), hid=(PG, W, FO),
        s2=(PG, L, C), r2=(PG, L, C), lrg=(PG, W, C), frl=(PG, L, C), cg=(PG, L, C), dc=(PG, W, HC),
        ms2=(HC, C), mr2=(HC, C), tt=(2 * max(CR, FR), PG * W), tm_=(256, PG * L),
        bp=(2, H, CR, QC), tp=(CR, QC), bm=(2, H, SR, C), tm=(SR, C), bu=(2, H, CR, FO), tu=(CR, FO),
        bd=(2, H, FR, C), td=(FR, C),
        fu=(CR, FO), fur=(G, SR, FO), fp=(CR, QC), fpr=(G, SR, QC),
    )
    wide = dict(
        ss=(8, LANES), sm=(D, G, 8, LANES), probs=(PG * heads, W, W), nh1=(PG, L, C),
        inv1=(PG, L, LANES), gp=(PG, W, FO), part=(PG * G, L, C), r1=(PG, 2, L, C), m1=(2, HC, C),
        bs=(2, H, TABLE, CR), ts=(TABLE, CR), vs=(TABLE, C), vp=(8, QC), vu=(8, FO), vc=(D, TABLE, CR),
        pv=(TABLE, C), ubv=(8, FO), pbv=(8, QC),
        fsm=(TABLE, CR), fsr=(G, TABLE, CR),
    )
    sems = dict(
        local_sem=(2 + PG,), gs=(6, 2, H), gr=(6, 2, H), rs=(6, 2, H), rr=(6, 2, H),
        xs=(7 + 5 * PG, 3), xr=(7 + 5 * PG, 3), fs_=(4 * PG + 1, 3), fr_=(4 * PG + 1, 3),
    )
    scratch = {k: pltpu.VMEM(v, BF16) for k, v in low.items()}
    scratch |= {k: pltpu.VMEM(v, F32) for k, v in wide.items()}
    scratch |= {k: pltpu.SemaphoreType.DMA(v) for k, v in sems.items()}
    return scratch


def fits(cfg):
    D, G, PG, L, C, F = cfg
    return (
        G == 4 and D % 2 == 0 and D >= 4 and L % 128 == 0 and (C // G) % 256 == 0 and C // D == 128 and F // (D * G) == 128
        and (HEADS // G) % 2 == 0 and PG == 2 and PG * L * G == C and F // G == C and (L * G) % (C // G) == 0
    )


def fused(cfg, *args):
    D, G, PG, L, C, F = cfg
    SR = C // (D * G)
    scratch = scratch_of(cfg)
    global NAMES
    NAMES = INPUTS + BIG + ["small"] + list(scratch)
    vmem, anywhere = pl.BlockSpec(memory_space=pltpu.VMEM), pl.BlockSpec(memory_space=pl.ANY)
    where = {"tok": anywhere, "mw": anywhere, "dw": anywhere, "lens": pl.BlockSpec(memory_space=pltpu.SMEM)}
    flat = [a.reshape(1, -1) if name not in ("lens",) and a.ndim == 1 else a for name, a in zip(INPUTS, args)]
    shapes = dict(
        out=(PG, L, C), tg=(PG, L, C), gpw=(SR, 3 * C), gpb=(2, SR), gmw=(SR, C), gmb=(1, SR), gfg=(1, SR), gfs=(1, SR),
        guw=(SR, F), gub=(1, F // (D * G)), gdw=(F // (D * G), C), gdb=(1, SR), glg=(1, SR), gls=(1, SR),
    )
    given = pl.pallas_call(
        functools.partial(layer_kernel, cfg),
        out_shape=[pltpu.VMEM(shapes[k], F32) for k in BIG] + [jax.ShapeDtypeStruct((TABLE, LANES), F32)],
        in_specs=[where.get(k, vmem) for k in INPUTS],
        out_specs=[vmem] * (len(BIG) + 1),
        scratch_shapes=list(scratch.values()),
        compiler_params=pltpu.CompilerParams(collective_id=0, has_side_effects=True, vmem_limit_bytes=VMEM_LIMIT),
        name="encoder_layer",
    )(*flat)
    count = len(BIG)
    results = pl.pallas_call(
        write_out,
        out_shape=[jax.ShapeDtypeStruct(shapes[k], F32) for k in OUTPUTS],
        in_specs=[vmem] * (count + 1),
        out_specs=[anywhere if k in BIG else vmem for k in OUTPUTS],
        scratch_shapes=[pltpu.SemaphoreType.DMA((count,))],
        compiler_params=pltpu.CompilerParams(vmem_limit_bytes=VMEM_LIMIT),
        name="write_out",
    )(*[pltpu.with_memory_space_constraint(v, pltpu.VMEM) for v in given[:-1]], given[-1])
    return tuple(v.reshape(-1) if v.shape[0] == 1 else v for v in results)


def write_out(*refs):
    count = len(BIG)
    given, small = refs[:count], refs[count]
    result = dict(zip(OUTPUTS, refs[count + 1:]))
    sems = refs[-1]
    store = [pltpu.make_async_copy(given[i], result[k], sems.at[i]) for i, k in enumerate(BIG)]
    for copy in store:
        copy.start()
    for k, (row, rows) in ROWS.items():
        result[k][...] = small[row:row + rows, 0:result[k].shape[1]]
    for copy in store:
        copy.wait()


VMEM_LIMIT = 58 << 20


def per_device(*args):
    tokens, up_weight = args[0], args[9]
    D, G = lax.axis_size("dp"), lax.axis_size("seq")
    cfg = (D, G, tokens.shape[0], tokens.shape[1], tokens.shape[2], up_weight.shape[1])
    return fused(cfg, *args) if fits(cfg) else plain(*args)


MICRO = 2


def matmul(left, right):
    return jnp.dot(left, right, preferred_element_type=jnp.float32)


def against(left, right):
    return jnp.einsum("re,fe->rf", left, right, preferred_element_type=jnp.float32)


def contract_rows(left, right):
    return jnp.einsum("rd,re->de", left, right, preferred_element_type=jnp.float32)


def layer_norm(rows, gain, shift):
    center = rows - jnp.mean(rows, axis=-1, keepdims=True)
    spread = jnp.mean(center * center, axis=-1, keepdims=True)
    return center * lax.rsqrt(spread + 1e-05) * gain + shift


def gelu_exact(value):
    return 0.5 * value * (1.0 + lax.erf(value * 0.7071067811865476))


def masked_scores(query, keys, length):
    scores = jnp.einsum(
        "qhd,khd->hqk", query, keys, preferred_element_type=jnp.float32
    ) * query.shape[-1] ** (-0.5)
    valid = lax.iota(jnp.int32, keys.shape[0]) < length
    return jnp.where(valid[None, None, :], scores, -1e30)


def attend(packed, length):
    query, keys, values = (packed[:, 0], packed[:, 1], packed[:, 2])
    scores = masked_scores(query, keys, length)
    top = jnp.max(scores, axis=-1, keepdims=True)
    powers = jnp.exp(scores - top)
    total = jnp.sum(powers, axis=-1, keepdims=True)
    probs = (powers / total).astype(jnp.bfloat16)
    context = jnp.einsum("hqk,khd->qhd", probs, values, preferred_element_type=jnp.float32)
    return (
        context.astype(jnp.bfloat16).reshape(packed.shape[0], -1),
        (top + jnp.log(total))[..., 0],
    )


def attend_back(packed, context_grad, logsum, length):
    query, keys, values = (packed[:, 0], packed[:, 1], packed[:, 2])
    scale = query.shape[-1] ** (-0.5)
    scores = masked_scores(query, keys, length)
    probs = jnp.exp(scores - logsum[..., None])
    probs_grad = jnp.einsum(
        "qhd,khd->hqk", context_grad, values, preferred_element_type=jnp.float32
    )
    inner = jnp.sum(probs * probs_grad, axis=-1, keepdims=True)
    scores_grad = (probs * (probs_grad - inner)).astype(jnp.bfloat16)
    query_grad = (
        jnp.einsum("hqk,khd->qhd", scores_grad, keys, preferred_element_type=jnp.float32) * scale
    )
    keys_grad = (
        jnp.einsum("hqk,qhd->khd", scores_grad, query, preferred_element_type=jnp.float32) * scale
    )
    values_grad = jnp.einsum(
        "hqk,qhd->khd", probs.astype(jnp.bfloat16), context_grad, preferred_element_type=jnp.float32
    )
    return jnp.stack([query_grad, keys_grad, values_grad], axis=1).astype(jnp.bfloat16)


def plain(
    tokens,
    cotangent,
    lengths,
    project_weight,
    project_bias,
    mixing_weight,
    mixing_bias,
    first_gain,
    first_shift,
    up_weight,
    up_bias,
    down_weight,
    down_bias,
    last_gain,
    last_shift,
):
    groups = lax.axis_size("seq")
    (
        project_full,
        bias_pair,
        mixing_full,
        mixing_shift,
        first_scale,
        first_offset,
        up_full,
        up_shift,
        down_full,
        down_shift,
        last_scale,
        last_offset,
    ) = (
        lax.all_gather(project_weight, ("dp", "seq"), axis=0, tiled=True),
        lax.all_gather(project_bias, ("dp", "seq"), axis=1, tiled=True),
        lax.all_gather(mixing_weight, ("dp", "seq"), axis=0, tiled=True),
        lax.all_gather(mixing_bias, ("dp", "seq"), axis=0, tiled=True),
        lax.all_gather(first_gain, ("dp", "seq"), axis=0, tiled=True),
        lax.all_gather(first_shift, ("dp", "seq"), axis=0, tiled=True),
        lax.all_gather(up_weight, ("dp", "seq"), axis=0, tiled=True),
        lax.all_gather(up_bias, ("dp", "seq"), axis=0, tiled=True),
        lax.all_gather(down_weight, ("dp", "seq"), axis=0, tiled=True),
        lax.all_gather(down_bias, ("dp", "seq"), axis=0, tiled=True),
        lax.all_gather(last_gain, ("dp", "seq"), axis=0, tiled=True),
        lax.all_gather(last_shift, ("dp", "seq"), axis=0, tiled=True),
    )
    bias_pair = bias_pair.astype(jnp.float32)
    mixing_shift = mixing_shift.astype(jnp.float32)
    first_scale = first_scale.astype(jnp.float32)
    first_offset = first_offset.astype(jnp.float32)
    up_shift = up_shift.astype(jnp.float32)
    down_shift = down_shift.astype(jnp.float32)
    last_scale = last_scale.astype(jnp.float32)
    last_offset = last_offset.astype(jnp.float32)
    project_shift = jnp.concatenate([bias_pair[0], jnp.zeros_like(bias_pair[0]), bias_pair[1]])
    pages = tokens.shape[0] // MICRO
    local = tokens.shape[1]
    model = tokens.shape[2]
    width = local * groups
    slice_width = model // groups
    owned = HEADS // groups
    rows = pages * local
    outputs = []
    input_grads = []
    for micro in range(MICRO):
        begin = micro * pages
        flat = tokens[begin : begin + pages].reshape(rows, model)
        spans = lengths[begin : begin + pages]
        packed = (matmul(flat, project_full) + project_shift).astype(jnp.bfloat16)
        per_head = lax.all_to_all(
            packed.reshape(pages, local, 3, groups, slice_width),
            "seq",
            split_axis=3,
            concat_axis=1,
            tiled=True,
        )
        per_head = per_head.reshape(pages, width, 3, owned, HEAD_DIM)
        context, logsum = lax.map(lambda item: attend(item[0], item[1]), (per_head, spans))
        mixed = lax.all_to_all(context, "seq", split_axis=1, concat_axis=2, tiled=True).reshape(
            rows, model
        )
        residual = flat.astype(jnp.float32) + matmul(mixed, mixing_full) + mixing_shift
        normed, first_pull = jax.vjp(layer_norm, residual, first_scale, first_offset)
        normed_low = normed.astype(jnp.bfloat16)
        hidden_in = matmul(normed_low, up_full) + up_shift
        hidden_value, gelu_pull = jax.vjp(gelu_exact, hidden_in)
        activation = hidden_value.astype(jnp.bfloat16)
        last_resid = normed + matmul(activation, down_full) + down_shift
        output, last_pull = jax.vjp(layer_norm, last_resid, last_scale, last_offset)
        outputs.append(output.reshape(pages, local, model))
        seed_grad = cotangent[begin : begin + pages].reshape(rows, model).astype(jnp.float32)
        last_resid_grad, last_gain_grad, last_shift_grad = last_pull(seed_grad)
        down_bias_grad = jnp.sum(last_resid_grad, axis=0)
        last_resid_low = last_resid_grad.astype(jnp.bfloat16)
        down_weight_grad = contract_rows(activation, last_resid_low)
        (hidden_grad,) = gelu_pull(against(last_resid_low, down_full))
        up_bias_grad = jnp.sum(hidden_grad, axis=0)
        hidden_low = hidden_grad.astype(jnp.bfloat16)
        up_weight_grad = contract_rows(normed_low, hidden_low)
        feed_part = (
            up_weight_grad,
            up_bias_grad,
            down_weight_grad,
            down_bias_grad,
            last_gain_grad,
            last_shift_grad,
        )
        if micro == 0:
            feed_total = feed_part
        else:
            feed_total = tuple((a + b for a, b in zip(feed_total, feed_part)))
        normed_grad = last_resid_grad + against(hidden_low, up_full)
        first_resid_grad, first_gain_grad, first_shift_grad = first_pull(normed_grad)
        mixing_bias_grad = jnp.sum(first_resid_grad, axis=0)
        first_resid_low = first_resid_grad.astype(jnp.bfloat16)
        mixing_weight_grad = contract_rows(mixed, first_resid_low)
        context_grad = against(first_resid_low, mixing_full).astype(jnp.bfloat16)
        context_heads = lax.all_to_all(
            context_grad.reshape(pages, local, model),
            "seq",
            split_axis=2,
            concat_axis=1,
            tiled=True,
        )
        context_heads = context_heads.reshape(pages, width, owned, HEAD_DIM)
        packed_grad = lax.map(
            lambda item: attend_back(item[0], item[1], item[2], item[3]),
            (per_head, context_heads, logsum, spans),
        )
        packed_grad = lax.all_to_all(
            packed_grad.reshape(pages, width, 3, 1, slice_width),
            "seq",
            split_axis=1,
            concat_axis=3,
            tiled=True,
        )
        packed_grad = packed_grad.reshape(rows, 3 * model)
        bias_grad = jnp.stack(
            [
                jnp.sum(packed_grad[:, :model], axis=0, dtype=jnp.float32),
                jnp.sum(packed_grad[:, 2 * model :], axis=0, dtype=jnp.float32),
            ]
        )
        project_weight_grad = contract_rows(flat, packed_grad)
        input_grads.append(
            (first_resid_grad + against(packed_grad, project_full)).reshape(pages, local, model)
        )
        attend_part = (
            project_weight_grad,
            bias_grad,
            mixing_weight_grad,
            mixing_bias_grad,
            first_gain_grad,
            first_shift_grad,
        )
        if micro == 0:
            attend_total = attend_part
        else:
            attend_total = tuple((a + b for a, b in zip(attend_total, attend_part)))
    shards = (
        lax.psum_scatter(attend_total[0], ("dp", "seq"), scatter_dimension=0, tiled=True),
        lax.psum_scatter(attend_total[1], ("dp", "seq"), scatter_dimension=1, tiled=True),
        lax.psum_scatter(attend_total[2], ("dp", "seq"), scatter_dimension=0, tiled=True),
        lax.psum_scatter(attend_total[3], ("dp", "seq"), scatter_dimension=0, tiled=True),
        lax.psum_scatter(attend_total[4], ("dp", "seq"), scatter_dimension=0, tiled=True),
        lax.psum_scatter(attend_total[5], ("dp", "seq"), scatter_dimension=0, tiled=True),
        lax.psum_scatter(feed_total[0], ("dp", "seq"), scatter_dimension=0, tiled=True),
        lax.psum_scatter(feed_total[1], ("dp", "seq"), scatter_dimension=0, tiled=True),
        lax.psum_scatter(feed_total[2], ("dp", "seq"), scatter_dimension=0, tiled=True),
        lax.psum_scatter(feed_total[3], ("dp", "seq"), scatter_dimension=0, tiled=True),
        lax.psum_scatter(feed_total[4], ("dp", "seq"), scatter_dimension=0, tiled=True),
        lax.psum_scatter(feed_total[5], ("dp", "seq"), scatter_dimension=0, tiled=True),
    )
    layer_output = jnp.concatenate(outputs, axis=0)
    tokens_gradient = jnp.concatenate(input_grads, axis=0)
    return (
        layer_output,
        tokens_gradient,
        shards[0],
        shards[1],
        shards[2],
        shards[3],
        shards[4],
        shards[5],
        shards[6],
        shards[7],
        shards[8],
        shards[9],
        shards[10],
        shards[11],
    )


def solution(mesh):
    placed = (
        P("dp", "seq", None),
        P("dp", "seq", None),
        P("dp"),
        P(("dp", "seq"), None),
        P(None, ("dp", "seq")),
        P(("dp", "seq"), None),
        P(("dp", "seq")),
        P(("dp", "seq")),
        P(("dp", "seq")),
        P(("dp", "seq"), None),
        P(("dp", "seq")),
        P(("dp", "seq"), None),
        P(("dp", "seq")),
        P(("dp", "seq")),
        P(("dp", "seq")),
    )
    return jax.shard_map(
        per_device,
        mesh=mesh,
        in_specs=placed,
        out_specs=(
            P("dp", "seq", None),
            P("dp", "seq", None),
            P(("dp", "seq"), None),
            P(None, ("dp", "seq")),
            P(("dp", "seq"), None),
            P(("dp", "seq")),
            P(("dp", "seq")),
            P(("dp", "seq")),
            P(("dp", "seq"), None),
            P(("dp", "seq")),
            P(("dp", "seq"), None),
            P(("dp", "seq")),
            P(("dp", "seq")),
            P(("dp", "seq")),
        ),
        check_vma=False,
    )
```

```python
import functools
from types import SimpleNamespace

import jax
import jax.numpy as jnp
from jax import lax
from jax.experimental import pallas as pl
from jax.experimental.pallas import tpu as pltpu
from jax.sharding import PartitionSpec as P

HEADS = 16
HEAD_DIM = 64
F32 = jnp.float32
BF16 = jnp.bfloat16
MESH = pl.DeviceIdType.MESH
LANES = 128


def mm(left, right):
    return lax.dot_general(left, right, (((1,), (0,)), ((), ())), preferred_element_type=F32)


def mm_t(left, right):
    return lax.dot_general(left, right, (((1,), (1,)), ((), ())), preferred_element_type=F32)


def loop(count, body):
    def step(i, carry):
        body(i)
        return carry

    lax.fori_loop(0, count, step, 0)


def tile_of(columns, most=512):
    return next(size for size in (512, 384, 256, 128) if size <= most and columns % size == 0)


def lanes(index, size):
    return pl.ds(pl.multiple_of(index * size, size), size)


QUERY_BIAS, VALUE_BIAS, MIX_BIAS, GAIN1, SHIFT1, DOWN_BIAS, GAIN2, SHIFT2, UP_BIAS = range(9)
TABLE = 16
PROJECT, MIXING, UP, DOWN_A, DOWN_B, SMALL = range(6)
DOWN = DOWN_A


def layer_kernel(cfg, *refs):
    D, G, PG, L, C, F = cfg
    H = D // 2
    W = L * G
    HC = C // G
    FO = F // G
    CR = C // D
    SR = C // (D * G)
    FR = FO // D
    QC = 3 * HC
    heads = HEADS // G
    r = SimpleNamespace(**dict(zip(NAMES, refs)))

    dp = lax.axis_index("dp")
    s = lax.axis_index("seq")
    xx = lax.div(s, 2)
    cc = lax.rem(s, 2)
    side = lax.rem(dp, 2)
    pos = (1 - side) * lax.div(dp, 2) + side * (D - 1 - lax.div(dp, 2))

    def at_position(p):
        far = lax.div(p, H)
        return (1 - far) * 2 * p + far * (2 * (D - 1 - p) + 1)

    def shifted(k):
        return at_position(lax.rem(pos + (k + D) % D, D))

    right, left = (shifted(1), s), (shifted(-1), s)
    ways = (right, left)
    peer = {1: s + 1 - 2 * cc, 2: s + 2 - 4 * xx, 3: 3 - s}
    sibling, across = (dp, peer[1]), (dp, peer[2])

    def remote(src, dst, send, recv, device):
        return pltpu.make_async_remote_copy(
            src_ref=src, dst_ref=dst, send_sem=send, recv_sem=recv,
            device_id=device, device_id_type=MESH,
        )

    def block(index, size):
        return pl.ds(pl.multiple_of(index * size, size), size)

    local = []

    def load(src, dst):
        copy = pltpu.make_async_copy(src, dst, r.local_sem.at[len(local)])
        copy.start()
        local.append(copy)
        return copy

    load_mix = load(r.mw, r.wm.at[dp, s])
    load_tok = [load(r.tok.at[p], r.xg.at[p, block(s, L)]) for p in range(PG)]
    load_down = load(r.dw, r.wd.at[block(dp, FR)])

    barrier = pltpu.get_barrier_semaphore()
    partners = [right, left] + [(dp, peer[k]) for k in (1, 2, 3)]
    for device in partners:
        pl.semaphore_signal(barrier, inc=1, device_id=device, device_id_type=MESH)

    for q in range(G):
        for b in range(3):
            r.sp[q, :, b * HC:(b + 1) * HC] = r.pw[:, b * C + q * HC:b * C + (q + 1) * HC]
        for j in range(D):
            r.su[q, :, j * FR:(j + 1) * FR] = r.uw[:, (j * G + q) * FR:(j * G + q + 1) * FR]
    r.ss[...] = jnp.zeros_like(r.ss)
    per_row = LANES // SR
    smalls = {
        QUERY_BIAS: r.pb[0:1], VALUE_BIAS: r.pb[1:2], MIX_BIAS: r.mb[...], GAIN1: r.fg[...], SHIFT1: r.fs[...],
        DOWN_BIAS: r.db[...], GAIN2: r.lg[...], SHIFT2: r.ls[...],
    }
    for k, given in smalls.items():
        r.ss[k // per_row:k // per_row + 1, k % per_row * SR:(k % per_row + 1) * SR] = given.astype(F32)
    up_row = UP_BIAS // per_row
    r.ss[up_row:up_row + 1, :] = r.ub[...].astype(F32)

    pl.semaphore_wait(barrier, len(partners))

    exchanges = []

    def exchange(slot, source, target):
        def copy(k, which):
            return remote(source(peer[k]), target(which), r.xs.at[slot, k - 1], r.xr.at[slot, k - 1], (dp, peer[k]))

        def start():
            exchanges.append(lambda: [copy(k, s).wait_send() for k in (2, 3, 1)])
            for k in (2, 3, 1):
                copy(k, s).start()

        def finish():
            for k in (1, 2, 3):
                copy(k, peer[k]).wait_recv()

        return SimpleNamespace(start=start, finish=finish)

    def spread(slot, block):
        def copy(k):
            which = peer[2] if k == 2 else s
            device = across if k == 1 else sibling
            return remote(block(which), block(which), r.xs.at[slot, k], r.xr.at[slot, k], device)

        def arrived(k, which):
            return remote(block(which), block(which), r.xs.at[slot, k], r.xr.at[slot, k], sibling)

        def start():
            exchanges.append(lambda: [copy(k).wait_send() for k in range(3)])
            copy(1).start()
            copy(0).start()

        def forward():
            arrived(1, peer[2]).wait_recv()
            copy(2).start()

        def finish():
            arrived(0, peer[1]).wait_recv()
            arrived(2, peer[3]).wait_recv()

        return SimpleNamespace(start=start, forward=forward, finish=finish)

    def half_rows(count, half):
        return pl.ds(half * (count // 2), count // 2)

    def rows_of(ref, owner, count, half):
        if half is None:
            return ref.at[block(owner, count)]
        return ref.at[block(owner * 2 + half, count // 2)]

    def side_columns(half):
        return pl.ds(half * (C // 2), C // 2)

    def chunk_view(g, owner, half):
        if g == PROJECT:
            return rows_of(r.wq, owner, CR, half)
        if g == MIXING:
            return r.wm.at[owner, s] if half is None else r.wm.at[owner, s, half_rows(SR, half)]
        if g == UP:
            return rows_of(r.wu, owner, CR, half)
        if g in (DOWN_A, DOWN_B):
            return rows_of(r.wd.at[:, side_columns(g - DOWN_A)], owner, FR, half)
        return r.sm.at[owner] if half is None else r.sm.at[owner, half_rows(G, half)]

    def gather_copy(g, d, t, owner):
        view = chunk_view(g, owner, d if t == H else None)
        return remote(view, view, r.gs.at[g, d, t - 1], r.gr.at[g, d, t - 1], ways[d])

    def sent(d, t):
        return shifted(-(t - 1) if d == 0 else t - 1)

    def gather_send(g, t):
        for d in range(2):
            gather_copy(g, d, t, sent(d, t)).start()

    def gather_step(g, t):
        for d in range(2):
            gather_copy(g, d, t, shifted(-t if d == 0 else t)).wait_recv()
            if t < H:
                gather_copy(g, d, t + 1, sent(d, t + 1)).start()

    fetched = dict.fromkeys(range(6), 0)

    def fetch(g, to=None):
        to = min(H, fetched[g] + 1 if to is None else to)
        while fetched[g] < to:
            fetched[g] += 1
            gather_step(g, fetched[g])

    def gather_drain(g):
        for t in range(1, H + 1):
            for d in range(2):
                gather_copy(g, d, t, sent(d, t)).wait_send()

    give_project = exchange(0, lambda q: r.sp.at[q], lambda q: r.wq.at[block(dp * G + q, SR)])
    give_small = exchange(1, lambda q: r.ss, lambda q: r.sm.at[dp, q])
    give_up = exchange(2, lambda q: r.su.at[q], lambda q: r.wu.at[block(dp * G + q, SR)])
    tokens_in = [spread(3 + p, lambda q, p=p: r.xg.at[p, block(q, L)]) for p in range(PG)]
    give_project.start()
    give_small.start()
    load_mix.wait()
    gather_send(MIXING, 1)
    for p in range(PG):
        load_tok[p].wait()
        tokens_in[p].start()
    give_up.start()
    load_down.wait()
    gather_send(DOWN_A, 1)
    r.wq[block(dp * G + s, SR), :] = r.sp[s]
    r.wu[block(dp * G + s, SR), :] = r.su[s]
    r.sm[dp, s] = r.ss[...]
    mix_in = spread(3 + PG, lambda q: r.wm.at[:, q])
    fetch(MIXING)
    give_project.finish()
    gather_send(PROJECT, 1)
    give_small.finish()
    gather_send(SMALL, 1)
    r.vs[...] = jnp.zeros_like(r.vs)
    for t in range(1, H):
        if t == H - 1:
            give_up.finish()
            gather_send(UP, 1)
        fetch(MIXING)
        fetch(PROJECT)
        fetch(SMALL)
        if t <= PG:
            tokens_in[t - 1].forward()
    mix_in.start()
    fetch(DOWN_A)
    fetch(PROJECT)
    fetch(SMALL)
    fetch(UP)

    for row in range(UP_BIAS):
        piece = jnp.zeros((D, LANES), F32)
        lane = lax.broadcasted_iota(jnp.int32, piece.shape, 1)
        for q in range(G):
            turned = pltpu.roll(r.sm[:, q, row // per_row, :], (q - row % per_row) * SR % LANES, 1)
            piece = jnp.where((lane >= q * SR) & (lane < (q + 1) * SR), turned, piece)
        for j in range(D):
            r.pv[row:row + 1, j * CR:(j + 1) * CR] = piece[j:j + 1]
    for j in range(D):
        r.ubv[0:1, j * FR:(j + 1) * FR] = r.sm[j, s, up_row:up_row + 1, :]
    r.pbv[...] = jnp.zeros_like(r.pbv)
    own_heads = pl.ds(pl.multiple_of(s * HC, HC), HC)
    r.pbv[0:1, 0:HC] = r.pv[QUERY_BIAS:QUERY_BIAS + 1, own_heads]
    r.pbv[0:1, 2 * HC:3 * HC] = r.pv[VALUE_BIAS:VALUE_BIAS + 1, own_heads]

    def param(row):
        return r.pv[row:row + 1, :]

    tq = tile_of(QC)

    def project_page(p):
        def body(n):
            cols = lanes(n, tq)
            r.qkv[p, :, cols] = (mm(r.xg[p], r.wq[:, cols]) + r.pbv[0:1, cols]).astype(BF16)

        loop(QC // tq, body)


    pairs = heads // 2
    QB = 256 if W % 256 == 0 else W
    QF = W
    scale = HEAD_DIM ** -0.5

    def pair_of(p, hp):
        return [r.qkv[p, :, pl.ds(pl.multiple_of(b * HC + hp * LANES, LANES), LANES)] for b in range(3)]

    def only(half, rows):
        lane = lax.broadcasted_iota(jnp.int32, rows.shape, 1)
        mine = lane >= HEAD_DIM if half else lane < HEAD_DIM
        return jnp.where(mine, rows, jnp.zeros_like(rows))

    def attend_page(p):
        length = r.lens[p]

        def body(hp):
            query, keys, values = pair_of(p, hp)
            values_t = values.T
            halves = []
            for half in range(2):
                keys_h = only(half, keys)
                blocks = []
                for qb in range(W // QF):
                    scores = mm_t(keys_h, query[qb * QF:(qb + 1) * QF])
                    at_key = lax.broadcasted_iota(jnp.int32, scores.shape, 0)
                    scores = jnp.where(at_key < length, scores, -1e30)
                    top = jnp.max(scores, axis=0, keepdims=True)
                    powers = jnp.exp((scores - top) * scale)
                    probs = powers * (1.0 / jnp.sum(powers, axis=0, keepdims=True))
                    r.probs[(p * pairs + hp) * 2 + half, :, qb * QF:(qb + 1) * QF] = probs
                    blocks.append(mm(values_t[half * HEAD_DIM:(half + 1) * HEAD_DIM], probs.astype(BF16)))
                halves.append(jnp.concatenate(blocks, axis=1))
            both = jnp.concatenate(halves, axis=0).T
            r.ctx[p, :, lanes(hp, LANES)] = both.astype(BF16)

        loop(pairs, body)

    context_out = [
        exchange(4 + PG + p, lambda q, p=p: r.ctx.at[p, block(q, L)],
                 lambda q, p=p: r.cr.at[p, :, block(q, HC)])
        for p in range(PG)
    ]
    for p in range(PG):
        tokens_in[p].finish()
        project_page(p)
        if p:
            fetch(UP)
        attend_page(p)
        context_out[p].start()
        r.cr[p, :, own_heads] = r.ctx[p, block(s, L), :]
        fetch(DOWN_A)
        if p == 0:
            mix_in.forward()
            gather_send(DOWN_B, 1)
    fetch(DOWN_B)
    mix_in.finish()

    own_rows = pl.ds(pl.multiple_of(s * L, L), L)
    tc = tile_of(C)

    def mix_page(p):
        def body(n):
            cols = lanes(n, tc)
            r.tg[p, :, cols] = mm(r.cr[p], r.wm[:, :, :, cols].reshape(C, tc))

        loop(C // tc, body)

    RB = 32

    def by_rows(p, body):
        def step(i):
            body(pl.ds(pl.multiple_of(i * RB, RB), RB), pl.ds(pl.multiple_of(s * L + i * RB, RB), RB))

        loop(L // RB, step)

    def standard(rows):
        center = rows - jnp.mean(rows, axis=-1, keepdims=True)
        inverse = lax.rsqrt(jnp.mean(center * center, axis=-1, keepdims=True) + 1e-05)
        return center * inverse, inverse

    def unstandard(grad, nhat, inverse):
        return inverse * (
            grad - jnp.mean(grad, axis=-1, keepdims=True) - nhat * jnp.mean(grad * nhat, axis=-1, keepdims=True)
        )

    def add_row(row, rows):
        r.vs[row:row + 1, :] += jnp.sum(rows, axis=0, keepdims=True)

    normed_in = [spread(4 + 2 * PG + p, lambda q, p=p: r.nlg.at[p, block(q, L)]) for p in range(PG)]

    def first_norm(p):
        def body(rows, group_rows):
            resid = r.xg[p, group_rows, :].astype(F32) + r.tg[p, rows, :] + param(MIX_BIAS)
            nhat, inverse = standard(resid)
            normed = nhat * param(GAIN1) + param(SHIFT1)
            r.nh1[p, rows, :] = nhat
            r.inv1[p, rows, :] = jnp.broadcast_to(inverse, (RB, LANES))
            r.tg[p, rows, :] = normed
            r.nlg[p, group_rows, :] = normed.astype(BF16)

        by_rows(p, body)

    for p in range(PG):
        context_out[p].finish()
        mix_page(p)
        first_norm(p)
        normed_in[p].start()
    fetch(UP)

    tf = tile_of(FO)
    tu = tile_of(FO, 256)

    def up_page(p):
        def body(n):
            cols = lanes(n, tu)
            hidden = mm(r.nlg[p], r.wu[:, cols]) + r.ubv[0:1, cols]
            cdf = 0.5 * (1.0 + lax.erf(hidden * 0.7071067811865476))
            r.act[p, :, cols] = (hidden * cdf).astype(BF16)
            slope = cdf + hidden * (jnp.exp(hidden * hidden * -0.5) * 0.3989422804014327)
            r.gp[p, :, cols] = slope

        loop(FO // tu, body)

    normed_in[0].forward()
    fetch(DOWN_B)
    fetch(DOWN_A, H)
    fetch(UP, H)

    def fold(slot, part, r1, s2, r2):
        def near(k):
            return remote(part(2 * k + 1 - cc), r1.at[k], r.fs_.at[slot, k], r.fr_.at[slot, k], sibling)

        def far():
            return remote(s2, r2, r.fs_.at[slot, 2], r.fr_.at[slot, 2], across)

        def start():
            for k in range(2):
                near(k).start()

        def drain():
            for k in range(2):
                near(k).wait_send()
            far().wait_send()

        def middle():
            for k in range(2):
                near(k).wait_recv()
            count = s2.shape[0]

            def body(i):
                rows = pl.ds(pl.multiple_of(i * RB, RB), RB)
                s2[rows, :] = (part(peer[2])[rows, :] + r1[1 - xx, rows, :]).astype(BF16)

            loop(count // RB, body)
            far().start()

        def finish():
            far().wait_recv()

        def own(rows):
            return part(s)[rows, :] + r1[xx, rows, :] + r2[rows, :].astype(F32)

        return SimpleNamespace(start=start, middle=middle, finish=finish, own=own, drain=drain)

    def page_fold(slot, p, cols=slice(None)):
        return fold(slot, lambda q: r.part.at[p * G + q, :, cols], r.r1.at[p, :, :, cols], r.s2.at[p, :, cols], r.r2.at[p, :, cols])

    def into_part(p, cols, value):
        r.part[p * G:(p + 1) * G, :, cols] = value.reshape(G, L, value.shape[-1])

    half_columns = C // 2
    down_fold = [[page_fold(2 * p + a, p, pl.ds(a * half_columns, half_columns)) for a in range(2)] for p in range(PG)]

    def down_page(p, a):
        def body(n):
            cols = pl.ds(pl.multiple_of(a * half_columns + n * tc, tc), tc)
            into_part(p, cols, mm(r.act[p], r.wd[:, cols]))

        loop(half_columns // tc, body)

    for p in range(PG):
        normed_in[p].finish()
        up_page(p)
        if p:
            down_fold[p - 1][0].middle()
        if p + 1 < PG:
            normed_in[p + 1].forward()
        down_page(p, 0)
        down_fold[p][0].start()
        if p + 1 < PG:
            fetch(DOWN_B)
    down_fold[PG - 1][0].middle()
    fetch(DOWN_B, H)
    for p in range(PG):
        down_page(p, 1)
        down_fold[p][1].start()
        if p:
            down_fold[p - 1][1].middle()
    down_fold[PG - 1][1].middle()

    def down_own(p, rows):
        return r.part[p * G + s, rows, :] + r.r1[p, xx, rows, :] + r.r2[p, rows, :].astype(F32)

    last_in = [spread(4 + 3 * PG + p, lambda q, p=p: r.lrg.at[p, block(q, L)]) for p in range(PG)]

    def last_norm(p):
        def body(rows, group_rows):
            resid = r.tg[p, rows, :] + down_own(p, rows) + param(DOWN_BIAS)
            nhat, inverse = standard(resid)
            r.out[p, rows, :] = nhat * param(GAIN2) + param(SHIFT2)
            cot = r.cot[p, rows, :].astype(F32)
            add_row(GAIN2, cot * nhat)
            add_row(SHIFT2, cot)
            grad = unstandard(cot * param(GAIN2), nhat, inverse)
            add_row(DOWN_BIAS, grad)
            r.tg[p, rows, :] = grad
            r.lrg[p, group_rows, :] = grad.astype(BF16)

        by_rows(p, body)

    for p in range(PG):
        for a in range(2):
            down_fold[p][a].finish()
        last_norm(p)
        last_in[p].start()

    def weight_chunks(lhs, rhs, owners, columns, width):
        count = len(owners)
        for i, j in enumerate(owners):
            for p in range(PG):
                r.tt[i * width:(i + 1) * width, p * W:(p + 1) * W] = lhs[p, :, block(j, width)].T
        tn = tile_of(columns)

        def value(n):
            block = rhs[:, :, lanes(n, tn)].reshape(PG * W, tn)
            full = mm(r.tt[0:count * width, :], block)
            return [full[i * width:(i + 1) * width] for i in range(count)]

        return value, columns // tn, tn

    def grad_chunks(g, owners):
        if g == PROJECT:
            return weight_chunks(r.xg, r.qkv, owners, QC, CR)
        if g == UP:
            return weight_chunks(r.nlg, r.hid, owners, FO, CR)
        if g == DOWN:
            return weight_chunks(r.act, r.lrg, owners, C, FR)
        if g == MIXING:
            return (lambda n: [mix_part(s)[block(j, SR), lanes(n, tc)] for j in owners]), C // tc, tc
        return (lambda n: [r.vc[j] for j in owners]), 1, CR

    bufs = {PROJECT: (r.bp, r.tp), MIXING: (r.bm, r.tm), UP: (r.bu, r.tu), DOWN: (r.bd, r.td), SMALL: (r.bs, r.ts)}

    def ring_copy(g, d, t):
        buf, first = bufs[g]
        count = first.shape[0]
        if t == 1:
            src, dst = first.at[half_rows(count, d)], buf.at[d, 0, half_rows(count, d)]
        else:
            src, dst = buf.at[d, t - 2], buf.at[d, t - 1]
        return remote(src, dst, r.rs.at[g, d, t - 1], r.rr.at[g, d, t - 1], ways[d])

    def ring_first(g):
        buf, first = bufs[g]
        value, count, tn = grad_chunks(g, [shifted(H)])

        def body(n):
            first[:, lanes(n, tn)] = value(n)[0].astype(first.dtype)

        loop(count, body)
        for d in range(2):
            ring_copy(g, d, 1).start()

    def ahead(g, held, value, count, tn):
        if g != PROJECT:
            return value, count, tn

        def body(n):
            for i, val in enumerate(value(n)):
                r.m1[i, 0:CR, lanes(n, tn)] = val

        loop(count, body)
        return (lambda n: [r.m1[i, 0:CR, lanes(n, tn)] for i in range(held)]), count, tn

    def ring_next(g, t):
        buf, first = bufs[g]
        size = first.shape[0]
        hop = H + 1 - t
        value, count, tn = ahead(g, 2, *grad_chunks(g, [shifted(hop), shifted(-hop)]))
        for d in range(2):
            ring_copy(g, d, t - 1).wait_recv()

        def body(n):
            cols = lanes(n, tn)
            for d, val in enumerate(value(n)):
                if t == 2:
                    near, off = half_rows(size, d), half_rows(size, 1 - d)
                    lo, hi = d * (size // 2), (1 - d) * (size // 2)
                    buf[d, 0, near, cols] = (val[lo:lo + size // 2] + buf[d, 0, near, cols].astype(F32)).astype(buf.dtype)
                    buf[d, 0, off, cols] = val[hi:hi + size // 2].astype(buf.dtype)
                else:
                    buf[d, t - 2, :, cols] = (val + buf[d, t - 2, :, cols].astype(F32)).astype(buf.dtype)

        loop(count, body)
        for d in range(2):
            ring_copy(g, d, t).start()

    def ring_last(g, put):
        advance(g, H)
        buf, first = bufs[g]
        value, count, tn = ahead(g, 1, *grad_chunks(g, [dp]))
        for d in range(2):
            ring_copy(g, d, H).wait_recv()

        def body(n):
            cols = lanes(n, tn)
            put(cols, value(n)[0] + buf[0, H - 1, :, cols].astype(F32) + buf[1, H - 1, :, cols].astype(F32))

        loop(count, body)
        for t in range(1, H + 1):
            for d in range(2):
                ring_copy(g, d, t).wait_send()

    reached = dict.fromkeys(range(6), 0)

    def advance(g, to=None):
        to = min(H, reached[g] + 1 if to is None else to)
        while reached[g] < to:
            reached[g] += 1
            ring_first(g) if reached[g] == 1 else ring_next(g, reached[g])

    def hidden_page(p):
        def body(n):
            cols = lanes(n, tf)
            grad = mm_t(r.lrg[p], r.wd[cols, :]) * r.gp[p, :, cols]
            r.vu[0:1, cols] += jnp.sum(grad, axis=0, keepdims=True)
            r.hid[p, :, cols] = grad.astype(BF16)

        loop(FO // tf, body)

    r.vu[...] = jnp.zeros_like(r.vu)
    normed_fold = [page_fold(2 * PG + p, p) for p in range(PG)]

    def normed_page(p):
        def body(n):
            cols = lanes(n, tc)
            into_part(p, cols, mm_t(r.hid[p], r.wu[cols, :]))

        loop(C // tc, body)

    for p in range(PG):
        last_in[p].forward()
        last_in[p].finish()
        if p:
            normed_fold[p - 1].middle()
        if p == PG - 1:
            advance(DOWN)
        hidden_page(p)
        for a in range(2):
            down_fold[p][a].drain()
        normed_page(p)
        normed_fold[p].start()
    advance(UP)
    normed_fold[PG - 1].middle()
    advance(DOWN)

    grads_out = [
        exchange(4 + 4 * PG + p, lambda q, p=p: r.cg.at[p, :, block(q, HC)],
                 lambda q, p=p: r.dc.at[p, block(q, L)])
        for p in range(PG)
    ]

    def first_back(p):
        def body(rows, group_rows):
            grad = r.tg[p, rows, :] + normed_fold[p].own(rows)
            nhat = r.nh1[p, rows, :]
            add_row(GAIN1, grad * nhat)
            add_row(SHIFT1, grad)
            grad = unstandard(grad * param(GAIN1), nhat, r.inv1[p, rows, 0:1])
            add_row(MIX_BIAS, grad)
            r.tg[p, rows, :] = grad
            r.frl[p, rows, :] = grad.astype(BF16)

        by_rows(p, body)

    def context_back(p):
        def body(n):
            cols = lanes(n, tc)
            r.cg[p, :, cols] = mm_t(r.frl[p], r.wm[block(n, tc // CR)].reshape(tc, C)).astype(BF16)

        loop(C // tc, body)

    for p in range(PG):
        normed_fold[p].finish()
        first_back(p)
        context_back(p)
        grads_out[p].start()
        r.dc[p, own_rows, :] = r.cg[p, :, own_heads]
        advance(DOWN if p else UP)

    def mix_part(q):
        return r.gp.at[lax.div(q, W // HC), block(lax.rem(q, W // HC), HC)]

    def mix_grad():
        for i in range(C // 256):
            for p in range(PG):
                r.tm_[:, p * L:(p + 1) * L] = r.cr[p, :, i * 256:(i + 1) * 256].T

            def body(n, i=i):
                cols = lanes(n, tc)
                full = mm(r.tm_[...], r.frl[:, :, cols].reshape(PG * L, tc))
                for k in range(256 // SR):
                    j, q = divmod(i * (256 // SR) + k, G)
                    r.gp[q * HC // W, q * HC % W + j * SR:q * HC % W + (j + 1) * SR, cols] = full[k * SR:(k + 1) * SR]

            loop(C // tc, body)

    mix_fold = fold(4 * PG, mix_part, r.m1, r.ms2, r.mr2)

    def attend_back_page(p):
        def body(hp):
            query, keys, values = pair_of(p, hp)
            d_ctx = r.dc[p, :, lanes(hp, LANES)]
            keys_t = keys.T
            for half in range(2):
                values_h = only(half, values)
                for qb in range(W // QB):
                    span = slice(qb * QB, (qb + 1) * QB)
                    d_probs = mm_t(values_h, d_ctx[span])
                    probs = r.probs[(p * pairs + hp) * 2 + half, :, span]
                    inner = jnp.sum(probs * d_probs, axis=0, keepdims=True)
                    at = slice(half * W + qb * QB, half * W + (qb + 1) * QB)
                    r.wd[0:W, at] = (probs * (d_probs - inner)).astype(BF16)
                    r.wd[W:2 * W, at] = probs.astype(BF16)
            d_keys = mm(r.wd[0:W, :], jnp.concatenate([only(0, query), only(1, query)], axis=0))
            d_values = mm(r.wd[W:2 * W, :], jnp.concatenate([only(0, d_ctx), only(1, d_ctx)], axis=0))
            d_query = [
                mm(keys_t[half * HEAD_DIM:(half + 1) * HEAD_DIM], r.wd[0:W, half * W:(half + 1) * W]) for half in range(2)
            ]
            d_query = jnp.concatenate(d_query, axis=0).T * scale
            for b, val in enumerate((d_query, d_keys * scale, d_values)):
                cols = pl.ds(pl.multiple_of(b * HC + hp * LANES, LANES), LANES)
                low = val.astype(BF16)
                r.qkv[p, :, cols] = low
                r.vp[0:1, cols] += jnp.sum(low.astype(F32), axis=0, keepdims=True)

        for hp in range(pairs):
            body(hp)
            ring_between(p, hp)

    r.vp[...] = jnp.zeros_like(r.vp)
    tokens_fold = [page_fold(3 * PG + p, p) for p in range(PG)]

    def tokens_page(p):
        def body(n):
            cols = lanes(n, tc)
            into_part(p, cols, mm_t(r.qkv[p], r.wq[cols, :]))

        loop(C // tc, body)

    def own_mix(i):
        rows = pl.ds(pl.multiple_of(i * RB, RB), RB)
        mix_part(s)[rows, :] = mix_fold.own(rows)

    def ring_between(p, hp):
        step = p * pairs + hp
        if step == 0:
            advance(UP)
        if step == 1:
            mix_grad()
            mix_fold.start()
        if step == 2:
            mix_fold.middle()
            advance(DOWN)

    for g in (DOWN_A, DOWN_B):
        gather_drain(g)
    for p in range(PG):
        grads_out[p].finish()
        attend_back_page(p)
    advance(PROJECT)
    advance(UP)

    r.vs[QUERY_BIAS:QUERY_BIAS + 1, own_heads] = r.vp[0:1, 0:HC]
    r.vs[VALUE_BIAS:VALUE_BIAS + 1, own_heads] = r.vp[0:1, 2 * HC:3 * HC]
    for j in range(D):
        r.vc[j] = r.vs[:, j * CR:(j + 1) * CR]
        r.vc[j, UP_BIAS:UP_BIAS + 1, :] = r.vu[0:1, j * FR:(j + 1) * FR]
    advance(SMALL)
    up_out = exchange(4 + 5 * PG, lambda q: r.fu.at[block(q, SR)], lambda q: r.fur.at[q])
    for p in range(PG):
        normed_fold[p].drain()
        tokens_page(p)
        tokens_fold[p].start()
        if p:
            tokens_fold[p - 1].middle()
    ring_last(DOWN, lambda cols, val: r.gdw.__setitem__((slice(None), cols), val))
    tokens_fold[PG - 1].middle()
    mix_fold.finish()
    loop(HC // RB, own_mix)
    advance(MIXING)
    advance(PROJECT)
    advance(SMALL)
    ring_last(UP, lambda cols, val: r.fu.__setitem__((slice(None), cols), val.astype(BF16)))
    up_out.start()
    r.fur[s] = r.fu[block(s, SR), :]
    for t in range(3, H + 1):
        advance(MIXING)
        advance(PROJECT)
        advance(SMALL)
    advance(MIXING, H)

    for p in range(PG):
        tokens_fold[p].finish()

        def token_rows(rows, group_rows, p=p):
            r.tg[p, rows, :] = r.tg[p, rows, :] + tokens_fold[p].own(rows)

        by_rows(p, token_rows)
    up_out.finish()
    for q in range(G):
        for j in range(D):
            r.guw[:, (j * G + q) * FR:(j * G + q + 1) * FR] = r.fur[q, :, j * FR:(j + 1) * FR].astype(F32)

    project_out = exchange(5 + 5 * PG, lambda q: r.fp.at[block(q, SR)], lambda q: r.fpr.at[q])
    small_out = exchange(6 + 5 * PG, lambda q: r.fsm, lambda q: r.fsr.at[q])
    ring_last(PROJECT, lambda cols, val: r.fp.__setitem__((slice(None), cols), val.astype(BF16)))
    project_out.start()
    ring_last(SMALL, lambda cols, val: r.fsm.__setitem__((slice(None), cols), val))
    small_out.start()
    ring_last(MIXING, lambda cols, val: r.gmw.__setitem__((slice(None), cols), val))
    r.fpr[s] = r.fp[block(s, SR), :]
    r.fsr[s] = r.fsm[...]
    project_out.finish()
    for q in range(G):
        for b in range(3):
            r.gpw[:, b * C + q * HC:b * C + (q + 1) * HC] = r.fpr[q, :, b * HC:(b + 1) * HC].astype(F32)
    small_out.finish()
    total = r.fsr[0]
    for q in range(1, G):
        total = total + r.fsr[q]
    mine = jnp.zeros((TABLE, SR), F32)
    for q in range(G):
        mine = mine + jnp.where(s == q, 1.0, 0.0) * pltpu.roll(total, (CR - q * SR) % CR, 1)[:, 0:SR]
    r.small[:, 0:SR] = mine
    r.small[UP_BIAS:UP_BIAS + 1, :] = r.fsm[UP_BIAS:UP_BIAS + 1, :]

    for g in (PROJECT, MIXING, UP, SMALL):
        gather_drain(g)
    for one in tokens_fold + [mix_fold]:
        one.drain()
    for done in exchanges:
        done()

INPUTS = ["tok", "cot", "lens", "pw", "pb", "mw", "mb", "fg", "fs", "uw", "ub", "dw", "db", "lg", "ls"]
BIG = ["out", "tg", "gpw", "gmw", "guw", "gdw"]
OUTPUTS = ["out", "tg", "gpw", "gpb", "gmw", "gmb", "gfg", "gfs", "guw", "gub", "gdw", "gdb", "glg", "gls"]
ROWS = dict(
    gpb=(QUERY_BIAS, 2), gmb=(MIX_BIAS, 1), gfg=(GAIN1, 1), gfs=(SHIFT1, 1), gub=(UP_BIAS, 1), gdb=(DOWN_BIAS, 1),
    glg=(GAIN2, 1), gls=(SHIFT2, 1),
)


def scratch_of(cfg):
    D, G, PG, L, C, F = cfg
    H = D // 2
    W, HC, FO, CR, SR = L * G, C // G, F // G, C // D, C // (D * G)
    FR, QC, heads = FO // D, 3 * HC, HEADS // G
    low = dict(
        wq=(C, QC), wm=(D, G, SR, C), wu=(C, FO), wd=(FO, C), sp=(G, SR, QC), su=(G, SR, FO), xg=(PG, W, C),
        qkv=(PG, W, QC), ctx=(PG, W, HC), cr=(PG, L, C), nlg=(PG, W, C), act=(PG, W, FO), hid=(PG, W, FO),
        s2=(PG, L, C), r2=(PG, L, C), lrg=(PG, W, C), frl=(PG, L, C), cg=(PG, L, C), dc=(PG, W, HC),
        ms2=(HC, C), mr2=(HC, C), tt=(2 * max(CR, FR), PG * W), tm_=(256, PG * L),
        bp=(2, H, CR, QC), tp=(CR, QC), bm=(2, H, SR, C), tm=(SR, C), bu=(2, H, CR, FO), tu=(CR, FO),
        bd=(2, H, FR, C), td=(FR, C),
        fu=(CR, FO), fur=(G, SR, FO), fp=(CR, QC), fpr=(G, SR, QC),
    )
    wide = dict(
        ss=(8, LANES), sm=(D, G, 8, LANES), probs=(PG * heads, W, W), nh1=(PG, L, C),
        inv1=(PG, L, LANES), gp=(PG, W, FO), part=(PG * G, L, C), r1=(PG, 2, L, C), m1=(2, HC, C),
        bs=(2, H, TABLE, CR), ts=(TABLE, CR), vs=(TABLE, C), vp=(8, QC), vu=(8, FO), vc=(D, TABLE, CR),
        pv=(TABLE, C), ubv=(8, FO), pbv=(8, QC),
        fsm=(TABLE, CR), fsr=(G, TABLE, CR),
    )
    sems = dict(
        local_sem=(2 + PG,), gs=(6, 2, H), gr=(6, 2, H), rs=(6, 2, H), rr=(6, 2, H),
        xs=(7 + 5 * PG, 3), xr=(7 + 5 * PG, 3), fs_=(4 * PG + 1, 3), fr_=(4 * PG + 1, 3),
    )
    scratch = {k: pltpu.VMEM(v, BF16) for k, v in low.items()}
    scratch |= {k: pltpu.VMEM(v, F32) for k, v in wide.items()}
    scratch |= {k: pltpu.SemaphoreType.DMA(v) for k, v in sems.items()}
    return scratch


def fits(cfg):
    D, G, PG, L, C, F = cfg
    return (
        G == 4 and D % 2 == 0 and D >= 4 and L % 128 == 0 and (C // G) % 256 == 0 and C // D == 128 and F // (D * G) == 128
        and (HEADS // G) % 2 == 0 and PG == 2 and PG * L * G == C and F // G == C and (L * G) % (C // G) == 0
    )


def fused(cfg, *args):
    D, G, PG, L, C, F = cfg
    SR = C // (D * G)
    scratch = scratch_of(cfg)
    global NAMES
    NAMES = INPUTS + BIG + ["small"] + list(scratch)
    vmem, anywhere = pl.BlockSpec(memory_space=pltpu.VMEM), pl.BlockSpec(memory_space=pl.ANY)
    where = {"tok": anywhere, "mw": anywhere, "dw": anywhere, "lens": pl.BlockSpec(memory_space=pltpu.SMEM)}
    flat = [a.reshape(1, -1) if name not in ("lens",) and a.ndim == 1 else a for name, a in zip(INPUTS, args)]
    shapes = dict(
        out=(PG, L, C), tg=(PG, L, C), gpw=(SR, 3 * C), gpb=(2, SR), gmw=(SR, C), gmb=(1, SR), gfg=(1, SR), gfs=(1, SR),
        guw=(SR, F), gub=(1, F // (D * G)), gdw=(F // (D * G), C), gdb=(1, SR), glg=(1, SR), gls=(1, SR),
    )
    given = pl.pallas_call(
        functools.partial(layer_kernel, cfg),
        out_shape=[pltpu.VMEM(shapes[k], F32) for k in BIG] + [jax.ShapeDtypeStruct((TABLE, LANES), F32)],
        in_specs=[where.get(k, vmem) for k in INPUTS],
        out_specs=[vmem] * (len(BIG) + 1),
        scratch_shapes=list(scratch.values()),
        compiler_params=pltpu.CompilerParams(collective_id=0, has_side_effects=True, vmem_limit_bytes=VMEM_LIMIT),
        name="encoder_layer",
    )(*flat)
    count = len(BIG)
    results = pl.pallas_call(
        write_out,
        out_shape=[jax.ShapeDtypeStruct(shapes[k], F32) for k in OUTPUTS],
        in_specs=[vmem] * (count + 1),
        out_specs=[anywhere if k in BIG else vmem for k in OUTPUTS],
        scratch_shapes=[pltpu.SemaphoreType.DMA((count,))],
        compiler_params=pltpu.CompilerParams(vmem_limit_bytes=VMEM_LIMIT),
        name="write_out",
    )(*[pltpu.with_memory_space_constraint(v, pltpu.VMEM) for v in given[:-1]], given[-1])
    return tuple(v.reshape(-1) if v.shape[0] == 1 else v for v in results)


def write_out(*refs):
    count = len(BIG)
    given, small = refs[:count], refs[count]
    result = dict(zip(OUTPUTS, refs[count + 1:]))
    sems = refs[-1]
    store = [pltpu.make_async_copy(given[i], result[k], sems.at[i]) for i, k in enumerate(BIG)]
    for copy in store:
        copy.start()
    for k, (row, rows) in ROWS.items():
        result[k][...] = small[row:row + rows, 0:result[k].shape[1]]
    for copy in store:
        copy.wait()


VMEM_LIMIT = 58 << 20


def per_device(*args):
    tokens, up_weight = args[0], args[9]
    D, G = lax.axis_size("dp"), lax.axis_size("seq")
    cfg = (D, G, tokens.shape[0], tokens.shape[1], tokens.shape[2], up_weight.shape[1])
    return fused(cfg, *args) if fits(cfg) else plain(*args)


MICRO = 2


def matmul(left, right):
    return jnp.dot(left, right, preferred_element_type=jnp.float32)


def against(left, right):
    return jnp.einsum("re,fe->rf", left, right, preferred_element_type=jnp.float32)


def contract_rows(left, right):
    return jnp.einsum("rd,re->de", left, right, preferred_element_type=jnp.float32)


def layer_norm(rows, gain, shift):
    center = rows - jnp.mean(rows, axis=-1, keepdims=True)
    spread = jnp.mean(center * center, axis=-1, keepdims=True)
    return center * lax.rsqrt(spread + 1e-05) * gain + shift


def gelu_exact(value):
    return 0.5 * value * (1.0 + lax.erf(value * 0.7071067811865476))


def masked_scores(query, keys, length):
    scores = jnp.einsum(
        "qhd,khd->hqk", query, keys, preferred_element_type=jnp.float32
    ) * query.shape[-1] ** (-0.5)
    valid = lax.iota(jnp.int32, keys.shape[0]) < length
    return jnp.where(valid[None, None, :], scores, -1e30)


def attend(packed, length):
    query, keys, values = (packed[:, 0], packed[:, 1], packed[:, 2])
    scores = masked_scores(query, keys, length)
    top = jnp.max(scores, axis=-1, keepdims=True)
    powers = jnp.exp(scores - top)
    total = jnp.sum(powers, axis=-1, keepdims=True)
    probs = (powers / total).astype(jnp.bfloat16)
    context = jnp.einsum("hqk,khd->qhd", probs, values, preferred_element_type=jnp.float32)
    return (
        context.astype(jnp.bfloat16).reshape(packed.shape[0], -1),
        (top + jnp.log(total))[..., 0],
    )


def attend_back(packed, context_grad, logsum, length):
    query, keys, values = (packed[:, 0], packed[:, 1], packed[:, 2])
    scale = query.shape[-1] ** (-0.5)
    scores = masked_scores(query, keys, length)
    probs = jnp.exp(scores - logsum[..., None])
    probs_grad = jnp.einsum(
        "qhd,khd->hqk", context_grad, values, preferred_element_type=jnp.float32
    )
    inner = jnp.sum(probs * probs_grad, axis=-1, keepdims=True)
    scores_grad = (probs * (probs_grad - inner)).astype(jnp.bfloat16)
    query_grad = (
        jnp.einsum("hqk,khd->qhd", scores_grad, keys, preferred_element_type=jnp.float32) * scale
    )
    keys_grad = (
        jnp.einsum("hqk,qhd->khd", scores_grad, query, preferred_element_type=jnp.float32) * scale
    )
    values_grad = jnp.einsum(
        "hqk,qhd->khd", probs.astype(jnp.bfloat16), context_grad, preferred_element_type=jnp.float32
    )
    return jnp.stack([query_grad, keys_grad, values_grad], axis=1).astype(jnp.bfloat16)


def plain(
    tokens,
    cotangent,
    lengths,
    project_weight,
    project_bias,
    mixing_weight,
    mixing_bias,
    first_gain,
    first_shift,
    up_weight,
    up_bias,
    down_weight,
    down_bias,
    last_gain,
    last_shift,
):
    groups = lax.axis_size("seq")
    (
        project_full,
        bias_pair,
        mixing_full,
        mixing_shift,
        first_scale,
        first_offset,
        up_full,
        up_shift,
        down_full,
        down_shift,
        last_scale,
        last_offset,
    ) = (
        lax.all_gather(project_weight, ("dp", "seq"), axis=0, tiled=True),
        lax.all_gather(project_bias, ("dp", "seq"), axis=1, tiled=True),
        lax.all_gather(mixing_weight, ("dp", "seq"), axis=0, tiled=True),
        lax.all_gather(mixing_bias, ("dp", "seq"), axis=0, tiled=True),
        lax.all_gather(first_gain, ("dp", "seq"), axis=0, tiled=True),
        lax.all_gather(first_shift, ("dp", "seq"), axis=0, tiled=True),
        lax.all_gather(up_weight, ("dp", "seq"), axis=0, tiled=True),
        lax.all_gather(up_bias, ("dp", "seq"), axis=0, tiled=True),
        lax.all_gather(down_weight, ("dp", "seq"), axis=0, tiled=True),
        lax.all_gather(down_bias, ("dp", "seq"), axis=0, tiled=True),
        lax.all_gather(last_gain, ("dp", "seq"), axis=0, tiled=True),
        lax.all_gather(last_shift, ("dp", "seq"), axis=0, tiled=True),
    )
    bias_pair = bias_pair.astype(jnp.float32)
    mixing_shift = mixing_shift.astype(jnp.float32)
    first_scale = first_scale.astype(jnp.float32)
    first_offset = first_offset.astype(jnp.float32)
    up_shift = up_shift.astype(jnp.float32)
    down_shift = down_shift.astype(jnp.float32)
    last_scale = last_scale.astype(jnp.float32)
    last_offset = last_offset.astype(jnp.float32)
    project_shift = jnp.concatenate([bias_pair[0], jnp.zeros_like(bias_pair[0]), bias_pair[1]])
    pages = tokens.shape[0] // MICRO
    local = tokens.shape[1]
    model = tokens.shape[2]
    width = local * groups
    slice_width = model // groups
    owned = HEADS // groups
    rows = pages * local
    outputs = []
    input_grads = []
    for micro in range(MICRO):
        begin = micro * pages
        flat = tokens[begin : begin + pages].reshape(rows, model)
        spans = lengths[begin : begin + pages]
        packed = (matmul(flat, project_full) + project_shift).astype(jnp.bfloat16)
        per_head = lax.all_to_all(
            packed.reshape(pages, local, 3, groups, slice_width),
            "seq",
            split_axis=3,
            concat_axis=1,
            tiled=True,
        )
        per_head = per_head.reshape(pages, width, 3, owned, HEAD_DIM)
        context, logsum = lax.map(lambda item: attend(item[0], item[1]), (per_head, spans))
        mixed = lax.all_to_all(context, "seq", split_axis=1, concat_axis=2, tiled=True).reshape(
            rows, model
        )
        residual = flat.astype(jnp.float32) + matmul(mixed, mixing_full) + mixing_shift
        normed, first_pull = jax.vjp(layer_norm, residual, first_scale, first_offset)
        normed_low = normed.astype(jnp.bfloat16)
        hidden_in = matmul(normed_low, up_full) + up_shift
        hidden_value, gelu_pull = jax.vjp(gelu_exact, hidden_in)
        activation = hidden_value.astype(jnp.bfloat16)
        last_resid = normed + matmul(activation, down_full) + down_shift
        output, last_pull = jax.vjp(layer_norm, last_resid, last_scale, last_offset)
        outputs.append(output.reshape(pages, local, model))
        seed_grad = cotangent[begin : begin + pages].reshape(rows, model).astype(jnp.float32)
        last_resid_grad, last_gain_grad, last_shift_grad = last_pull(seed_grad)
        down_bias_grad = jnp.sum(last_resid_grad, axis=0)
        last_resid_low = last_resid_grad.astype(jnp.bfloat16)
        down_weight_grad = contract_rows(activation, last_resid_low)
        (hidden_grad,) = gelu_pull(against(last_resid_low, down_full))
        up_bias_grad = jnp.sum(hidden_grad, axis=0)
        hidden_low = hidden_grad.astype(jnp.bfloat16)
        up_weight_grad = contract_rows(normed_low, hidden_low)
        feed_part = (
            up_weight_grad,
            up_bias_grad,
            down_weight_grad,
            down_bias_grad,
            last_gain_grad,
            last_shift_grad,
        )
        if micro == 0:
            feed_total = feed_part
        else:
            feed_total = tuple((a + b for a, b in zip(feed_total, feed_part)))
        normed_grad = last_resid_grad + against(hidden_low, up_full)
        first_resid_grad, first_gain_grad, first_shift_grad = first_pull(normed_grad)
        mixing_bias_grad = jnp.sum(first_resid_grad, axis=0)
        first_resid_low = first_resid_grad.astype(jnp.bfloat16)
        mixing_weight_grad = contract_rows(mixed, first_resid_low)
        context_grad = against(first_resid_low, mixing_full).astype(jnp.bfloat16)
        context_heads = lax.all_to_all(
            context_grad.reshape(pages, local, model),
            "seq",
            split_axis=2,
            concat_axis=1,
            tiled=True,
        )
        context_heads = context_heads.reshape(pages, width, owned, HEAD_DIM)
        packed_grad = lax.map(
            lambda item: attend_back(item[0], item[1], item[2], item[3]),
            (per_head, context_heads, logsum, spans),
        )
        packed_grad = lax.all_to_all(
            packed_grad.reshape(pages, width, 3, 1, slice_width),
            "seq",
            split_axis=1,
            concat_axis=3,
            tiled=True,
        )
        packed_grad = packed_grad.reshape(rows, 3 * model)
        bias_grad = jnp.stack(
            [
                jnp.sum(packed_grad[:, :model], axis=0, dtype=jnp.float32),
                jnp.sum(packed_grad[:, 2 * model :], axis=0, dtype=jnp.float32),
            ]
        )
        project_weight_grad = contract_rows(flat, packed_grad)
        input_grads.append(
            (first_resid_grad + against(packed_grad, project_full)).reshape(pages, local, model)
        )
        attend_part = (
            project_weight_grad,
            bias_grad,
            mixing_weight_grad,
            mixing_bias_grad,
            first_gain_grad,
            first_shift_grad,
        )
        if micro == 0:
            attend_total = attend_part
        else:
            attend_total = tuple((a + b for a, b in zip(attend_total, attend_part)))
    shards = (
        lax.psum_scatter(attend_total[0], ("dp", "seq"), scatter_dimension=0, tiled=True),
        lax.psum_scatter(attend_total[1], ("dp", "seq"), scatter_dimension=1, tiled=True),
        lax.psum_scatter(attend_total[2], ("dp", "seq"), scatter_dimension=0, tiled=True),
        lax.psum_scatter(attend_total[3], ("dp", "seq"), scatter_dimension=0, tiled=True),
        lax.psum_scatter(attend_total[4], ("dp", "seq"), scatter_dimension=0, tiled=True),
        lax.psum_scatter(attend_total[5], ("dp", "seq"), scatter_dimension=0, tiled=True),
        lax.psum_scatter(feed_total[0], ("dp", "seq"), scatter_dimension=0, tiled=True),
        lax.psum_scatter(feed_total[1], ("dp", "seq"), scatter_dimension=0, tiled=True),
        lax.psum_scatter(feed_total[2], ("dp", "seq"), scatter_dimension=0, tiled=True),
        lax.psum_scatter(feed_total[3], ("dp", "seq"), scatter_dimension=0, tiled=True),
        lax.psum_scatter(feed_total[4], ("dp", "seq"), scatter_dimension=0, tiled=True),
        lax.psum_scatter(feed_total[5], ("dp", "seq"), scatter_dimension=0, tiled=True),
    )
    layer_output = jnp.concatenate(outputs, axis=0)
    tokens_gradient = jnp.concatenate(input_grads, axis=0)
    return (
        layer_output,
        tokens_gradient,
        shards[0],
        shards[1],
        shards[2],
        shards[3],
        shards[4],
        shards[5],
        shards[6],
        shards[7],
        shards[8],
        shards[9],
        shards[10],
        shards[11],
    )


def solution(mesh):
    placed = (
        P("dp", "seq", None),
        P("dp", "seq", None),
        P("dp"),
        P(("dp", "seq"), None),
        P(None, ("dp", "seq")),
        P(("dp", "seq"), None),
        P(("dp", "seq")),
        P(("dp", "seq")),
        P(("dp", "seq")),
        P(("dp", "seq"), None),
        P(("dp", "seq")),
        P(("dp", "seq"), None),
        P(("dp", "seq")),
        P(("dp", "seq")),
        P(("dp", "seq")),
    )
    return jax.shard_map(
        per_device,
        mesh=mesh,
        in_specs=placed,
        out_specs=(
            P("dp", "seq", None),
            P("dp", "seq", None),
            P(("dp", "seq"), None),
            P(None, ("dp", "seq")),
            P(("dp", "seq"), None),
            P(("dp", "seq")),
            P(("dp", "seq")),
            P(("dp", "seq")),
            P(("dp", "seq"), None),
            P(("dp", "seq")),
            P(("dp", "seq"), None),
            P(("dp", "seq")),
            P(("dp", "seq")),
            P(("dp", "seq")),
        ),
        check_vma=False,
    )
```
